32 devices in a mesh: row: 4 (over z), col: 4 (over x, core), filt: 2 (over y).
Axes of the slice: x: 2, y: 2, z: 4, core: 2. Of those that a mesh axis runs over, the one named last changes fastest.
Arguments:
- features: bfloat16 [512, 64, 512], P('filt', 'row', 'col'), may hold values from -6 to 6
- kernel: bfloat16 [3, 3, 512, 512], replicated, may hold values from -0.09375 to 0.09375
- bias: float32 [512], replicated, may hold values from -3 to 3
Outputs:
- convolved: bfloat16 [512, 64, 512], P('filt', 'row', 'col')
The draws below stay inside these ranges and needn't reach their ends.
All inputs are finite; a program needn't handle non-finite values.
Results may differ from the reference program's by a relative error of at most 0.001.
Values may be sent and summed in bfloat16 or wider, within the bound.
No kernel may reach another device: no remote copies, remote signals or barrier semaphores. Data moves between devices by JAX's collectives and lax.ppermute only.
A program may use at most 64 MiB of HBM per device.

```python
import jax
import jax.numpy as jnp
from jax import lax

C = 512
H = 64
W = 512


def block_levels(key, dims, shards, least, largest):
    def one(dim, blocks):
        steps = jax.random.uniform(jax.random.fold_in(jax.random.fold_in(key, 6), dim), (blocks,), jnp.float32, least / len(shards), largest / len(shards))
        return jnp.repeat(jnp.exp(steps), dims[dim] // blocks).reshape((-1,) + (1,) * (len(dims) - dim - 1))

    level = one(*shards[0])
    for cut in shards[1:]:
        level = level * one(*cut)
    return level


def gaussian(own_key, extent, deviation, bound, cuts=(), kind=jnp.bfloat16):
    array = jax.random.normal(own_key, extent, jnp.float32) * deviation
    if len(cuts) > 0:
        array = block_levels(own_key, extent, cuts, -0.22, 0.18) * array
    return jnp.clip(array, min=-bound, max=bound).astype(kind)


def setup_inputs(seed: int = 0) -> dict:
    seeds = jax.random.split(jax.random.key(seed), 4)
    return {
        "features": gaussian(seeds[0], (C, H, W), 1.0, 6.0, ((0, 2), (1, 4), (2, 4))),
        "kernel": gaussian(seeds[1], (3, 3, C, C), (9 * C) ** -0.5, 0.09375),
        "bias": gaussian(seeds[2], (C,), 0.5, 3.0, (), jnp.float32),
    }


def reference(features, kernel, bias):
    padded = jnp.pad(features, ((0, 0), (1, 1), (1, 1)))
    result = lax.conv_general_dilated(padded.astype(jnp.float32)[None], kernel.astype(jnp.float32), (1, 1), "VALID", dimension_numbers=("NCHW", "HWIO", "NCHW"), precision=lax.Precision.HIGHEST)[0]
    return (result + bias[:, None, None]).astype(jnp.bfloat16)
```

```python
import functools

import jax
import jax.numpy as jnp
from jax import lax
from jax.experimental import pallas as pl
from jax.experimental.pallas import tpu as pltpu
from jax.sharding import PartitionSpec as P

BF16, F32 = jnp.bfloat16, jnp.float32
VMEM = pl.BlockSpec(memory_space=pltpu.VMEM)
ANY = pl.BlockSpec(memory_space=pl.ANY)
PARAMS = pltpu.CompilerParams(vmem_limit_bytes=24 << 20)
BLOCK = 4


def relayout_kernel(chunks, x_ref, rim_ref, *refs):
    outs, col_ref = refs[:-1], refs[-1]
    slab, rows, width = x_ref.shape
    for base in range(0, rows, 8):
        group = jnp.swapaxes(x_ref[:, base : base + 8, :].astype(F32), 0, 1)
        for h in range(base, base + 8):
            pixels = group[h - base].T
            col_ref[h : h + 1, :] = pixels[0:1, :]
            col_ref[rows + h : rows + h + 1, :] = pixels[width - 1 : width, :]
            pixels = pixels.astype(BF16)
            if h == 0:
                rim_ref[0:width, :] = pixels
            elif h == rows - 1:
                rim_ref[width : 2 * width, :] = pixels
            else:
                for out, (first, last) in zip(outs, chunks):
                    if first <= h < last:
                        out[h - first] = pixels
    rim_ref[2 * width :, :] = col_ref[...].astype(BF16)


def relayout(features, chunks):
    slab, rows, width = features.shape
    shapes = [(2 * width + 2 * rows, slab)] + [(last - first, width, slab) for first, last in chunks]
    return pl.pallas_call(
        functools.partial(relayout_kernel, chunks),
        out_shape=[jax.ShapeDtypeStruct(s, BF16) for s in shapes],
        in_specs=[VMEM],
        out_specs=[VMEM] * len(shapes),
        scratch_shapes=[pltpu.VMEM((2 * rows, slab), F32)],
        compiler_params=PARAMS,
        name="relayout",
    )(features)


def add_rows(spans, pieces, left_ref, right_ref, w_ref, total_ref, x_ref, written):
    height, width, _ = total_ref.shape
    slab = w_ref.shape[2]
    edge = lax.broadcasted_iota(jnp.int32, (16, slab), 0)
    at = 0
    for piece, local, row, count in spans:
        for start in range(0, count, BLOCK):
            size = min(BLOCK, count - start)
            for i in range(size):
                value = piece[local + start + i]
                r = row + start + i + 1
                x_ref[1, at + i] = value
                x_ref[0, at + i, 0 : width - 16, :] = value[0 : width - 16]
                last = value[width - 16 :].astype(F32)
                x_ref[0, at + i, width - 16 :, :] = jnp.where(edge == 15, left_ref[r : r + 1, :], last).astype(BF16)
                x_ref[2, at + i, 16:, :] = value[16:]
                lead = value[0:16].astype(F32)
                x_ref[2, at + i, 0:16, :] = jnp.where(edge == 0, right_ref[r : r + 1, :], lead).astype(BF16)
            for a in range(3):
                low = max(0, row + start + 1 - a)
                high = min(height, row + start + size + 1 - a)
                if high <= low:
                    continue
                skip = low - (row + start + 1 - a)
                n = high - low
                for b in range(3):
                    lhs = x_ref[b, at + skip : at + skip + n].reshape(n * width, slab)
                    part = jnp.dot(lhs, w_ref[a, b], preferred_element_type=F32).reshape(n, width, -1)
                    for i in range(n):
                        term = part[i] if b == 1 else pltpu.roll(part[i], 1 if b == 0 else width - 1, 0)
                        if low + i in written:
                            total_ref[low + i] += term
                        else:
                            total_ref[low + i] = term
                            written.add(low + i)
            at += size


def store_rows(total_ref, bias_ref, rows, out_ref):
    turned = jnp.stack([(total_ref[h] + bias_ref[...]).T for h in rows], 0)
    out_ref[...] = jnp.swapaxes(turned, 0, 1).astype(BF16)


def accumulate_kernel(spans, n, started, *refs):
    pieces = refs[:n]
    left_ref, right_ref, w_ref = refs[n : n + 3]
    total_ref, x_ref = refs[-2:]
    written = set(range(total_ref.shape[0])) if started else set()
    spans = [(pieces[p], local, row, count) for p, local, row, count in spans]
    add_rows(spans, pieces, left_ref, right_ref, w_ref, total_ref, x_ref, written)


def accumulate(spans, pieces, left, right, weights, total, shape):
    count = sum(s[3] for s in spans)
    width, slab = shape[1], weights.shape[2]
    operands = [*pieces, left, right, weights]
    aliases = {}
    if total is not None:
        aliases = {len(operands): 0}
        operands.append(total)
    flops = 2 * count * width * 9 * slab * shape[2]
    return pl.pallas_call(
        functools.partial(accumulate_kernel, spans, len(pieces), total is not None),
        out_shape=jax.ShapeDtypeStruct(shape, F32),
        in_specs=[VMEM] * len(operands),
        out_specs=VMEM,
        scratch_shapes=[pltpu.VMEM((3, count, width, slab), BF16)],
        input_output_aliases=aliases,
        compiler_params=PARAMS,
        cost_estimate=pl.CostEstimate(flops=flops, bytes_accessed=1 << 20, transcendentals=0),
        name="accumulate",
    )(*operands)


def upper_kernel(total_ref, bias_ref, out_ref):
    store_rows(total_ref, bias_ref, range(out_ref.shape[1]), out_ref)


def upper(total, bias, half):
    return pl.pallas_call(
        upper_kernel,
        out_shape=jax.ShapeDtypeStruct((total.shape[2], half, total.shape[1]), BF16),
        in_specs=[VMEM] * 2,
        out_specs=VMEM,
        compiler_params=PARAMS,
        name="upper",
    )(total, bias)


def last_kernel(span, piece, left_ref, right_ref, w_ref, total_in, bias_ref, upper_ref, out_ref, total_ref, x_ref, lower_ref, sems):
    half = upper_ref.shape[1]
    height = out_ref.shape[1]
    first = pltpu.make_async_copy(upper_ref, out_ref.at[:, 0:half, :], sems.at[0])
    first.start()
    total_ref[half:] = total_in[half:]
    add_rows([(piece, *span)], None, left_ref, right_ref, w_ref, total_ref, x_ref, set(range(height)))
    store_rows(total_ref, bias_ref, range(half, height), lower_ref)
    second = pltpu.make_async_copy(lower_ref, out_ref.at[:, half:height, :], sems.at[1])
    second.start()
    first.wait()
    second.wait()


def last(span, piece, left, right, weights, total, bias, top):
    height, width, outs = total.shape
    slab = weights.shape[2]
    half = top.shape[1]
    return pl.pallas_call(
        functools.partial(last_kernel, span),
        out_shape=jax.ShapeDtypeStruct((outs, height, width), BF16),
        in_specs=[VMEM] * 7,
        out_specs=ANY,
        scratch_shapes=[
            pltpu.VMEM(total.shape, F32),
            pltpu.VMEM((3, span[2], width, slab), BF16),
            pltpu.VMEM((outs, height - half, width), BF16),
            pltpu.SemaphoreType.DMA((2,)),
        ],
        compiler_params=PARAMS,
        name="last",
    )(piece, left, right, weights, total, bias, top)


def body(features, kernel, bias):
    groups = lax.axis_size("filt")
    owner = lax.axis_index("filt")
    slab, height, width = features.shape
    outs = kernel.shape[3] // groups
    half = height // 2
    chunks = ((1, half), (half, height - 3), (height - 3, height - 1))
    own_kernel = lax.dynamic_slice_in_dim(kernel, owner * outs, outs, 3)
    own_bias = lax.dynamic_slice_in_dim(bias, owner * outs, outs, 0)[None, :]

    parts = relayout(features, chunks)
    sets = [parts]
    for shift in range(1, groups):
        ring = [(i, (i + shift) % groups) for i in range(groups)]
        sets.append([lax.ppermute(part, "filt", ring) for part in parts])
    weights = [
        lax.dynamic_slice_in_dim(own_kernel, lax.rem(owner - shift + groups, groups) * slab, slab, 2)
        for shift in range(groups)
    ]

    rims = [s[0] for s in sets]
    count = lax.axis_size("row")
    forward = [(i, i + 1) for i in range(count - 1)]
    backward = [(t, s) for s, t in forward]
    above = lax.ppermute(jnp.stack([r[width : 2 * width] for r in rims]), "row", forward)
    below = lax.ppermute(jnp.stack([r[0:width] for r in rims]), "row", backward)
    count = lax.axis_size("col")
    forward = [(i, i + 1) for i in range(count - 1)]
    backward = [(t, s) for s, t in forward]
    inner = jnp.stack([r[2 * width :] for r in rims])
    first = jnp.concatenate([above[:, 0:1], inner[:, 0:height], below[:, 0:1]], 1)
    final = jnp.concatenate([above[:, width - 1 :], inner[:, height:], below[:, width - 1 :]], 1)
    left = lax.ppermute(final, "col", forward).astype(F32)
    right = lax.ppermute(first, "col", backward).astype(F32)

    shape = (height, width, outs)
    total = None
    for g in range(groups):
        rim, a, b, c = sets[g]
        halo = jnp.stack([above[g], rim[0:width], rim[width : 2 * width], below[g]])
        spans = [(0, 0, -1, 2), (0, 2, height - 1, 2)]
        args = left[g], right[g], weights[g]
        if g == 0:
            spans += [(1 + i, 0, first_, last_ - first_) for i, (first_, last_) in enumerate(chunks)]
            total = accumulate(spans, [halo, a, b, c], *args, None, shape)
            continue
        total = accumulate(spans, [halo], *args, total, shape)
        total = accumulate([(0, 0, chunks[0][0], a.shape[0])], [a], *args, total, shape)
        total = accumulate([(0, 0, chunks[1][0], b.shape[0])], [b], *args, total, shape)
        if g < groups - 1:
            total = accumulate([(0, 0, chunks[2][0], c.shape[0])], [c], *args, total, shape)
    top = upper(total, own_bias, half)
    return last((0, chunks[2][0], c.shape[0]), c, *args, total, own_bias, top)


def solution(mesh):
    return jax.shard_map(
        body,
        mesh=mesh,
        in_specs=(P("filt", "row", "col"), P(), P()),
        out_specs=P("filt", "row", "col"),
        check_vma=False,
    )
```

```python
import functools

import jax
import jax.numpy as jnp
from jax import lax
from jax.experimental import pallas as pl
from jax.experimental.pallas import tpu as pltpu
from jax.sharding import PartitionSpec as P

BF16, F32 = jnp.bfloat16, jnp.float32
VMEM = pl.BlockSpec(memory_space=pltpu.VMEM)
ANY = pl.BlockSpec(memory_space=pl.ANY)
PARAMS = pltpu.CompilerParams(vmem_limit_bytes=24 << 20)
BLOCK = 4


def relayout_kernel(chunks, x_ref, rim_ref, *refs):
    outs, col_ref = refs[:-1], refs[-1]
    slab, rows, width = x_ref.shape
    for base in range(0, rows, 8):
        group = jnp.swapaxes(x_ref[:, base : base + 8, :].astype(F32), 0, 1)
        for h in range(base, base + 8):
            pixels = group[h - base].T
            col_ref[h : h + 1, :] = pixels[0:1, :]
            col_ref[rows + h : rows + h + 1, :] = pixels[width - 1 : width, :]
            pixels = pixels.astype(BF16)
            if h == 0:
                rim_ref[0:width, :] = pixels
            elif h == rows - 1:
                rim_ref[width : 2 * width, :] = pixels
            else:
                for out, (first, last) in zip(outs, chunks):
                    if first <= h < last:
                        out[h - first] = pixels
    rim_ref[2 * width :, :] = col_ref[...].astype(BF16)


def relayout(features, chunks):
    slab, rows, width = features.shape
    shapes = [(2 * width + 2 * rows, slab)] + [(last - first, width, slab) for first, last in chunks]
    return pl.pallas_call(
        functools.partial(relayout_kernel, chunks),
        out_shape=[jax.ShapeDtypeStruct(s, BF16) for s in shapes],
        in_specs=[VMEM],
        out_specs=[VMEM] * len(shapes),
        scratch_shapes=[pltpu.VMEM((2 * rows, slab), F32)],
        compiler_params=PARAMS,
        name="relayout",
    )(features)


def put_row(x_ref, at, value):
    width, slab = value.shape
    edge = lax.broadcasted_iota(jnp.int32, (16, slab), 0)
    x_ref[1, at] = value
    x_ref[0, at, 0 : width - 16, :] = value[0 : width - 16]
    x_ref[0, at, width - 16 :, :] = jnp.where(edge == 15, 0, value[width - 16 :].astype(F32)).astype(BF16)
    x_ref[2, at, 16:, :] = value[16:]
    x_ref[2, at, 0:16, :] = jnp.where(edge == 0, 0, value[0:16].astype(F32)).astype(BF16)


def turn(part, b):
    return part if b == 1 else pltpu.roll(part, 1 if b == 0 else part.shape[0] - 1, 0)


def add_rows(spans, w_ref, total_ref, x_ref, written):
    height, width, _ = total_ref.shape
    slab = w_ref.shape[2]
    at = 0
    for piece, local, row, count in spans:
        for start in range(0, count, BLOCK):
            size = min(BLOCK, count - start)
            for i in range(size):
                put_row(x_ref, at + i, piece[local + start + i])
            for a in range(3):
                low = max(0, row + start + 1 - a)
                high = min(height, row + start + size + 1 - a)
                if high <= low:
                    continue
                skip = low - (row + start + 1 - a)
                n = high - low
                for b in range(3):
                    lhs = x_ref[b, at + skip : at + skip + n].reshape(n * width, slab)
                    part = jnp.dot(lhs, w_ref[a, b], preferred_element_type=F32).reshape(n, width, -1)
                    for i in range(n):
                        term = turn(part[i], b)
                        if low + i in written:
                            total_ref[low + i] += term
                        else:
                            total_ref[low + i] = term
                            written.add(low + i)
            at += size


def accumulate_kernel(spans, n, started, *refs):
    pieces, w_ref, total_ref, x_ref = refs[:n], refs[n], refs[-2], refs[-1]
    written = set(range(total_ref.shape[0])) if started else set()
    spans = [(pieces[p], local, row, count) for p, local, row, count in spans]
    add_rows(spans, w_ref, total_ref, x_ref, written)


def accumulate(spans, pieces, weights, total, shape):
    count = sum(s[3] for s in spans)
    width, slab = shape[1], weights.shape[2]
    operands = [*pieces, weights]
    aliases = {}
    if total is not None:
        aliases = {len(operands): 0}
        operands.append(total)
    return pl.pallas_call(
        functools.partial(accumulate_kernel, spans, len(pieces), total is not None),
        out_shape=jax.ShapeDtypeStruct(shape, F32),
        in_specs=[VMEM] * len(operands),
        out_specs=VMEM,
        scratch_shapes=[pltpu.VMEM((3, count, width, slab), BF16)],
        input_output_aliases=aliases,
        compiler_params=PARAMS,
        cost_estimate=cost(count * width * 9, slab, shape[2]),
        name="accumulate",
    )(*operands)


def cost(pixels, slab, outs):
    return pl.CostEstimate(flops=2 * pixels * slab * outs, bytes_accessed=1 << 20, transcendentals=0)


def outer_rows_kernel(groups, above_ref, below_ref, *refs):
    w_refs, fix_ref, x_ref = refs[:groups], refs[-2], refs[-1]
    for i, (ref, a) in enumerate(((above_ref, 0), (below_ref, 2))):
        fix = None
        for g in range(groups):
            put_row(x_ref, 0, ref[g])
            for b in range(3):
                part = turn(jnp.dot(x_ref[b, 0], w_refs[g][a, b], preferred_element_type=F32), b)
                fix = part if fix is None else fix + part
        fix_ref[i] = fix


def outer_cols_kernel(groups, left_ref, right_ref, *refs):
    w_refs, fix_ref = refs[:groups], refs[-1]
    height = fix_ref.shape[1]
    for i, (ref, b) in enumerate(((left_ref, 0), (right_ref, 2))):
        fix = None
        for g in range(groups):
            pixels = ref[g]
            for a in range(3):
                part = jnp.dot(pixels, w_refs[g][a, b], preferred_element_type=F32)[a : a + height]
                fix = part if fix is None else fix + part
        fix_ref[i] = fix


def finish_row(total_ref, h, bias_ref, rows_ref, cols_ref):
    height, width = cols_ref.shape[1], total_ref.shape[1]
    value = total_ref[h] + bias_ref[...]
    if h == 0:
        value += rows_ref[0]
    if h == height - 1:
        value += rows_ref[1]
    edge = lax.broadcasted_iota(jnp.int32, (8, value.shape[1]), 0)
    first = value[0:8] + jnp.where(edge == 0, cols_ref[0, h : h + 1, :], 0)
    final = value[width - 8 :] + jnp.where(edge == 7, cols_ref[1, h : h + 1, :], 0)
    return jnp.concatenate([first, value[8 : width - 8], final], 0)


def store_rows(total_ref, bias_ref, rows_ref, cols_ref, rows, out_ref):
    turned = jnp.stack([finish_row(total_ref, h, bias_ref, rows_ref, cols_ref).T for h in rows], 0)
    out_ref[...] = jnp.swapaxes(turned, 0, 1).astype(BF16)


def upper_kernel(total_ref, bias_ref, rows_ref, cols_ref, out_ref):
    store_rows(total_ref, bias_ref, rows_ref, cols_ref, range(out_ref.shape[1]), out_ref)


def last_kernel(span, piece, w_ref, total_in, bias_ref, rows_ref, cols_ref, upper_ref, out_ref, total_ref, x_ref, lower_ref, sems):
    half = upper_ref.shape[1]
    height = out_ref.shape[1]
    first = pltpu.make_async_copy(upper_ref, out_ref.at[:, 0:half, :], sems.at[0])
    first.start()
    total_ref[half:] = total_in[half:]
    add_rows([(piece, *span)], w_ref, total_ref, x_ref, set(range(height)))
    store_rows(total_ref, bias_ref, rows_ref, cols_ref, range(half, height), lower_ref)
    second = pltpu.make_async_copy(lower_ref, out_ref.at[:, half:height, :], sems.at[1])
    second.start()
    first.wait()
    second.wait()


def call(kernel, name, shape, dtype, operands, estimate, scratch=(), out=VMEM):
    return pl.pallas_call(
        kernel,
        out_shape=jax.ShapeDtypeStruct(shape, dtype),
        in_specs=[VMEM] * len(operands),
        out_specs=out,
        scratch_shapes=scratch,
        compiler_params=PARAMS,
        cost_estimate=estimate,
        name=name,
    )(*operands)


def weights_kernel(groups, kernel_ref, *refs):
    outs, sems = refs[:-1], refs[-1]
    slab, width = outs[0].shape[2:]
    owner = lax.axis_index("filt")
    copies = []
    for shift, out in enumerate(outs):
        group = lax.rem(owner - shift + groups, groups)
        source = kernel_ref.at[:, :, pl.ds(pl.multiple_of(group * slab, slab), slab), pl.ds(pl.multiple_of(owner * width, width), width)]
        copies.append(pltpu.make_async_copy(source, out, sems.at[shift]))
    for copy in copies:
        copy.start()
    for copy in copies:
        copy.wait()


def split_weights(kernel, groups, slab, outs):
    if outs % 128 == 0 and slab % 128 == 0:
        return pl.pallas_call(
            functools.partial(weights_kernel, groups),
            out_shape=[jax.ShapeDtypeStruct((3, 3, slab, outs), BF16)] * groups,
            in_specs=[ANY],
            out_specs=[VMEM] * groups,
            scratch_shapes=[pltpu.SemaphoreType.DMA((groups,))],
            compiler_params=PARAMS,
            name="split_weights",
        )(kernel)
    owner = lax.axis_index("filt")
    own = lax.dynamic_slice_in_dim(kernel, owner * outs, outs, 3)
    order = [lax.rem(owner - shift + groups, groups) for shift in range(groups)]
    return [lax.dynamic_slice_in_dim(own, group * slab, slab, 2) for group in order]


def body(features, kernel, bias):
    groups = lax.axis_size("filt")
    owner = lax.axis_index("filt")
    slab, height, width = features.shape
    outs = kernel.shape[3] // groups
    half = height // 2
    chunks = ((1, half), (half, height - 3), (height - 3, height - 1))
    own_bias = lax.dynamic_slice_in_dim(bias, owner * outs, outs, 0)[None, :]

    parts = relayout(features, chunks)
    sets = [parts]
    for shift in range(1, groups):
        ring = [(i, (i + shift) % groups) for i in range(groups)]
        sets.append([lax.ppermute(part, "filt", ring) for part in parts])
    weights = split_weights(kernel, groups, slab, outs)

    rims = [s[0] for s in sets]
    count = lax.axis_size("row")
    forward = [(i, i + 1) for i in range(count - 1)]
    backward = [(t, s) for s, t in forward]
    above = lax.ppermute(jnp.stack([r[width : 2 * width] for r in rims]), "row", forward)
    below = lax.ppermute(jnp.stack([r[0:width] for r in rims]), "row", backward)
    count = lax.axis_size("col")
    forward = [(i, i + 1) for i in range(count - 1)]
    backward = [(t, s) for s, t in forward]
    inner = jnp.stack([r[2 * width :] for r in rims])
    first = jnp.concatenate([above[:, 0:1], inner[:, 0:height], below[:, 0:1]], 1)
    final = jnp.concatenate([above[:, width - 1 :], inner[:, height:], below[:, width - 1 :]], 1)
    left = lax.ppermute(final, "col", forward)
    right = lax.ppermute(first, "col", backward)

    rows_fix = call(
        functools.partial(outer_rows_kernel, groups), "outer_rows", (2, width, outs), F32,
        [above, below, *weights], cost(6 * width * groups, slab, outs), [pltpu.VMEM((3, 1, width, slab), BF16)],
    )
    cols_fix = call(
        functools.partial(outer_cols_kernel, groups), "outer_cols", (2, height, outs), F32,
        [left, right, *weights], cost(6 * 256 * groups, slab, outs),
    )

    shape = (height, width, outs)
    total = None
    for g in range(groups):
        rim, a, b, c = sets[g]
        rim = rim[0 : 2 * width].reshape(2, width, slab)
        spans = [(0, 0, 0, 1), (0, 1, height - 1, 1)]
        if g == 0:
            spans += [(1 + i, 0, first_, last_ - first_) for i, (first_, last_) in enumerate(chunks)]
            total = accumulate(spans, [rim, a, b, c], weights[g], None, shape)
            continue
        total = accumulate(spans, [rim], weights[g], total, shape)
        total = accumulate([(0, 0, chunks[0][0], a.shape[0])], [a], weights[g], total, shape)
        total = accumulate([(0, 0, chunks[1][0], b.shape[0])], [b], weights[g], total, shape)
        if g < groups - 1:
            total = accumulate([(0, 0, chunks[2][0], c.shape[0])], [c], weights[g], total, shape)
    top = call(upper_kernel, "upper", (outs, half, width), BF16, [total, own_bias, rows_fix, cols_fix], cost(256, slab, outs))
    scratch = [
        pltpu.VMEM(shape, F32),
        pltpu.VMEM((3, c.shape[0], width, slab), BF16),
        pltpu.VMEM((outs, height - half, width), BF16),
        pltpu.SemaphoreType.DMA((2,)),
    ]
    span = (0, chunks[2][0], c.shape[0])
    return call(
        functools.partial(last_kernel, span), "last", (outs, height, width), BF16,
        [c, weights[-1], total, own_bias, rows_fix, cols_fix, top], cost(9 * 256, slab, outs), scratch, ANY,
    )


def solution(mesh):
    return jax.shard_map(
        body,
        mesh=mesh,
        in_specs=(P("filt", "row", "col"), P(), P()),
        out_specs=P("filt", "row", "col"),
        check_vma=False,
    )
```

```python
import functools

import jax
import jax.numpy as jnp
from jax import lax
from jax.experimental import pallas as pl
from jax.experimental.pallas import tpu as pltpu
from jax.sharding import PartitionSpec as P

BF16, F32 = jnp.bfloat16, jnp.float32
VMEM = pl.BlockSpec(memory_space=pltpu.VMEM)
HBM = pl.BlockSpec(memory_space=pltpu.HBM)
PARAMS = pltpu.CompilerParams(vmem_limit_bytes=10 << 20)
BLOCK = 4


def relayout_kernel(chunks, x_ref, rim_ref, *refs):
    outs, col_ref = refs[:-1], refs[-1]
    slab, rows, width = x_ref.shape
    for base in range(0, rows, 8):
        group = jnp.swapaxes(x_ref[:, base : base + 8, :].astype(F32), 0, 1)
        for h in range(base, base + 8):
            pixels = group[h - base].T
            col_ref[h : h + 1, :] = pixels[0:1, :]
            col_ref[rows + h : rows + h + 1, :] = pixels[width - 1 : width, :]
            pixels = pixels.astype(BF16)
            if h == 0:
                rim_ref[0:width, :] = pixels
            elif h == rows - 1:
                rim_ref[width : 2 * width, :] = pixels
            else:
                for out, (first, last) in zip(outs, chunks):
                    if first <= h < last:
                        out[h - first] = pixels
    rim_ref[2 * width :, :] = col_ref[...].astype(BF16)


def relayout(features, chunks):
    slab, rows, width = features.shape
    shapes = [(2 * width + 2 * rows, slab)] + [(last - first, width, slab) for first, last in chunks]
    return pl.pallas_call(
        functools.partial(relayout_kernel, chunks),
        out_shape=[jax.ShapeDtypeStruct(s, BF16) for s in shapes],
        in_specs=[VMEM],
        out_specs=[VMEM] * len(shapes),
        scratch_shapes=[pltpu.VMEM((2 * rows, slab), F32)],
        compiler_params=PARAMS,
        name="relayout",
    )(features)


def put_row(x_ref, at, value):
    width, slab = value.shape
    edge = lax.broadcasted_iota(jnp.int32, (16, slab), 0)
    x_ref[1, at] = value
    x_ref[0, at, 0 : width - 16, :] = value[0 : width - 16]
    x_ref[0, at, width - 16 :, :] = jnp.where(edge == 15, 0, value[width - 16 :].astype(F32)).astype(BF16)
    x_ref[2, at, 16:, :] = value[16:]
    x_ref[2, at, 0:16, :] = jnp.where(edge == 0, 0, value[0:16].astype(F32)).astype(BF16)


def turn(part, b):
    return part if b == 1 else pltpu.roll(part, 1 if b == 0 else part.shape[0] - 1, 0)


def add_rows(spans, w_ref, total_ref, x_ref, written):
    height, width, _ = total_ref.shape
    slab = w_ref.shape[2]
    at = 0
    for piece, local, row, count in spans:
        for start in range(0, count, BLOCK):
            size = min(BLOCK, count - start)
            for i in range(size):
                put_row(x_ref, at + i, piece[local + start + i])
            for a in range(3):
                low = max(0, row + start + 1 - a)
                high = min(height, row + start + size + 1 - a)
                if high <= low:
                    continue
                skip = low - (row + start + 1 - a)
                n = high - low
                for b in range(3):
                    lhs = x_ref[b, at + skip : at + skip + n].reshape(n * width, slab)
                    part = jnp.dot(lhs, w_ref[a, b], preferred_element_type=F32).reshape(n, width, -1)
                    for i in range(n):
                        term = turn(part[i], b)
                        if low + i in written:
                            total_ref[low + i] += term
                        else:
                            total_ref[low + i] = term
                            written.add(low + i)
            at += size


def accumulate_kernel(spans, n, started, *refs):
    pieces, w_ref, total_ref, x_ref = refs[:n], refs[n], refs[-2], refs[-1]
    written = set(range(total_ref.shape[0])) if started else set()
    spans = [(pieces[p], local, row, count) for p, local, row, count in spans]
    add_rows(spans, w_ref, total_ref, x_ref, written)


def accumulate(spans, pieces, weights, total, shape, after=None):
    count = sum(s[3] for s in spans)
    width, slab = shape[1], weights.shape[2]
    operands = [*pieces, weights]
    aliases = {}
    if total is not None:
        aliases = {len(operands): 0}
        operands.append(total)
    if after is not None:
        operands.append(after)
    return pl.pallas_call(
        functools.partial(accumulate_kernel, spans, len(pieces), total is not None),
        out_shape=jax.ShapeDtypeStruct(shape, F32),
        in_specs=[VMEM] * len(operands),
        out_specs=VMEM,
        scratch_shapes=[pltpu.VMEM((3, count, width, slab), BF16)],
        input_output_aliases=aliases,
        compiler_params=PARAMS,
        cost_estimate=cost(count * width * 9, slab, shape[2]),
        name="accumulate",
    )(*operands)


def pick_kernel(low, high, rows_ref, after_ref, out_ref):
    out_ref[...] = rows_ref[low:high]


def pick(rows, low, high, after):
    shape = (high - low, *rows.shape[1:])
    return call(functools.partial(pick_kernel, low, high), "pick", shape, BF16, [rows, after], cost(1, 1, 1))


def cost(pixels, slab, outs):
    return pl.CostEstimate(flops=2 * pixels * slab * outs, bytes_accessed=1 << 20, transcendentals=0)


def outer_rows_kernel(groups, above_ref, below_ref, *refs):
    w_refs, fix_ref, x_ref = refs[:groups], refs[-2], refs[-1]
    for i, (ref, a) in enumerate(((above_ref, 0), (below_ref, 2))):
        fix = None
        for g in range(groups):
            put_row(x_ref, 0, ref[g])
            for b in range(3):
                part = turn(jnp.dot(x_ref[b, 0], w_refs[g][a, b], preferred_element_type=F32), b)
                fix = part if fix is None else fix + part
        fix_ref[i] = fix


def outer_cols_kernel(groups, left_ref, right_ref, *refs):
    w_refs, fix_ref = refs[:groups], refs[-1]
    height = fix_ref.shape[1]
    for i, (ref, b) in enumerate(((left_ref, 0), (right_ref, 2))):
        fix = None
        for g in range(groups):
            pixels = ref[g]
            for a in range(3):
                part = jnp.dot(pixels, w_refs[g][a, b], preferred_element_type=F32)[a : a + height]
                fix = part if fix is None else fix + part
        fix_ref[i] = fix


def finish_row(total_ref, h, bias_ref, rows_ref, cols_ref):
    height, width = cols_ref.shape[1], total_ref.shape[1]
    value = total_ref[h] + bias_ref[pl.ds(lax.axis_index("filt"), 1), :]
    if h == 0:
        value += rows_ref[0]
    if h == height - 1:
        value += rows_ref[1]
    edge = lax.broadcasted_iota(jnp.int32, (8, value.shape[1]), 0)
    first = value[0:8] + jnp.where(edge == 0, cols_ref[0, h : h + 1, :], 0)
    final = value[width - 8 :] + jnp.where(edge == 7, cols_ref[1, h : h + 1, :], 0)
    return jnp.concatenate([first, value[8 : width - 8], final], 0)


def store_rows(total_ref, bias_ref, rows_ref, cols_ref, rows, out_ref):
    turned = jnp.stack([finish_row(total_ref, h, bias_ref, rows_ref, cols_ref).T for h in rows], 0)
    out_ref[...] = jnp.swapaxes(turned, 0, 1).astype(BF16)


def upper_kernel(total_ref, bias_ref, rows_ref, cols_ref, out_ref):
    store_rows(total_ref, bias_ref, rows_ref, cols_ref, range(out_ref.shape[1]), out_ref)


def last_kernel(span, piece, w_ref, total_in, bias_ref, rows_ref, cols_ref, upper_ref, out_ref, total_ref, x_ref, lower_ref, sems):
    half = upper_ref.shape[1]
    height = out_ref.shape[1]
    first = pltpu.make_async_copy(upper_ref, out_ref.at[:, 0:half, :], sems.at[0])
    first.start()
    total_ref[half:] = total_in[half:]
    add_rows([(piece, *span)], w_ref, total_ref, x_ref, set(range(height)))
    store_rows(total_ref, bias_ref, rows_ref, cols_ref, range(half, height), lower_ref)
    second = pltpu.make_async_copy(lower_ref, out_ref.at[:, half:height, :], sems.at[1])
    second.start()
    first.wait()
    second.wait()


def call(kernel, name, shape, dtype, operands, estimate, scratch=(), out=VMEM):
    return pl.pallas_call(
        kernel,
        out_shape=jax.ShapeDtypeStruct(shape, dtype),
        in_specs=[VMEM] * len(operands),
        out_specs=out,
        scratch_shapes=scratch,
        compiler_params=PARAMS,
        cost_estimate=estimate,
        name=name,
    )(*operands)


def weights_kernel(groups, kernel_ref, *refs):
    outs, sems = refs[:-1], refs[-1]
    slab, width = outs[0].shape[2:]
    owner = lax.axis_index("filt")
    copies = []
    for shift, out in enumerate(outs):
        group = lax.rem(owner - shift + groups, groups)
        source = kernel_ref.at[:, :, pl.ds(pl.multiple_of(group * slab, slab), slab), pl.ds(pl.multiple_of(owner * width, width), width)]
        copies.append(pltpu.make_async_copy(source, out, sems.at[shift]))
    for copy in copies:
        copy.start()
    for copy in copies:
        copy.wait()


def split_weights(kernel, groups, slab, outs):
    if outs % 128 == 0 and slab % 128 == 0:
        return pl.pallas_call(
            functools.partial(weights_kernel, groups),
            out_shape=[jax.ShapeDtypeStruct((3, 3, slab, outs), BF16)] * groups,
            in_specs=[HBM],
            out_specs=[VMEM] * groups,
            scratch_shapes=[pltpu.SemaphoreType.DMA((groups,))],
            compiler_params=PARAMS,
            name="split_weights",
        )(kernel)
    owner = lax.axis_index("filt")
    own = lax.dynamic_slice_in_dim(kernel, owner * outs, outs, 3)
    order = [lax.rem(owner - shift + groups, groups) for shift in range(groups)]
    return [lax.dynamic_slice_in_dim(own, group * slab, slab, 2) for group in order]


def body(features, kernel, bias):
    groups = lax.axis_size("filt")
    slab, height, width = features.shape
    outs = kernel.shape[3] // groups
    half = height // 2
    chunks = ((1, half), (half, height - 3), (height - 3, height - 1))
    bias = bias.reshape(groups, outs)

    rim, upper_rows, lower_rows = relayout(features, ((1, half), (half, height - 1)))
    weights = split_weights(kernel, groups, slab, outs)
    rings = [[(i, (i + shift) % groups) for i in range(groups)] for shift in range(1, groups)]
    rims = [rim] + [lax.ppermute(rim, "filt", ring) for ring in rings]
    sets = [[lax.ppermute(upper_rows, "filt", ring)] for ring in rings]
    second = pick(lower_rows, 0, chunks[1][1] - half, rims[-1])
    for received, ring in zip(sets, rings):
        received.append(lax.ppermute(second, "filt", ring))

    count = lax.axis_size("row")
    forward = [(i, i + 1) for i in range(count - 1)]
    backward = [(t, s) for s, t in forward]
    below = lax.ppermute(jnp.stack([r[0:width] for r in rims]), "row", backward)
    above = lax.ppermute(jnp.stack([r[width : 2 * width] for r in rims]), "row", forward)
    third = pick(lower_rows, chunks[2][0] - half, chunks[2][1] - half, below)
    for received, ring in zip(sets, rings):
        received.append(lax.ppermute(third, "filt", ring))

    count = lax.axis_size("col")
    forward = [(i, i + 1) for i in range(count - 1)]
    backward = [(t, s) for s, t in forward]
    inner = jnp.stack([r[2 * width :] for r in rims])
    first = jnp.concatenate([above[:, 0:1], inner[:, 0:height], below[:, 0:1]], 1)
    final = jnp.concatenate([above[:, width - 1 :], inner[:, height:], below[:, width - 1 :]], 1)
    left = lax.ppermute(final, "col", forward)
    right = lax.ppermute(first, "col", backward)

    rows_fix = call(
        functools.partial(outer_rows_kernel, groups), "outer_rows", (2, width, outs), F32,
        [above, below, *weights], cost(6 * width * groups, slab, outs), [pltpu.VMEM((3, 1, width, slab), BF16)],
    )
    cols_fix = call(
        functools.partial(outer_cols_kernel, groups), "outer_cols", (2, height, outs), F32,
        [left, right, *weights], cost(6 * 256 * groups, slab, outs),
    )

    shape = (height, width, outs)
    total = None
    for g in range(groups):
        rim = rims[g][0 : 2 * width].reshape(2, width, slab)
        spans = [(0, 0, 0, 1), (0, 1, height - 1, 1)]
        if g == 0:
            spans += [(1, 0, 1, half - 1), (2, 0, half, half - 1)]
            total = accumulate(spans, [rim, upper_rows, lower_rows], weights[g], None, shape, rims[-1])
            continue
        a, b, c = sets[g - 1]
        total = accumulate(spans, [rim], weights[g], total, shape)
        total = accumulate([(0, 0, chunks[0][0], a.shape[0])], [a], weights[g], total, shape)
        total = accumulate([(0, 0, chunks[1][0], b.shape[0])], [b], weights[g], total, shape)
        if g < groups - 1:
            total = accumulate([(0, 0, chunks[2][0], c.shape[0])], [c], weights[g], total, shape)
    top = call(upper_kernel, "upper", (outs, half, width), BF16, [total, bias, rows_fix, cols_fix], cost(256, slab, outs))
    scratch = [
        pltpu.VMEM(shape, F32),
        pltpu.VMEM((3, c.shape[0], width, slab), BF16),
        pltpu.VMEM((outs, height - half, width), BF16),
        pltpu.SemaphoreType.DMA((2,)),
    ]
    span = (0, chunks[2][0], c.shape[0])
    return call(
        functools.partial(last_kernel, span), "last", (outs, height, width), BF16,
        [c, weights[-1], total, bias, rows_fix, cols_fix, top], cost(9 * 256, slab, outs), scratch, HBM,
    )


def solution(mesh):
    return jax.shard_map(
        body,
        mesh=mesh,
        in_specs=(P("filt", "row", "col"), P(), P()),
        out_specs=P("filt", "row", "col"),
        check_vma=False,
    )
```

```python
import functools

import jax
import jax.numpy as jnp
from jax import lax
from jax.experimental import pallas as pl
from jax.experimental.pallas import tpu as pltpu
from jax.sharding import PartitionSpec as P

BF16, F32 = jnp.bfloat16, jnp.float32
VMEM = pl.BlockSpec(memory_space=pltpu.VMEM)
HBM = pl.BlockSpec(memory_space=pltpu.HBM)
PARAMS = pltpu.CompilerParams(vmem_limit_bytes=10 << 20)
BLOCK = 4


def relayout_kernel(chunks, x_ref, rim_ref, *refs):
    outs, col_ref = refs[:-1], refs[-1]
    slab, rows, width = x_ref.shape
    for base in range(0, rows, 8):
        group = jnp.swapaxes(x_ref[:, base : base + 8, :].astype(F32), 0, 1)
        for h in range(base, base + 8):
            pixels = group[h - base].T
            col_ref[h : h + 1, :] = pixels[0:1, :]
            col_ref[rows + h : rows + h + 1, :] = pixels[width - 1 : width, :]
            pixels = pixels.astype(BF16)
            if h == 0:
                rim_ref[0:width, :] = pixels
            elif h == rows - 1:
                rim_ref[width : 2 * width, :] = pixels
            else:
                for out, (first, last) in zip(outs, chunks):
                    if first <= h < last:
                        out[h - first] = pixels
    rim_ref[2 * width :, :] = col_ref[...].astype(BF16)


def relayout(features, chunks):
    slab, rows, width = features.shape
    shapes = [(2 * width + 2 * rows, slab)] + [(last - first, width, slab) for first, last in chunks]
    return pl.pallas_call(
        functools.partial(relayout_kernel, chunks),
        out_shape=[jax.ShapeDtypeStruct(s, BF16) for s in shapes],
        in_specs=[VMEM],
        out_specs=[VMEM] * len(shapes),
        scratch_shapes=[pltpu.VMEM((2 * rows, slab), F32)],
        compiler_params=PARAMS,
        name="relayout",
    )(features)


def put_row(x_ref, at, value):
    width, slab = value.shape
    edge = lax.broadcasted_iota(jnp.int32, (16, slab), 0)
    x_ref[1, at] = value
    x_ref[0, at, 0 : width - 16, :] = value[0 : width - 16]
    x_ref[0, at, width - 16 :, :] = jnp.where(edge == 15, 0, value[width - 16 :].astype(F32)).astype(BF16)
    x_ref[2, at, 16:, :] = value[16:]
    x_ref[2, at, 0:16, :] = jnp.where(edge == 0, 0, value[0:16].astype(F32)).astype(BF16)


def turn(part, b):
    return part if b == 1 else pltpu.roll(part, 1 if b == 0 else part.shape[0] - 1, 0)


def add_rows(spans, w_ref, total_ref, x_ref, written):
    height, width, _ = total_ref.shape
    slab = w_ref.shape[2]
    at = 0
    for piece, local, row, count in spans:
        for start in range(0, count, BLOCK):
            size = min(BLOCK, count - start)
            for i in range(size):
                put_row(x_ref, at + i, piece[local + start + i])
            for a in range(3):
                low = max(0, row + start + 1 - a)
                high = min(height, row + start + size + 1 - a)
                if high <= low:
                    continue
                skip = low - (row + start + 1 - a)
                n = high - low
                for b in range(3):
                    lhs = x_ref[b, at + skip : at + skip + n].reshape(n * width, slab)
                    part = jnp.dot(lhs, w_ref[a, b], preferred_element_type=F32).reshape(n, width, -1)
                    for i in range(n):
                        term = turn(part[i], b)
                        if low + i in written:
                            total_ref[low + i] += term
                        else:
                            total_ref[low + i] = term
                            written.add(low + i)
            at += size


def accumulate_kernel(spans, n, started, *refs):
    pieces, w_ref, total_ref, x_ref = refs[:n], refs[n], refs[-2], refs[-1]
    written = set(range(total_ref.shape[0])) if started else set()
    spans = [(pieces[p], local, row, count) for p, local, row, count in spans]
    add_rows(spans, w_ref, total_ref, x_ref, written)


def accumulate(spans, pieces, weights, total, shape, after=None):
    count = sum(s[3] for s in spans)
    width, slab = shape[1], weights.shape[2]
    operands = [*pieces, weights]
    aliases = {}
    if total is not None:
        aliases = {len(operands): 0}
        operands.append(total)
    if after is not None:
        operands.append(after)
    return pl.pallas_call(
        functools.partial(accumulate_kernel, spans, len(pieces), total is not None),
        out_shape=jax.ShapeDtypeStruct(shape, F32),
        in_specs=[VMEM] * len(operands),
        out_specs=VMEM,
        scratch_shapes=[pltpu.VMEM((3, count, width, slab), BF16)],
        input_output_aliases=aliases,
        compiler_params=PARAMS,
        cost_estimate=cost(count * width * 9, slab, shape[2]),
        name="accumulate",
    )(*operands)


def pick_kernel(low, high, rows_ref, after_ref, out_ref):
    out_ref[...] = rows_ref[low:high]


def pick(rows, low, high, after):
    shape = (high - low, *rows.shape[1:])
    return call(functools.partial(pick_kernel, low, high), "pick", shape, BF16, [rows, after], cost(1, 1, 1))


def cost(pixels, slab, outs):
    return pl.CostEstimate(flops=2 * pixels * slab * outs, bytes_accessed=1 << 20, transcendentals=0)


def outer_rows_kernel(groups, above_ref, below_ref, *refs):
    w_refs, fix_ref, x_ref = refs[:groups], refs[-2], refs[-1]
    for i, (ref, a) in enumerate(((above_ref, 0), (below_ref, 2))):
        fix = None
        for g in range(groups):
            put_row(x_ref, 0, ref[g])
            for b in range(3):
                part = turn(jnp.dot(x_ref[b, 0], w_refs[g][a, b], preferred_element_type=F32), b)
                fix = part if fix is None else fix + part
        fix_ref[i] = fix


def outer_cols_kernel(groups, left_ref, right_ref, *refs):
    w_refs, fix_ref = refs[:groups], refs[-1]
    height = fix_ref.shape[1]
    for i, (ref, b) in enumerate(((left_ref, 0), (right_ref, 2))):
        fix = None
        for g in range(groups):
            pixels = ref[g]
            for a in range(3):
                part = jnp.dot(pixels, w_refs[g][a, b], preferred_element_type=F32)[a : a + height]
                fix = part if fix is None else fix + part
        fix_ref[i] = fix


def finish_row(total_ref, h, bias_ref, rows_ref, cols_ref):
    height, width = cols_ref.shape[1], total_ref.shape[1]
    value = total_ref[h] + bias_ref[...]
    if h == 0:
        value += rows_ref[0]
    if h == height - 1:
        value += rows_ref[1]
    edge = lax.broadcasted_iota(jnp.int32, (8, value.shape[1]), 0)
    first = value[0:8] + jnp.where(edge == 0, cols_ref[0, h : h + 1, :], 0)
    final = value[width - 8 :] + jnp.where(edge == 7, cols_ref[1, h : h + 1, :], 0)
    return jnp.concatenate([first, value[8 : width - 8], final], 0)


def store_rows(total_ref, bias_ref, rows_ref, cols_ref, rows, out_ref):
    turned = jnp.stack([finish_row(total_ref, h, bias_ref, rows_ref, cols_ref).T for h in rows], 0)
    out_ref[...] = jnp.swapaxes(turned, 0, 1).astype(BF16)


def upper_kernel(total_ref, bias_ref, rows_ref, cols_ref, out_ref):
    store_rows(total_ref, bias_ref, rows_ref, cols_ref, range(out_ref.shape[1]), out_ref)


def last_kernel(span, piece, w_ref, total_in, bias_ref, rows_ref, cols_ref, upper_ref, out_ref, total_ref, x_ref, lower_ref, sems):
    half = upper_ref.shape[1]
    height = out_ref.shape[1]
    first = pltpu.make_async_copy(upper_ref, out_ref.at[:, 0:half, :], sems.at[0])
    first.start()
    total_ref[half:] = total_in[half:]
    add_rows([(piece, *span)], w_ref, total_ref, x_ref, set(range(height)))
    store_rows(total_ref, bias_ref, rows_ref, cols_ref, range(half, height), lower_ref)
    second = pltpu.make_async_copy(lower_ref, out_ref.at[:, half:height, :], sems.at[1])
    second.start()
    first.wait()
    second.wait()


def call(kernel, name, shape, dtype, operands, estimate, scratch=(), out=VMEM):
    return pl.pallas_call(
        kernel,
        out_shape=jax.ShapeDtypeStruct(shape, dtype),
        in_specs=[VMEM] * len(operands),
        out_specs=out,
        scratch_shapes=scratch,
        compiler_params=PARAMS,
        cost_estimate=estimate,
        name=name,
    )(*operands)


def weights_kernel(groups, kernel_ref, bias_ref, *refs):
    outs, own_bias_ref, sems = refs[:-2], refs[-2], refs[-1]
    slab, width = outs[0].shape[2:]
    owner = lax.axis_index("filt")
    own = pl.ds(pl.multiple_of(owner * width, width), width)
    copies = []
    for shift, out in enumerate(outs):
        group = lax.rem(owner - shift + groups, groups)
        source = kernel_ref.at[:, :, pl.ds(pl.multiple_of(group * slab, slab), slab), own]
        copies.append(pltpu.make_async_copy(source, out, sems.at[shift]))
    for copy in copies:
        copy.start()
    own_bias_ref[...] = bias_ref[:, own]
    for copy in copies:
        copy.wait()


def split_weights(kernel, bias, groups, slab, outs):
    if outs % 128 == 0 and slab % 128 == 0:
        shapes = [jax.ShapeDtypeStruct((3, 3, slab, outs), BF16)] * groups
        return pl.pallas_call(
            functools.partial(weights_kernel, groups),
            out_shape=[*shapes, jax.ShapeDtypeStruct((1, outs), F32)],
            in_specs=[HBM, VMEM],
            out_specs=[VMEM] * (groups + 1),
            scratch_shapes=[pltpu.SemaphoreType.DMA((groups,))],
            compiler_params=PARAMS,
            name="split_weights",
        )(kernel, bias)
    owner = lax.axis_index("filt")
    own = lax.dynamic_slice_in_dim(kernel, owner * outs, outs, 3)
    order = [lax.rem(owner - shift + groups, groups) for shift in range(groups)]
    weights = [lax.dynamic_slice_in_dim(own, group * slab, slab, 2) for group in order]
    return [*weights, lax.dynamic_slice_in_dim(bias, owner * outs, outs, 1)]


def body(features, kernel, bias):
    groups = lax.axis_size("filt")
    slab, height, width = features.shape
    outs = kernel.shape[3] // groups
    half = height // 2
    chunks = ((1, half), (half, height - 3), (height - 3, height - 1))

    rim, upper_rows, lower_rows = relayout(features, ((1, half), (half, height - 1)))
    *weights, bias = split_weights(kernel, bias[None, :], groups, slab, outs)
    rings = [[(i, (i + shift) % groups) for i in range(groups)] for shift in range(1, groups)]
    rims = [rim] + [lax.ppermute(rim, "filt", ring) for ring in rings]
    sets = [[lax.ppermute(upper_rows, "filt", ring)] for ring in rings]
    second = pick(lower_rows, 0, chunks[1][1] - half, weights[0])
    for received, ring in zip(sets, rings):
        received.append(lax.ppermute(second, "filt", ring))

    count = lax.axis_size("row")
    forward = [(i, i + 1) for i in range(count - 1)]
    backward = [(t, s) for s, t in forward]
    below = lax.ppermute(jnp.stack([r[0:width] for r in rims]), "row", backward)
    above = lax.ppermute(jnp.stack([r[width : 2 * width] for r in rims]), "row", forward)
    count = lax.axis_size("col")
    forward = [(i, i + 1) for i in range(count - 1)]
    backward = [(t, s) for s, t in forward]
    inner = jnp.stack([r[2 * width :] for r in rims])
    first = jnp.concatenate([above[:, 0:1], inner[:, 0:height], below[:, 0:1]], 1)
    final = jnp.concatenate([above[:, width - 1 :], inner[:, height:], below[:, width - 1 :]], 1)
    left = lax.ppermute(final, "col", forward)
    right = lax.ppermute(first, "col", backward)

    shape = (height, width, outs)
    pairs = [r[0 : 2 * width].reshape(2, width, slab) for r in rims]
    outer = [(0, 0, 0, 1), (0, 1, height - 1, 1)]
    spans = [*outer, (1, 0, 1, half - 1), (2, 0, half, half - 1)]
    total = accumulate(spans, [pairs[0], upper_rows, lower_rows], weights[0], None, shape, rims[-1])
    third = pick(lower_rows, chunks[2][0] - half, chunks[2][1] - half, sets[-1][0])
    for received, ring in zip(sets, rings):
        received.append(lax.ppermute(third, "filt", ring))
    rows_fix = call(
        functools.partial(outer_rows_kernel, groups), "outer_rows", (2, width, outs), F32,
        [above, below, *weights], cost(6 * width * groups, slab, outs), [pltpu.VMEM((3, 1, width, slab), BF16)],
    )
    for g in range(1, groups):
        total = accumulate(outer, [pairs[g]], weights[g], total, shape, rows_fix)
        total = accumulate([(0, 0, chunks[0][0], half - 1)], [sets[g - 1][0]], weights[g], total, shape)
    cols_fix = call(
        functools.partial(outer_cols_kernel, groups), "outer_cols", (2, height, outs), F32,
        [left, right, *weights, total], cost(6 * 256 * groups, slab, outs),
    )
    for g in range(1, groups):
        b, c = sets[g - 1][1:]
        total = accumulate([(0, 0, chunks[1][0], b.shape[0])], [b], weights[g], total, shape)
        if g < groups - 1:
            total = accumulate([(0, 0, chunks[2][0], c.shape[0])], [c], weights[g], total, shape)
    top = call(upper_kernel, "upper", (outs, half, width), BF16, [total, bias, rows_fix, cols_fix], cost(256, slab, outs))
    scratch = [
        pltpu.VMEM(shape, F32),
        pltpu.VMEM((3, c.shape[0], width, slab), BF16),
        pltpu.VMEM((outs, height - half, width), BF16),
        pltpu.SemaphoreType.DMA((2,)),
    ]
    span = (0, chunks[2][0], c.shape[0])
    return call(
        functools.partial(last_kernel, span), "last", (outs, height, width), BF16,
        [c, weights[-1], total, bias, rows_fix, cols_fix, top], cost(9 * 256, slab, outs), scratch, HBM,
    )


def solution(mesh):
    return jax.shard_map(
        body,
        mesh=mesh,
        in_specs=(P("filt", "row", "col"), P(), P()),
        out_specs=P("filt", "row", "col"),
        check_vma=False,
    )
```

```python
import functools

import jax
import jax.numpy as jnp
from jax import lax
from jax.experimental import pallas as pl
from jax.experimental.pallas import tpu as pltpu
from jax.sharding import PartitionSpec as P

BF16, F32 = jnp.bfloat16, jnp.float32
VMEM = pl.BlockSpec(memory_space=pltpu.VMEM)
HBM = pl.BlockSpec(memory_space=pltpu.HBM)
PARAMS = pltpu.CompilerParams(vmem_limit_bytes=10 << 20)
BLOCK = 4


def relayout_kernel(chunks, x_ref, rim_ref, *refs):
    outs, col_ref = refs[:-1], refs[-1]
    slab, rows, width = x_ref.shape
    for base in range(0, rows, 8):
        group = jnp.swapaxes(x_ref[:, base : base + 8, :].astype(F32), 0, 1)
        for h in range(base, base + 8):
            pixels = group[h - base].T
            col_ref[h : h + 1, :] = pixels[0:1, :]
            col_ref[rows + h : rows + h + 1, :] = pixels[width - 1 : width, :]
            pixels = pixels.astype(BF16)
            if h == 0:
                rim_ref[0:width, :] = pixels
            elif h == rows - 1:
                rim_ref[width : 2 * width, :] = pixels
            else:
                for out, (first, last) in zip(outs, chunks):
                    if first <= h < last:
                        out[h - first] = pixels
    rim_ref[2 * width :, :] = col_ref[...].astype(BF16)


def relayout(features, chunks):
    slab, rows, width = features.shape
    shapes = [(2 * width + 2 * rows, slab)] + [(last - first, width, slab) for first, last in chunks]
    return pl.pallas_call(
        functools.partial(relayout_kernel, chunks),
        out_shape=[jax.ShapeDtypeStruct(s, BF16) for s in shapes],
        in_specs=[VMEM],
        out_specs=[VMEM] * len(shapes),
        scratch_shapes=[pltpu.VMEM((2 * rows, slab), F32)],
        compiler_params=PARAMS,
        name="relayout",
    )(features)


def put_row(x_ref, at, value):
    width, slab = value.shape
    edge = lax.broadcasted_iota(jnp.int32, (16, slab), 0)
    x_ref[1, at] = value
    x_ref[0, at, 0 : width - 16, :] = value[0 : width - 16]
    x_ref[0, at, width - 16 :, :] = jnp.where(edge == 15, 0, value[width - 16 :].astype(F32)).astype(BF16)
    x_ref[2, at, 16:, :] = value[16:]
    x_ref[2, at, 0:16, :] = jnp.where(edge == 0, 0, value[0:16].astype(F32)).astype(BF16)


def turn(part, b):
    return part if b == 1 else pltpu.roll(part, 1 if b == 0 else part.shape[0] - 1, 0)


def add_rows(spans, w_ref, total_ref, x_ref, written):
    height, width, _ = total_ref.shape
    slab = w_ref.shape[2]
    at = 0
    for piece, local, row, count in spans:
        for start in range(0, count, BLOCK):
            size = min(BLOCK, count - start)
            for i in range(size):
                put_row(x_ref, at + i, piece[local + start + i])
            for a in range(3):
                low = max(0, row + start + 1 - a)
                high = min(height, row + start + size + 1 - a)
                if high <= low:
                    continue
                skip = low - (row + start + 1 - a)
                n = high - low
                for b in range(3):
                    lhs = x_ref[b, at + skip : at + skip + n].reshape(n * width, slab)
                    part = jnp.dot(lhs, w_ref[a, b], preferred_element_type=F32).reshape(n, width, -1)
                    for i in range(n):
                        term = turn(part[i], b)
                        if low + i in written:
                            total_ref[low + i] += term
                        else:
                            total_ref[low + i] = term
                            written.add(low + i)
            at += size


def accumulate_kernel(spans, n, started, *refs):
    pieces, w_ref, total_ref, x_ref = refs[:n], refs[n], refs[-2], refs[-1]
    written = set(range(total_ref.shape[0])) if started else set()
    spans = [(pieces[p], local, row, count) for p, local, row, count in spans]
    add_rows(spans, w_ref, total_ref, x_ref, written)


def accumulate(spans, pieces, weights, total, shape, after=None, estimate=None):
    count = sum(s[3] for s in spans)
    width, slab = shape[1], weights.shape[2]
    operands = [*pieces, weights]
    aliases = {}
    if total is not None:
        aliases = {len(operands): 0}
        operands.append(total)
    if after is not None:
        operands.append(after)
    return pl.pallas_call(
        functools.partial(accumulate_kernel, spans, len(pieces), total is not None),
        out_shape=jax.ShapeDtypeStruct(shape, F32),
        in_specs=[VMEM] * len(operands),
        out_specs=VMEM,
        scratch_shapes=[pltpu.VMEM((3, count, width, slab), BF16)],
        input_output_aliases=aliases,
        compiler_params=PARAMS,
        cost_estimate=estimate or cost(count * width * 9, slab, shape[2]),
        name="accumulate",
    )(*operands)


def pick_kernel(low, high, rows_ref, after_ref, out_ref):
    out_ref[...] = rows_ref[low:high]


def pick(rows, low, high, after):
    shape = (high - low, *rows.shape[1:])
    return call(functools.partial(pick_kernel, low, high), "pick", shape, BF16, [rows, after], cost(1, 1, 1))


def cost(pixels, slab, outs):
    return pl.CostEstimate(flops=2 * pixels * slab * outs, bytes_accessed=1 << 20, transcendentals=0)


def edges_kernel(groups, *refs):
    rims, (above_ref, below_ref), outs, col_ref = refs[:groups], refs[groups : groups + 2], refs[-3:-1], refs[-1]
    width = above_ref.shape[1]
    height = col_ref.shape[0] - 2
    for side, out_ref in enumerate(outs):
        for g in range(groups):
            rows = rims[g][2 * width + side * height : 2 * width + (side + 1) * height, :].astype(F32)
            col_ref[1 : height + 1, :] = rows
            for row, ref in ((0, above_ref), (height + 1, below_ref)):
                if side:
                    col_ref[row : row + 1, :] = ref[g, width - 16 :, :].astype(F32)[15:16, :]
                else:
                    col_ref[row : row + 1, :] = ref[g, 0:16, :].astype(F32)[0:1, :]
            out_ref[g] = col_ref[...].astype(BF16)


def outer_rows_kernel(groups, above_ref, below_ref, *refs):
    w_refs, fix_ref, x_ref = refs[:groups], refs[-2], refs[-1]
    for i, (ref, a) in enumerate(((above_ref, 0), (below_ref, 2))):
        fix = None
        for g in range(groups):
            put_row(x_ref, 0, ref[g])
            for b in range(3):
                part = turn(jnp.dot(x_ref[b, 0], w_refs[g][a, b], preferred_element_type=F32), b)
                fix = part if fix is None else fix + part
        fix_ref[i] = fix


def outer_cols_kernel(groups, left_ref, right_ref, *refs):
    w_refs, fix_ref = refs[:groups], refs[-1]
    height = fix_ref.shape[1]
    for i, (ref, b) in enumerate(((left_ref, 0), (right_ref, 2))):
        fix = None
        for g in range(groups):
            pixels = ref[g]
            for a in range(3):
                part = jnp.dot(pixels, w_refs[g][a, b], preferred_element_type=F32)[a : a + height]
                fix = part if fix is None else fix + part
        fix_ref[i] = fix


def finish_row(total_ref, h, bias_ref, rows_ref, cols_ref):
    height, width = cols_ref.shape[1], total_ref.shape[1]
    value = total_ref[h] + bias_ref[...]
    if h == 0:
        value += rows_ref[0]
    if h == height - 1:
        value += rows_ref[1]
    edge = lax.broadcasted_iota(jnp.int32, (8, value.shape[1]), 0)
    first = value[0:8] + jnp.where(edge == 0, cols_ref[0, h : h + 1, :], 0)
    final = value[width - 8 :] + jnp.where(edge == 7, cols_ref[1, h : h + 1, :], 0)
    return jnp.concatenate([first, value[8 : width - 8], final], 0)


def store_rows(total_ref, bias_ref, rows_ref, cols_ref, rows, out_ref):
    turned = jnp.stack([finish_row(total_ref, h, bias_ref, rows_ref, cols_ref).T for h in rows], 0)
    out_ref[...] = jnp.swapaxes(turned, 0, 1).astype(BF16)


def upper_kernel(total_ref, bias_ref, rows_ref, cols_ref, out_ref):
    store_rows(total_ref, bias_ref, rows_ref, cols_ref, range(out_ref.shape[1]), out_ref)


def last_kernel(span, piece, w_ref, total_in, bias_ref, rows_ref, cols_ref, upper_ref, out_ref, total_ref, x_ref, lower_ref, sems):
    half = upper_ref.shape[1]
    height = out_ref.shape[1]
    first = pltpu.make_async_copy(upper_ref, out_ref.at[:, 0:half, :], sems.at[0])
    first.start()
    total_ref[half:] = total_in[half:]
    add_rows([(piece, *span)], w_ref, total_ref, x_ref, set(range(height)))
    store_rows(total_ref, bias_ref, rows_ref, cols_ref, range(half, height), lower_ref)
    second = pltpu.make_async_copy(lower_ref, out_ref.at[:, half:height, :], sems.at[1])
    second.start()
    first.wait()
    second.wait()


def call(kernel, name, shape, dtype, operands, estimate, scratch=(), out=VMEM):
    return pl.pallas_call(
        kernel,
        out_shape=jax.ShapeDtypeStruct(shape, dtype),
        in_specs=[VMEM] * len(operands),
        out_specs=out,
        scratch_shapes=scratch,
        compiler_params=PARAMS,
        cost_estimate=estimate,
        name=name,
    )(*operands)


def weights_kernel(groups, kernel_ref, bias_ref, *refs):
    outs, own_bias_ref, sems = refs[:-2], refs[-2], refs[-1]
    slab, width = outs[0].shape[2:]
    owner = lax.axis_index("filt")
    own = pl.ds(pl.multiple_of(owner * width, width), width)
    copies = []
    for shift, out in enumerate(outs):
        group = lax.rem(owner - shift + groups, groups)
        source = kernel_ref.at[:, :, pl.ds(pl.multiple_of(group * slab, slab), slab), own]
        copies.append(pltpu.make_async_copy(source, out, sems.at[shift]))
    for copy in copies:
        copy.start()
    own_bias_ref[...] = bias_ref[:, own]
    for copy in copies:
        copy.wait()


def split_weights(kernel, bias, groups, slab, outs):
    if outs % 128 == 0 and slab % 128 == 0:
        shapes = [jax.ShapeDtypeStruct((3, 3, slab, outs), BF16)] * groups
        return pl.pallas_call(
            functools.partial(weights_kernel, groups),
            out_shape=[*shapes, jax.ShapeDtypeStruct((1, outs), F32)],
            in_specs=[HBM, VMEM],
            out_specs=[VMEM] * (groups + 1),
            scratch_shapes=[pltpu.SemaphoreType.DMA((groups,))],
            compiler_params=pltpu.CompilerParams(vmem_limit_bytes=48 << 20),
            name="split_weights",
        )(kernel, bias)
    owner = lax.axis_index("filt")
    own = lax.dynamic_slice_in_dim(kernel, owner * outs, outs, 3)
    order = [lax.rem(owner - shift + groups, groups) for shift in range(groups)]
    weights = [lax.dynamic_slice_in_dim(own, group * slab, slab, 2) for group in order]
    return [*weights, lax.dynamic_slice_in_dim(bias, owner * outs, outs, 1)]


def body(features, kernel, bias):
    groups = lax.axis_size("filt")
    slab, height, width = features.shape
    outs = kernel.shape[3] // groups
    half = height // 2
    chunks = ((1, half), (half, height - 3), (height - 3, height - 1))

    rim, upper_rows, lower_rows = relayout(features, ((1, half), (half, height - 1)))
    rings = [[(i, (i + shift) % groups) for i in range(groups)] for shift in range(1, groups)]
    rims = [rim] + [lax.ppermute(rim, "filt", ring) for ring in rings]
    sets = [[lax.ppermute(upper_rows, "filt", ring)] for ring in rings]
    pairs = [r[0 : 2 * width].reshape(2, width, slab) for r in rims]
    outer = [(0, 0, 0, 1), (0, 1, height - 1, 1)]
    shape = (height, width, outs)

    *weights, bias = split_weights(kernel, bias[None, :], groups, slab, outs)
    spans = [*outer, (1, 0, 1, half - 1), (2, 0, half, half - 1)]
    total = accumulate(spans, [pairs[0], upper_rows, lower_rows], weights[0], None, shape)
    second = pick(lower_rows, 0, chunks[1][1] - half, weights[0])
    for received, ring in zip(sets, rings):
        received.append(lax.ppermute(second, "filt", ring))

    count = lax.axis_size("row")
    forward = [(i, i + 1) for i in range(count - 1)]
    backward = [(t, s) for s, t in forward]
    below = lax.ppermute(jnp.stack([r[0:width] for r in rims]), "row", backward)
    above = lax.ppermute(jnp.stack([r[width : 2 * width] for r in rims]), "row", forward)
    for g in range(1, groups):
        total = accumulate(outer, [pairs[g]], weights[g], total, shape)
        total = accumulate([(0, 0, chunks[0][0], half - 1)], [sets[g - 1][0]], weights[g], total, shape)
    third = pick(lower_rows, chunks[2][0] - half, chunks[2][1] - half, total)
    for received, ring in zip(sets, rings):
        received.append(lax.ppermute(third, "filt", ring))
    count = lax.axis_size("col")
    forward = [(i, i + 1) for i in range(count - 1)]
    backward = [(t, s) for s, t in forward]
    columns = [jax.ShapeDtypeStruct((groups, height + 2, slab), BF16)] * 2
    first, final = pl.pallas_call(
        functools.partial(edges_kernel, groups),
        out_shape=columns,
        in_specs=[VMEM] * (groups + 3),
        out_specs=[VMEM] * 2,
        scratch_shapes=[pltpu.VMEM((height + 2, slab), F32)],
        compiler_params=PARAMS,
        cost_estimate=cost(1, 1, 1),
        name="edges",
    )(*rims, above, below, total)
    left = lax.ppermute(final, "col", forward)
    right = lax.ppermute(first, "col", backward)

    rows_fix = call(
        functools.partial(outer_rows_kernel, groups), "outer_rows", (2, width, outs), F32,
        [above, below, *weights, first], cost(6 * width * groups, slab, outs), [pltpu.VMEM((3, 1, width, slab), BF16)],
    )
    for g in range(1, groups):
        b, c = sets[g - 1][1:]
        total = accumulate([(0, 0, chunks[1][0], b.shape[0])], [b], weights[g], total, shape, rows_fix)
        if g < groups - 1:
            total = accumulate([(0, 0, chunks[2][0], c.shape[0])], [c], weights[g], total, shape)
    cols_fix = call(
        functools.partial(outer_cols_kernel, groups), "outer_cols", (2, height, outs), F32,
        [left, right, *weights, total], cost(6 * 256 * groups, slab, outs),
    )
    top = call(upper_kernel, "upper", (outs, half, width), BF16, [total, bias, rows_fix, cols_fix], cost(256, slab, outs))
    scratch = [
        pltpu.VMEM(shape, F32),
        pltpu.VMEM((3, c.shape[0], width, slab), BF16),
        pltpu.VMEM((outs, height - half, width), BF16),
        pltpu.SemaphoreType.DMA((2,)),
    ]
    span = (0, chunks[2][0], c.shape[0])
    return call(
        functools.partial(last_kernel, span), "last", (outs, height, width), BF16,
        [c, weights[-1], total, bias, rows_fix, cols_fix, top], cost(9 * 256, slab, outs), scratch, HBM,
    )


def solution(mesh):
    return jax.shard_map(
        body,
        mesh=mesh,
        in_specs=(P("filt", "row", "col"), P(), P()),
        out_specs=P("filt", "row", "col"),
        check_vma=False,
    )
```

```python
import functools

import jax
import jax.numpy as jnp
from jax import lax
from jax.experimental import pallas as pl
from jax.experimental.pallas import tpu as pltpu
from jax.sharding import PartitionSpec as P

BF16, F32 = jnp.bfloat16, jnp.float32
VMEM = pl.BlockSpec(memory_space=pltpu.VMEM)
HBM = pl.BlockSpec(memory_space=pltpu.HBM)
PARAMS = pltpu.CompilerParams(vmem_limit_bytes=10 << 20)
WAIT = pl.CostEstimate(flops=6 * 10**9, bytes_accessed=1 << 20, transcendentals=0)
BLOCK = 4


def relayout_kernel(chunks, x_ref, rim_ref, *refs):
    outs, col_ref = refs[:-1], refs[-1]
    slab, rows, width = x_ref.shape
    for base in range(0, rows, 8):
        group = jnp.swapaxes(x_ref[:, base : base + 8, :].astype(F32), 0, 1)
        for h in range(base, base + 8):
            pixels = group[h - base].T
            col_ref[h : h + 1, :] = pixels[0:1, :]
            col_ref[rows + h : rows + h + 1, :] = pixels[width - 1 : width, :]
            pixels = pixels.astype(BF16)
            if h == 0:
                rim_ref[0:width, :] = pixels
            elif h == rows - 1:
                rim_ref[width : 2 * width, :] = pixels
            else:
                for out, (first, last) in zip(outs, chunks):
                    if first <= h < last:
                        out[h - first] = pixels
    rim_ref[2 * width :, :] = col_ref[...].astype(BF16)


def relayout(features, chunks):
    slab, rows, width = features.shape
    shapes = [(2 * width + 2 * rows, slab)] + [(last - first, width, slab) for first, last in chunks]
    return pl.pallas_call(
        functools.partial(relayout_kernel, chunks),
        out_shape=[jax.ShapeDtypeStruct(s, BF16) for s in shapes],
        in_specs=[VMEM],
        out_specs=[VMEM] * len(shapes),
        scratch_shapes=[pltpu.VMEM((2 * rows, slab), F32)],
        compiler_params=PARAMS,
        name="relayout",
    )(features)


def put_row(x_ref, at, value):
    width, slab = value.shape
    edge = lax.broadcasted_iota(jnp.int32, (16, slab), 0)
    x_ref[1, at] = value
    x_ref[0, at, 0 : width - 16, :] = value[0 : width - 16]
    x_ref[0, at, width - 16 :, :] = jnp.where(edge == 15, 0, value[width - 16 :].astype(F32)).astype(BF16)
    x_ref[2, at, 16:, :] = value[16:]
    x_ref[2, at, 0:16, :] = jnp.where(edge == 0, 0, value[0:16].astype(F32)).astype(BF16)


def turn(part, b):
    return part if b == 1 else pltpu.roll(part, 1 if b == 0 else part.shape[0] - 1, 0)


def add_rows(spans, w_ref, total_ref, x_ref, written):
    height, width, _ = total_ref.shape
    slab = w_ref.shape[2]
    at = 0
    for piece, local, row, count in spans:
        for start in range(0, count, BLOCK):
            size = min(BLOCK, count - start)
            for i in range(size):
                put_row(x_ref, at + i, piece[local + start + i])
            for a in range(3):
                low = max(0, row + start + 1 - a)
                high = min(height, row + start + size + 1 - a)
                if high <= low:
                    continue
                skip = low - (row + start + 1 - a)
                n = high - low
                for b in range(3):
                    lhs = x_ref[b, at + skip : at + skip + n].reshape(n * width, slab)
                    part = jnp.dot(lhs, w_ref[a, b], preferred_element_type=F32).reshape(n, width, -1)
                    for i in range(n):
                        term = turn(part[i], b)
                        if low + i in written:
                            total_ref[low + i] += term
                        else:
                            total_ref[low + i] = term
                            written.add(low + i)
            at += size


def accumulate_kernel(spans, n, started, *refs):
    pieces, w_ref, total_ref, x_ref = refs[:n], refs[n], refs[-2], refs[-1]
    written = set(range(total_ref.shape[0])) if started else set()
    spans = [(pieces[p], local, row, count) for p, local, row, count in spans]
    add_rows(spans, w_ref, total_ref, x_ref, written)


def accumulate(spans, pieces, weights, total, shape, after=None, estimate=None):
    count = sum(s[3] for s in spans)
    width, slab = shape[1], weights.shape[2]
    operands = [*pieces, weights]
    aliases = {}
    if total is not None:
        aliases = {len(operands): 0}
        operands.append(total)
    if after is not None:
        operands.append(after)
    return pl.pallas_call(
        functools.partial(accumulate_kernel, spans, len(pieces), total is not None),
        out_shape=jax.ShapeDtypeStruct(shape, F32),
        in_specs=[VMEM] * len(operands),
        out_specs=VMEM,
        scratch_shapes=[pltpu.VMEM((3, count, width, slab), BF16)],
        input_output_aliases=aliases,
        compiler_params=PARAMS,
        cost_estimate=estimate or cost(count * width * 9, slab, shape[2]),
        name="accumulate",
    )(*operands)


def pick_kernel(low, high, rows_ref, after_ref, out_ref):
    out_ref[...] = rows_ref[low:high]


def pick(rows, low, high, after):
    shape = (high - low, *rows.shape[1:])
    return call(functools.partial(pick_kernel, low, high), "pick", shape, BF16, [rows, after], cost(1, 1, 1))


def cost(pixels, slab, outs):
    return pl.CostEstimate(flops=2 * pixels * slab * outs, bytes_accessed=1 << 20, transcendentals=0)


def parity(axis):
    return lax.rem(lax.axis_index(axis), 2)


def swap_pairs(axis):
    count = lax.axis_size(axis)
    return [[p for i in range(start, count - 1, 2) for p in ((i, i + 1), (i + 1, i))] for start in (1, 0)]


def outermost_kernel(groups, *refs):
    rims, outs = refs[:groups], refs[-2:]
    width = outs[0].shape[1]
    odd = parity("row")
    for swap, out_ref in enumerate(outs):
        start = pl.multiple_of((odd if swap == 0 else 1 - odd) * width, width)
        for g in range(groups):
            out_ref[g] = rims[g][pl.ds(start, width), :]


def edges_kernel(groups, *refs):
    rims, swapped, outs, col_ref = refs[:groups], refs[groups : groups + 2], refs[-3:-1], refs[-1]
    width = swapped[0].shape[1]
    height = outs[0].shape[1] - 2
    odd_row, odd_col = parity("row") == 1, parity("col") == 1
    for g in range(groups):
        for side, at in enumerate((0, width - 16)):
            pixels = [ref[g, at : at + 16, :].astype(F32)[side * 15 : side * 15 + 1, :] for ref in swapped]
            start = 2 * width + side * height
            col_ref[side, 0:1, :] = jnp.where(odd_row, pixels[1], pixels[0])
            col_ref[side, 1 : height + 1, :] = rims[g][start : start + height, :].astype(F32)
            col_ref[side, height + 1 :, :] = jnp.where(odd_row, pixels[0], pixels[1])
        outs[0][g] = jnp.where(odd_col, col_ref[1], col_ref[0]).astype(BF16)
        outs[1][g] = jnp.where(odd_col, col_ref[0], col_ref[1]).astype(BF16)


def outer_rows_kernel(groups, *refs):
    swapped, w_refs, fix_ref, x_ref = refs[:2], refs[2 : 2 + groups], refs[-2], refs[-1]
    odd = parity("row") == 1
    for i, a in enumerate((0, 2)):
        fix = None
        for g in range(groups):
            put_row(x_ref, 0, jnp.where(odd, swapped[1 - i][g], swapped[i][g]))
            for b in range(3):
                part = turn(jnp.dot(x_ref[b, 0], w_refs[g][a, b], preferred_element_type=F32), b)
                fix = part if fix is None else fix + part
        fix_ref[i] = fix


def outer_cols_kernel(groups, *refs):
    swapped, w_refs, fix_ref = refs[:2], refs[2 : 2 + groups], refs[-1]
    height = fix_ref.shape[1]
    odd = parity("col") == 1
    for i, b in enumerate((0, 2)):
        fix = None
        for g in range(groups):
            pixels = jnp.where(odd, swapped[1 - i][g], swapped[i][g])
            for a in range(3):
                part = jnp.dot(pixels, w_refs[g][a, b], preferred_element_type=F32)[a : a + height]
                fix = part if fix is None else fix + part
        fix_ref[i] = fix


def finish_row(total_ref, h, bias_ref, rows_ref, cols_ref):
    height, width = cols_ref.shape[1], total_ref.shape[1]
    outs = total_ref.shape[2]
    if bias_ref.shape[1] == outs:
        bias = bias_ref[...]
    else:
        bias = bias_ref[:, pl.ds(pl.multiple_of(lax.axis_index("filt") * outs, outs), outs)]
    value = total_ref[h] + bias
    if h == 0:
        value += rows_ref[0]
    if h == height - 1:
        value += rows_ref[1]
    edge = lax.broadcasted_iota(jnp.int32, (8, value.shape[1]), 0)
    first = value[0:8] + jnp.where(edge == 0, cols_ref[0, h : h + 1, :], 0)
    final = value[width - 8 :] + jnp.where(edge == 7, cols_ref[1, h : h + 1, :], 0)
    return jnp.concatenate([first, value[8 : width - 8], final], 0)


def store_rows(total_ref, bias_ref, rows_ref, cols_ref, rows, out_ref):
    turned = jnp.stack([finish_row(total_ref, h, bias_ref, rows_ref, cols_ref).T for h in rows], 0)
    out_ref[...] = jnp.swapaxes(turned, 0, 1).astype(BF16)


def upper_kernel(total_ref, bias_ref, rows_ref, cols_ref, out_ref):
    store_rows(total_ref, bias_ref, rows_ref, cols_ref, range(out_ref.shape[1]), out_ref)


def last_kernel(span, piece, w_ref, total_in, bias_ref, rows_ref, cols_ref, upper_ref, out_ref, total_ref, x_ref, lower_ref, sems):
    half = upper_ref.shape[1]
    height = out_ref.shape[1]
    first = pltpu.make_async_copy(upper_ref, out_ref.at[:, 0:half, :], sems.at[0])
    first.start()
    total_ref[half:] = total_in[half:]
    add_rows([(piece, *span)], w_ref, total_ref, x_ref, set(range(height)))
    store_rows(total_ref, bias_ref, rows_ref, cols_ref, range(half, height), lower_ref)
    second = pltpu.make_async_copy(lower_ref, out_ref.at[:, half:height, :], sems.at[1])
    second.start()
    first.wait()
    second.wait()


def call(kernel, name, shape, dtype, operands, estimate, scratch=(), out=VMEM):
    return pl.pallas_call(
        kernel,
        out_shape=jax.ShapeDtypeStruct(shape, dtype),
        in_specs=[VMEM] * len(operands),
        out_specs=out,
        scratch_shapes=scratch,
        compiler_params=PARAMS,
        cost_estimate=estimate,
        name=name,
    )(*operands)


def calls(kernel, name, shapes, operands, scratch=(), estimate=None):
    return pl.pallas_call(
        kernel,
        out_shape=[jax.ShapeDtypeStruct(shape, BF16) for shape in shapes],
        in_specs=[VMEM] * len(operands),
        out_specs=[VMEM] * len(shapes),
        scratch_shapes=scratch,
        compiler_params=PARAMS,
        cost_estimate=estimate or cost(1, 1, 1),
        name=name,
    )(*operands)


def weights_kernel(groups, kernel_ref, *refs):
    outs, sems = refs[:-1], refs[-1]
    slab, width = outs[0].shape[2:]
    owner = lax.axis_index("filt")
    own = pl.ds(pl.multiple_of(owner * width, width), width)
    copies = []
    for shift, out in enumerate(outs):
        group = pl.ds(pl.multiple_of(lax.rem(owner - shift + groups, groups) * slab, slab), slab)
        for a in range(3):
            copies.append(pltpu.make_async_copy(kernel_ref.at[a, :, group, own], out.at[a], sems.at[shift, a]))
    for copy in copies:
        copy.start()
    for copy in copies:
        copy.wait()


def split_weights(kernel, groups, slab, outs):
    if outs % 128 == 0 and slab % 128 == 0:
        return pl.pallas_call(
            functools.partial(weights_kernel, groups),
            out_shape=[jax.ShapeDtypeStruct((3, 3, slab, outs), BF16)] * groups,
            in_specs=[HBM],
            out_specs=[VMEM] * groups,
            scratch_shapes=[pltpu.SemaphoreType.DMA((groups, 3))],
            compiler_params=pltpu.CompilerParams(vmem_limit_bytes=48 << 20),
            name="split_weights",
        )(kernel)
    owner = lax.axis_index("filt")
    own = lax.dynamic_slice_in_dim(kernel, owner * outs, outs, 3)
    order = [lax.rem(owner - shift + groups, groups) for shift in range(groups)]
    return [lax.dynamic_slice_in_dim(own, group * slab, slab, 2) for group in order]


def body(features, kernel, bias):
    groups = lax.axis_size("filt")
    slab, height, width = features.shape
    outs = kernel.shape[3] // groups
    half = height // 2
    chunks = ((1, half), (half, height - 3), (height - 3, height - 1))

    rim, upper_rows, lower_rows = relayout(features, ((1, half), (half, height - 1)))
    rings = [[(i, (i + shift) % groups) for i in range(groups)] for shift in range(1, groups)]
    rims = [rim] + [lax.ppermute(rim, "filt", ring) for ring in rings]
    sets = [[lax.ppermute(upper_rows, "filt", ring)] for ring in rings]
    pairs = [r[0 : 2 * width].reshape(2, width, slab) for r in rims]
    outer = [(0, 0, 0, 1), (0, 1, height - 1, 1)]
    shape = (height, width, outs)

    weights = split_weights(kernel, groups, slab, outs)
    bias = bias[None, :]
    if outs % 128 != 0:
        bias = lax.dynamic_slice_in_dim(bias, lax.axis_index("filt") * outs, outs, 1)
    spans = [*outer, (1, 0, 1, half - 1), (2, 0, half, half - 1)]
    second = pick(lower_rows, 0, chunks[1][1] - half, weights[0])
    for received, ring in zip(sets, rings):
        received.append(lax.ppermute(second, "filt", ring))

    row_pairs, col_pairs = swap_pairs("row"), swap_pairs("col")
    sent = calls(functools.partial(outermost_kernel, groups), "outermost", [(groups, width, slab)] * 2, rims, estimate=WAIT)
    outer_rows = [lax.ppermute(v, "row", p) for v, p in zip(sent, row_pairs)]
    total = accumulate(spans, [pairs[0], upper_rows, lower_rows], weights[0], None, shape, rims[-1])
    for g in range(1, groups):
        total = accumulate(outer, [pairs[g]], weights[g], total, shape)
    third = pick(lower_rows, chunks[2][0] - half, chunks[2][1] - half, total)
    for received, ring in zip(sets, rings):
        received.append(lax.ppermute(third, "filt", ring))

    edge = pltpu.VMEM((2, height + 2, slab), F32)
    sent = calls(functools.partial(edges_kernel, groups), "edges", [(groups, height + 2, slab)] * 2, [*rims, *outer_rows, third], [edge])
    outer_cols = [lax.ppermute(v, "col", p) for v, p in zip(sent, col_pairs)]
    rows_fix = call(
        functools.partial(outer_rows_kernel, groups), "outer_rows", (2, width, outs), F32,
        [*outer_rows, *weights, *sent], cost(6 * width * groups, slab, outs), [pltpu.VMEM((3, 1, width, slab), BF16)],
    )
    for g in range(1, groups):
        a, b, c = sets[g - 1]
        total = accumulate([(0, 0, chunks[0][0], half - 1)], [a], weights[g], total, shape, rows_fix)
        total = accumulate([(0, 0, chunks[1][0], b.shape[0])], [b], weights[g], total, shape)
        if g < groups - 1:
            total = accumulate([(0, 0, chunks[2][0], c.shape[0])], [c], weights[g], total, shape)
    cols_fix = call(
        functools.partial(outer_cols_kernel, groups), "outer_cols", (2, height, outs), F32,
        [*outer_cols, *weights, total], cost(6 * 256 * groups, slab, outs),
    )
    top = call(upper_kernel, "upper", (outs, half, width), BF16, [total, bias, rows_fix, cols_fix], cost(256, slab, outs))
    scratch = [
        pltpu.VMEM(shape, F32),
        pltpu.VMEM((3, c.shape[0], width, slab), BF16),
        pltpu.VMEM((outs, height - half, width), BF16),
        pltpu.SemaphoreType.DMA((2,)),
    ]
    span = (0, chunks[2][0], c.shape[0])
    return call(
        functools.partial(last_kernel, span), "last", (outs, height, width), BF16,
        [c, weights[-1], total, bias, rows_fix, cols_fix, top], cost(9 * 256, slab, outs), scratch, HBM,
    )


def solution(mesh):
    return jax.shard_map(
        body,
        mesh=mesh,
        in_specs=(P("filt", "row", "col"), P(), P()),
        out_specs=P("filt", "row", "col"),
        check_vma=False,
    )
```

```python
import functools

import jax
import jax.numpy as jnp
from jax import lax
from jax.experimental import pallas as pl
from jax.experimental.pallas import tpu as pltpu
from jax.sharding import PartitionSpec as P

BF16, F32 = jnp.bfloat16, jnp.float32
VMEM = pl.BlockSpec(memory_space=pltpu.VMEM)
HBM = pl.BlockSpec(memory_space=pltpu.HBM)
PARAMS = pltpu.CompilerParams(vmem_limit_bytes=10 << 20)
WAIT = pl.CostEstimate(flops=4 * 10**9, bytes_accessed=1 << 20, transcendentals=0)
BLOCK = 4


def relayout_kernel(chunks, x_ref, rim_ref, *refs):
    outs, col_ref = refs[:-1], refs[-1]
    slab, rows, width = x_ref.shape
    for base in range(0, rows, 8):
        group = jnp.swapaxes(x_ref[:, base : base + 8, :].astype(F32), 0, 1)
        for h in range(base, base + 8):
            pixels = group[h - base].T
            col_ref[h : h + 1, :] = pixels[0:1, :]
            col_ref[rows + h : rows + h + 1, :] = pixels[width - 1 : width, :]
            pixels = pixels.astype(BF16)
            if h == 0:
                rim_ref[0:width, :] = pixels
            elif h == rows - 1:
                rim_ref[width : 2 * width, :] = pixels
            else:
                for out, (first, last) in zip(outs, chunks):
                    if first <= h < last:
                        out[h - first] = pixels
    rim_ref[2 * width :, :] = col_ref[...].astype(BF16)


def relayout(features, chunks):
    slab, rows, width = features.shape
    shapes = [(2 * width + 2 * rows, slab)] + [(last - first, width, slab) for first, last in chunks]
    return pl.pallas_call(
        functools.partial(relayout_kernel, chunks),
        out_shape=[jax.ShapeDtypeStruct(s, BF16) for s in shapes],
        in_specs=[VMEM],
        out_specs=[VMEM] * len(shapes),
        scratch_shapes=[pltpu.VMEM((2 * rows, slab), F32)],
        compiler_params=PARAMS,
        name="relayout",
    )(features)


def put_row(x_ref, at, value):
    width, slab = value.shape
    edge = lax.broadcasted_iota(jnp.int32, (16, slab), 0)
    x_ref[1, at] = value
    x_ref[0, at, 0 : width - 16, :] = value[0 : width - 16]
    x_ref[0, at, width - 16 :, :] = jnp.where(edge == 15, 0, value[width - 16 :].astype(F32)).astype(BF16)
    x_ref[2, at, 16:, :] = value[16:]
    x_ref[2, at, 0:16, :] = jnp.where(edge == 0, 0, value[0:16].astype(F32)).astype(BF16)


def turn(part, b):
    return part if b == 1 else pltpu.roll(part, 1 if b == 0 else part.shape[0] - 1, 0)


def add_rows(spans, w_ref, total_ref, x_ref, written, initial=None):
    height, width, _ = total_ref.shape
    slab = w_ref.shape[2]
    at = 0
    for piece, local, row, count in spans:
        for start in range(0, count, BLOCK):
            size = min(BLOCK, count - start)
            for i in range(size):
                put_row(x_ref, at + i, piece[local + start + i])
            for a in range(3):
                low = max(0, row + start + 1 - a)
                high = min(height, row + start + size + 1 - a)
                if high <= low:
                    continue
                skip = low - (row + start + 1 - a)
                n = high - low
                for b in range(3):
                    lhs = x_ref[b, at + skip : at + skip + n].reshape(n * width, slab)
                    part = jnp.dot(lhs, w_ref[a, b], preferred_element_type=F32).reshape(n, width, -1)
                    for i in range(n):
                        term = turn(part[i], b)
                        if low + i in written:
                            total_ref[low + i] += term
                        else:
                            total_ref[low + i] = term + initial
                            written.add(low + i)
            at += size


def accumulate_kernel(spans, n, started, *refs):
    pieces, w_ref, total_ref, x_ref = refs[:n], refs[n], refs[-2], refs[-1]
    written = set(range(total_ref.shape[0])) if started else set()
    spans = [(pieces[p], local, row, count) for p, local, row, count in spans]
    add_rows(spans, w_ref, total_ref, x_ref, written, None if started else own_bias(refs[n + 1], total_ref.shape[2]))


def own_bias(bias_ref, outs):
    if bias_ref.shape[1] == outs:
        return bias_ref[...]
    return bias_ref[:, pl.ds(pl.multiple_of(lax.axis_index("filt") * outs, outs), outs)]


def accumulate(spans, pieces, weights, total, shape, after=None, bias=None):
    count = sum(s[3] for s in spans)
    width, slab = shape[1], weights.shape[2]
    operands = [*pieces, weights]
    aliases = {}
    if total is not None:
        aliases = {len(operands): 0}
        operands.append(total)
    else:
        operands.append(bias)
    if after is not None:
        operands.append(after)
    return pl.pallas_call(
        functools.partial(accumulate_kernel, spans, len(pieces), total is not None),
        out_shape=jax.ShapeDtypeStruct(shape, F32),
        in_specs=[VMEM] * len(operands),
        out_specs=VMEM,
        scratch_shapes=[pltpu.VMEM((3, count, width, slab), BF16)],
        input_output_aliases=aliases,
        compiler_params=PARAMS,
        cost_estimate=cost(count * width * 9, slab, shape[2]),
        name="accumulate",
    )(*operands)


def pick_kernel(low, high, rows_ref, after_ref, out_ref):
    out_ref[...] = rows_ref[low:high]


def pick(rows, low, high, after):
    shape = (high - low, *rows.shape[1:])
    return call(functools.partial(pick_kernel, low, high), "pick", shape, BF16, [rows, after], cost(1, 1, 1))


def cost(pixels, slab, outs):
    return pl.CostEstimate(flops=2 * pixels * slab * outs, bytes_accessed=1 << 20, transcendentals=0)


def parity(axis):
    return lax.rem(lax.axis_index(axis), 2)


def swap_pairs(axis):
    count = lax.axis_size(axis)
    return [[p for i in range(start, count - 1, 2) for p in ((i, i + 1), (i + 1, i))] for start in (1, 0)]


def outermost_kernel(groups, *refs):
    rims, outs = refs[:groups], refs[-2:]
    width = outs[0].shape[1]
    odd = parity("row")
    for swap, out_ref in enumerate(outs):
        start = pl.multiple_of((odd if swap == 0 else 1 - odd) * width, width)
        for g in range(groups):
            out_ref[g] = rims[g][pl.ds(start, width), :]


def edges_kernel(groups, *refs):
    rims, swapped, outs, col_ref = refs[:groups], refs[groups : groups + 2], refs[-3:-1], refs[-1]
    width = swapped[0].shape[1]
    height = outs[0].shape[1] - 2
    odd_row, odd_col = parity("row") == 1, parity("col") == 1
    for g in range(groups):
        for side, at in enumerate((0, width - 16)):
            pixels = [ref[g, at : at + 16, :].astype(F32)[side * 15 : side * 15 + 1, :] for ref in swapped]
            start = 2 * width + side * height
            col_ref[side, 0:1, :] = jnp.where(odd_row, pixels[1], pixels[0])
            col_ref[side, 1 : height + 1, :] = rims[g][start : start + height, :].astype(F32)
            col_ref[side, height + 1 :, :] = jnp.where(odd_row, pixels[0], pixels[1])
        outs[0][g] = jnp.where(odd_col, col_ref[1], col_ref[0]).astype(BF16)
        outs[1][g] = jnp.where(odd_col, col_ref[0], col_ref[1]).astype(BF16)


def outer_rows_kernel(groups, *refs):
    swapped, w_refs, fix_ref, x_ref = refs[:2], refs[2 : 2 + groups], refs[-2], refs[-1]
    odd = parity("row") == 1
    for i, a in enumerate((0, 2)):
        fix = None
        for g in range(groups):
            put_row(x_ref, 0, jnp.where(odd, swapped[1 - i][g], swapped[i][g]))
            for b in range(3):
                part = turn(jnp.dot(x_ref[b, 0], w_refs[g][a, b], preferred_element_type=F32), b)
                fix = part if fix is None else fix + part
        fix_ref[i] = fix


def outer_cols_kernel(groups, *refs):
    swapped, w_refs, fix_ref = refs[:2], refs[2 : 2 + groups], refs[-1]
    height = fix_ref.shape[1]
    odd = parity("col") == 1
    for i, b in enumerate((0, 2)):
        fix = None
        for g in range(groups):
            pixels = jnp.where(odd, swapped[1 - i][g], swapped[i][g])
            for a in range(3):
                part = jnp.dot(pixels, w_refs[g][a, b], preferred_element_type=F32)[a : a + height]
                fix = part if fix is None else fix + part
        fix_ref[i] = fix


def finish_row(total_ref, h, rows_ref, cols_ref):
    height, width = cols_ref.shape[1], total_ref.shape[1]
    value = total_ref[h]
    if h == 0:
        value += rows_ref[0]
    if h == height - 1:
        value += rows_ref[1]
    edge = lax.broadcasted_iota(jnp.int32, (8, value.shape[1]), 0)
    first = value[0:8] + jnp.where(edge == 0, cols_ref[0, h : h + 1, :], 0)
    final = value[width - 8 :] + jnp.where(edge == 7, cols_ref[1, h : h + 1, :], 0)
    return jnp.concatenate([first, value[8 : width - 8], final], 0)


def store_rows(total_ref, rows_ref, cols_ref, rows, out_ref):
    turned = jnp.stack([finish_row(total_ref, h, rows_ref, cols_ref).T for h in rows], 0)
    out_ref[...] = jnp.swapaxes(turned, 0, 1).astype(BF16)


def upper_kernel(total_ref, rows_ref, cols_ref, out_ref):
    store_rows(total_ref, rows_ref, cols_ref, range(out_ref.shape[1]), out_ref)


def last_kernel(span, piece, w_ref, total_in, rows_ref, cols_ref, upper_ref, out_ref, total_ref, x_ref, lower_ref, sems):
    half = upper_ref.shape[1]
    height = out_ref.shape[1]
    first = pltpu.make_async_copy(upper_ref, out_ref.at[:, 0:half, :], sems.at[0])
    first.start()
    total_ref[half:] = total_in[half:]
    add_rows([(piece, *span)], w_ref, total_ref, x_ref, set(range(height)))
    store_rows(total_ref, rows_ref, cols_ref, range(half, height), lower_ref)
    second = pltpu.make_async_copy(lower_ref, out_ref.at[:, half:height, :], sems.at[1])
    second.start()
    first.wait()
    second.wait()


def call(kernel, name, shape, dtype, operands, estimate, scratch=(), out=VMEM):
    return pl.pallas_call(
        kernel,
        out_shape=jax.ShapeDtypeStruct(shape, dtype),
        in_specs=[VMEM] * len(operands),
        out_specs=out,
        scratch_shapes=scratch,
        compiler_params=PARAMS,
        cost_estimate=estimate,
        name=name,
    )(*operands)


def calls(kernel, name, shapes, operands, scratch=(), estimate=None):
    return pl.pallas_call(
        kernel,
        out_shape=[jax.ShapeDtypeStruct(shape, BF16) for shape in shapes],
        in_specs=[VMEM] * len(operands),
        out_specs=[VMEM] * len(shapes),
        scratch_shapes=scratch,
        compiler_params=PARAMS,
        cost_estimate=estimate or cost(1, 1, 1),
        name=name,
    )(*operands)


def weights_kernel(groups, kernel_ref, *refs):
    outs, sems = refs[:-1], refs[-1]
    slab, width = outs[0].shape[2:]
    owner = lax.axis_index("filt")
    own = pl.ds(pl.multiple_of(owner * width, width), width)
    copies = []
    for shift, out in enumerate(outs):
        group = pl.ds(pl.multiple_of(lax.rem(owner - shift + groups, groups) * slab, slab), slab)
        for a in range(3):
            copies.append(pltpu.make_async_copy(kernel_ref.at[a, :, group, own], out.at[a], sems.at[shift, a]))
    for copy in copies:
        copy.start()
    for copy in copies:
        copy.wait()


def split_weights(kernel, groups, slab, outs):
    if outs % 128 == 0 and slab % 128 == 0:
        return pl.pallas_call(
            functools.partial(weights_kernel, groups),
            out_shape=[jax.ShapeDtypeStruct((3, 3, slab, outs), BF16)] * groups,
            in_specs=[HBM],
            out_specs=[VMEM] * groups,
            scratch_shapes=[pltpu.SemaphoreType.DMA((groups, 3))],
            compiler_params=pltpu.CompilerParams(vmem_limit_bytes=48 << 20),
            name="split_weights",
        )(kernel)
    owner = lax.axis_index("filt")
    own = lax.dynamic_slice_in_dim(kernel, owner * outs, outs, 3)
    order = [lax.rem(owner - shift + groups, groups) for shift in range(groups)]
    return [lax.dynamic_slice_in_dim(own, group * slab, slab, 2) for group in order]


def body(features, kernel, bias):
    groups = lax.axis_size("filt")
    slab, height, width = features.shape
    outs = kernel.shape[3] // groups
    half = height // 2
    chunks = ((1, half), (half, height - 3), (height - 3, height - 1))

    rim, upper_rows, lower_rows = relayout(features, ((1, half), (half, height - 1)))
    rings = [[(i, (i + shift) % groups) for i in range(groups)] for shift in range(1, groups)]
    rims = [rim] + [lax.ppermute(rim, "filt", ring) for ring in rings]
    sets = [[lax.ppermute(upper_rows, "filt", ring)] for ring in rings]
    pairs = [r[0 : 2 * width].reshape(2, width, slab) for r in rims]
    outer = [(0, 0, 0, 1), (0, 1, height - 1, 1)]
    shape = (height, width, outs)

    weights = split_weights(kernel, groups, slab, outs)
    bias = bias[None, :]
    if outs % 128 != 0:
        bias = lax.dynamic_slice_in_dim(bias, lax.axis_index("filt") * outs, outs, 1)
    spans = [*outer, (1, 0, 1, half - 1), (2, 0, half, half - 1)]
    second = pick(lower_rows, 0, chunks[1][1] - half, weights[0])
    for received, ring in zip(sets, rings):
        received.append(lax.ppermute(second, "filt", ring))

    row_pairs, col_pairs = swap_pairs("row"), swap_pairs("col")
    sent = calls(functools.partial(outermost_kernel, groups), "outermost", [(groups, width, slab)] * 2, rims, estimate=WAIT)
    outer_rows = [lax.ppermute(v, "row", p) for v, p in zip(sent, row_pairs)]
    total = accumulate(spans, [pairs[0], upper_rows, lower_rows], weights[0], None, shape, rims[-1], bias)
    for g in range(1, groups):
        total = accumulate(outer, [pairs[g]], weights[g], total, shape)
    edge = pltpu.VMEM((2, height + 2, slab), F32)
    sent = calls(functools.partial(edges_kernel, groups), "edges", [(groups, height + 2, slab)] * 2, [*rims, *outer_rows], [edge])
    third = pick(lower_rows, chunks[2][0] - half, chunks[2][1] - half, sent[0])
    for received, ring in zip(sets, rings):
        received.append(lax.ppermute(third, "filt", ring))
    outer_cols = [lax.ppermute(v, "col", p) for v, p in zip(sent, col_pairs)]
    rows_fix = call(
        functools.partial(outer_rows_kernel, groups), "outer_rows", (2, width, outs), F32,
        [*outer_rows, *weights, *sent], cost(6 * width * groups, slab, outs), [pltpu.VMEM((3, 1, width, slab), BF16)],
    )
    for g in range(1, groups):
        a, b, c = sets[g - 1]
        total = accumulate([(0, 0, chunks[0][0], half - 1)], [a], weights[g], total, shape, rows_fix)
        total = accumulate([(0, 0, chunks[1][0], b.shape[0])], [b], weights[g], total, shape)
        if g < groups - 1:
            total = accumulate([(0, 0, chunks[2][0], c.shape[0])], [c], weights[g], total, shape)
    cols_fix = call(
        functools.partial(outer_cols_kernel, groups), "outer_cols", (2, height, outs), F32,
        [*outer_cols, *weights, total], cost(6 * 256 * groups, slab, outs),
    )
    top = call(upper_kernel, "upper", (outs, half, width), BF16, [total, rows_fix, cols_fix], cost(256, slab, outs))
    scratch = [
        pltpu.VMEM(shape, F32),
        pltpu.VMEM((3, c.shape[0], width, slab), BF16),
        pltpu.VMEM((outs, height - half, width), BF16),
        pltpu.SemaphoreType.DMA((2,)),
    ]
    span = (0, chunks[2][0], c.shape[0])
    return call(
        functools.partial(last_kernel, span), "last", (outs, height, width), BF16,
        [c, weights[-1], total, rows_fix, cols_fix, top], cost(9 * 256, slab, outs), scratch, HBM,
    )


def solution(mesh):
    return jax.shard_map(
        body,
        mesh=mesh,
        in_specs=(P("filt", "row", "col"), P(), P()),
        out_specs=P("filt", "row", "col"),
        check_vma=False,
    )
```

```python
import functools

import jax
import jax.numpy as jnp
from jax import lax
from jax.experimental import pallas as pl
from jax.experimental.pallas import tpu as pltpu
from jax.sharding import PartitionSpec as P

BF16, F32 = jnp.bfloat16, jnp.float32
VMEM = pl.BlockSpec(memory_space=pltpu.VMEM)
HBM = pl.BlockSpec(memory_space=pltpu.HBM)
PARAMS = pltpu.CompilerParams(vmem_limit_bytes=10 << 20)
WAIT = pl.CostEstimate(flops=4 * 10**9, bytes_accessed=1 << 20, transcendentals=0)
BLOCK = 4


def relayout_kernel(chunks, x_ref, rim_ref, *refs):
    outs, col_ref = refs[:-1], refs[-1]
    slab, rows, width = x_ref.shape
    for base in range(0, rows, 8):
        group = jnp.swapaxes(x_ref[:, base : base + 8, :].astype(F32), 0, 1)
        for h in range(base, base + 8):
            pixels = group[h - base].T
            col_ref[h : h + 1, :] = pixels[0:1, :]
            col_ref[rows + h : rows + h + 1, :] = pixels[width - 1 : width, :]
            pixels = pixels.astype(BF16)
            if h == 0:
                rim_ref[0:width, :] = pixels
            elif h == rows - 1:
                rim_ref[width : 2 * width, :] = pixels
            else:
                for out, (first, last) in zip(outs, chunks):
                    if first <= h < last:
                        out[h - first] = pixels
    rim_ref[2 * width :, :] = col_ref[...].astype(BF16)


def relayout(features, chunks):
    slab, rows, width = features.shape
    shapes = [(2 * width + 2 * rows, slab)] + [(last - first, width, slab) for first, last in chunks]
    return pl.pallas_call(
        functools.partial(relayout_kernel, chunks),
        out_shape=[jax.ShapeDtypeStruct(s, BF16) for s in shapes],
        in_specs=[VMEM],
        out_specs=[VMEM] * len(shapes),
        scratch_shapes=[pltpu.VMEM((2 * rows, slab), F32)],
        compiler_params=PARAMS,
        name="relayout",
    )(features)


def put_row(x_ref, at, value):
    width, slab = value.shape
    edge = lax.broadcasted_iota(jnp.int32, (16, slab), 0)
    x_ref[1, at] = value
    x_ref[0, at, 0 : width - 16, :] = value[0 : width - 16]
    x_ref[0, at, width - 16 :, :] = jnp.where(edge == 15, 0, value[width - 16 :].astype(F32)).astype(BF16)
    x_ref[2, at, 16:, :] = value[16:]
    x_ref[2, at, 0:16, :] = jnp.where(edge == 0, 0, value[0:16].astype(F32)).astype(BF16)


def turn(part, b):
    return part if b == 1 else pltpu.roll(part, 1 if b == 0 else part.shape[0] - 1, 0)


def add_rows(spans, w_ref, total_ref, x_ref, written, initial=None):
    height, width, _ = total_ref.shape
    slab = w_ref.shape[2]
    at = 0
    for piece, local, row, count in spans:
        for start in range(0, count, BLOCK):
            size = min(BLOCK, count - start)
            for i in range(size):
                put_row(x_ref, at + i, piece[local + start + i])
            for a in range(3):
                low = max(0, row + start + 1 - a)
                high = min(height, row + start + size + 1 - a)
                if high <= low:
                    continue
                skip = low - (row + start + 1 - a)
                n = high - low
                for b in range(3):
                    lhs = x_ref[b, at + skip : at + skip + n].reshape(n * width, slab)
                    part = jnp.dot(lhs, w_ref[a, b], preferred_element_type=F32).reshape(n, width, -1)
                    for i in range(n):
                        term = turn(part[i], b)
                        if low + i in written:
                            total_ref[low + i] += term
                        else:
                            total_ref[low + i] = term + initial
                            written.add(low + i)
            at += size


def accumulate_kernel(spans, n, started, *refs):
    pieces, w_ref, total_ref, x_ref = refs[:n], refs[n], refs[-2], refs[-1]
    written = set(range(total_ref.shape[0])) if started else set()
    spans = [(pieces[p], local, row, count) for p, local, row, count in spans]
    add_rows(spans, w_ref, total_ref, x_ref, written, None if started else own_bias(refs[n + 1], total_ref.shape[2]))


def own_bias(bias_ref, outs):
    if bias_ref.shape[1] == outs:
        return bias_ref[...]
    return bias_ref[:, pl.ds(pl.multiple_of(lax.axis_index("filt") * outs, outs), outs)]


def accumulate(spans, pieces, weights, total, shape, after=None, bias=None):
    count = sum(s[3] for s in spans)
    width, slab = shape[1], weights.shape[2]
    operands = [*pieces, weights]
    aliases = {}
    if total is not None:
        aliases = {len(operands): 0}
        operands.append(total)
    else:
        operands.append(bias)
    if after is not None:
        operands.append(after)
    return pl.pallas_call(
        functools.partial(accumulate_kernel, spans, len(pieces), total is not None),
        out_shape=jax.ShapeDtypeStruct(shape, F32),
        in_specs=[VMEM] * len(operands),
        out_specs=VMEM,
        scratch_shapes=[pltpu.VMEM((3, count, width, slab), BF16)],
        input_output_aliases=aliases,
        compiler_params=PARAMS,
        cost_estimate=cost(count * width * 9, slab, shape[2]),
        name="accumulate",
    )(*operands)


def pick_kernel(low, high, rows_ref, after_ref, out_ref):
    out_ref[...] = rows_ref[low:high]


def pick(rows, low, high, after):
    shape = (high - low, *rows.shape[1:])
    return call(functools.partial(pick_kernel, low, high), "pick", shape, BF16, [rows, after], cost(1, 1, 1))


def cost(pixels, slab, outs):
    return pl.CostEstimate(flops=2 * pixels * slab * outs, bytes_accessed=1 << 20, transcendentals=0)


def parity(axis):
    return lax.rem(lax.axis_index(axis), 2)


def swap_pairs(axis):
    count = lax.axis_size(axis)
    return [[p for i in range(start, count - 1, 2) for p in ((i, i + 1), (i + 1, i))] for start in (1, 0)]


def outermost_kernel(groups, *refs):
    rims, outs = refs[:groups], refs[-2:]
    width = outs[0].shape[1]
    odd = parity("row")
    for swap, out_ref in enumerate(outs):
        start = pl.multiple_of((odd if swap == 0 else 1 - odd) * width, width)
        for g in range(groups):
            out_ref[g] = rims[g][pl.ds(start, width), :]


def edges_kernel(groups, *refs):
    rims, swapped, outs, col_ref = refs[:groups], refs[groups : groups + 2], refs[-3:-1], refs[-1]
    width = swapped[0].shape[1]
    height = outs[0].shape[1] - 2
    odd_row, odd_col = parity("row") == 1, parity("col") == 1
    for g in range(groups):
        for side, at in enumerate((0, width - 16)):
            pixels = [ref[g, at : at + 16, :].astype(F32)[side * 15 : side * 15 + 1, :] for ref in swapped]
            start = 2 * width + side * height
            col_ref[side, 0:1, :] = jnp.where(odd_row, pixels[1], pixels[0])
            col_ref[side, 1 : height + 1, :] = rims[g][start : start + height, :].astype(F32)
            col_ref[side, height + 1 :, :] = jnp.where(odd_row, pixels[0], pixels[1])
        outs[0][g] = jnp.where(odd_col, col_ref[1], col_ref[0]).astype(BF16)
        outs[1][g] = jnp.where(odd_col, col_ref[0], col_ref[1]).astype(BF16)


def outer_rows_kernel(groups, *refs):
    swapped, w_refs, fix_ref, x_ref = refs[:2], refs[2 : 2 + groups], refs[-2], refs[-1]
    odd = parity("row") == 1
    for i, a in enumerate((0, 2)):
        fix = None
        for g in range(groups):
            put_row(x_ref, 0, jnp.where(odd, swapped[1 - i][g], swapped[i][g]))
            for b in range(3):
                part = turn(jnp.dot(x_ref[b, 0], w_refs[g][a, b], preferred_element_type=F32), b)
                fix = part if fix is None else fix + part
        fix_ref[i] = fix


def outer_cols_kernel(groups, *refs):
    swapped, w_refs, fix_ref = refs[:2], refs[2 : 2 + groups], refs[-1]
    height = fix_ref.shape[1]
    odd = parity("col") == 1
    for i, b in enumerate((0, 2)):
        fix = None
        for g in range(groups):
            pixels = jnp.where(odd, swapped[1 - i][g], swapped[i][g])
            for a in range(3):
                part = jnp.dot(pixels, w_refs[g][a, b], preferred_element_type=F32)[a : a + height]
                fix = part if fix is None else fix + part
        fix_ref[i] = fix


def finish_row(total_ref, h, rows_ref, cols_ref):
    height, width = cols_ref.shape[1], total_ref.shape[1]
    value = total_ref[h]
    if h == 0:
        value += rows_ref[0]
    if h == height - 1:
        value += rows_ref[1]
    edge = lax.broadcasted_iota(jnp.int32, (8, value.shape[1]), 0)
    first = value[0:8] + jnp.where(edge == 0, cols_ref[0, h : h + 1, :], 0)
    final = value[width - 8 :] + jnp.where(edge == 7, cols_ref[1, h : h + 1, :], 0)
    return jnp.concatenate([first, value[8 : width - 8], final], 0)


def store_rows(total_ref, rows_ref, cols_ref, rows, out_ref):
    turned = jnp.stack([finish_row(total_ref, h, rows_ref, cols_ref).T for h in rows], 0)
    out_ref[...] = jnp.swapaxes(turned, 0, 1).astype(BF16)


def upper_kernel(total_ref, rows_ref, cols_ref, out_ref):
    store_rows(total_ref, rows_ref, cols_ref, range(out_ref.shape[1]), out_ref)


def last_kernel(span, piece, w_ref, total_in, rows_ref, cols_ref, upper_ref, out_ref, total_ref, x_ref, lower_ref, sems):
    half = upper_ref.shape[1]
    height = out_ref.shape[1]
    first = pltpu.make_async_copy(upper_ref, out_ref.at[:, 0:half, :], sems.at[0])
    first.start()
    total_ref[half:] = total_in[half:]
    add_rows([(piece, *span)], w_ref, total_ref, x_ref, set(range(height)))
    store_rows(total_ref, rows_ref, cols_ref, range(half, height), lower_ref)
    second = pltpu.make_async_copy(lower_ref, out_ref.at[:, half:height, :], sems.at[1])
    second.start()
    first.wait()
    second.wait()


def call(kernel, name, shape, dtype, operands, estimate, scratch=(), out=VMEM):
    return pl.pallas_call(
        kernel,
        out_shape=jax.ShapeDtypeStruct(shape, dtype),
        in_specs=[VMEM] * len(operands),
        out_specs=out,
        scratch_shapes=scratch,
        compiler_params=PARAMS,
        cost_estimate=estimate,
        name=name,
    )(*operands)


def calls(kernel, name, shapes, operands, scratch=(), estimate=None):
    return pl.pallas_call(
        kernel,
        out_shape=[jax.ShapeDtypeStruct(shape, BF16) for shape in shapes],
        in_specs=[VMEM] * len(operands),
        out_specs=[VMEM] * len(shapes),
        scratch_shapes=scratch,
        compiler_params=PARAMS,
        cost_estimate=estimate or cost(1, 1, 1),
        name=name,
    )(*operands)


def greeting_kernel(out_ref):
    out_ref[...] = jnp.zeros_like(out_ref)


def weights_kernel(groups, kernel_ref, *refs):
    outs, sems = refs[:-1], refs[-1]
    slab, width = outs[0].shape[2:]
    owner = lax.axis_index("filt")
    own = pl.ds(pl.multiple_of(owner * width, width), width)
    copies = []
    for shift, out in enumerate(outs):
        group = pl.ds(pl.multiple_of(lax.rem(owner - shift + groups, groups) * slab, slab), slab)
        for a in range(3):
            copies.append(pltpu.make_async_copy(kernel_ref.at[a, :, group, own], out.at[a], sems.at[shift, a]))
    for copy in copies:
        copy.start()
    for copy in copies:
        copy.wait()


def split_weights(kernel, groups, slab, outs):
    if outs % 128 == 0 and slab % 128 == 0:
        return pl.pallas_call(
            functools.partial(weights_kernel, groups),
            out_shape=[jax.ShapeDtypeStruct((3, 3, slab, outs), BF16)] * groups,
            in_specs=[HBM],
            out_specs=[VMEM] * groups,
            scratch_shapes=[pltpu.SemaphoreType.DMA((groups, 3))],
            compiler_params=pltpu.CompilerParams(vmem_limit_bytes=48 << 20),
            name="split_weights",
        )(kernel)
    owner = lax.axis_index("filt")
    own = lax.dynamic_slice_in_dim(kernel, owner * outs, outs, 3)
    order = [lax.rem(owner - shift + groups, groups) for shift in range(groups)]
    return [lax.dynamic_slice_in_dim(own, group * slab, slab, 2) for group in order]


def body(features, kernel, bias):
    groups = lax.axis_size("filt")
    slab, height, width = features.shape
    outs = kernel.shape[3] // groups
    half = height // 2
    chunks = ((1, half), (half, height - 3), (height - 3, height - 1))

    rings = [[(i, (i + shift) % groups) for i in range(groups)] for shift in range(1, groups)]
    greeting = call(greeting_kernel, "greeting", (8, 128), F32, [], WAIT)
    greeting = lax.ppermute(greeting, "filt", rings[0])
    rim, upper_rows, lower_rows = relayout(features, ((1, half), (half, height - 1)))
    rim = pick(rim, 0, rim.shape[0], greeting)
    rims = [rim] + [lax.ppermute(rim, "filt", ring) for ring in rings]
    sets = [[lax.ppermute(upper_rows, "filt", ring)] for ring in rings]
    pairs = [r[0 : 2 * width].reshape(2, width, slab) for r in rims]
    outer = [(0, 0, 0, 1), (0, 1, height - 1, 1)]
    shape = (height, width, outs)

    weights = split_weights(kernel, groups, slab, outs)
    bias = bias[None, :]
    if outs % 128 != 0:
        bias = lax.dynamic_slice_in_dim(bias, lax.axis_index("filt") * outs, outs, 1)
    spans = [*outer, (1, 0, 1, half - 1), (2, 0, half, half - 1)]
    second = pick(lower_rows, 0, chunks[1][1] - half, weights[0])
    for received, ring in zip(sets, rings):
        received.append(lax.ppermute(second, "filt", ring))

    row_pairs, col_pairs = swap_pairs("row"), swap_pairs("col")
    sent = calls(functools.partial(outermost_kernel, groups), "outermost", [(groups, width, slab)] * 2, rims, estimate=WAIT)
    outer_rows = [lax.ppermute(v, "row", p) for v, p in zip(sent, row_pairs)]
    total = accumulate(spans, [pairs[0], upper_rows, lower_rows], weights[0], None, shape, rims[-1], bias)
    for g in range(1, groups):
        total = accumulate(outer, [pairs[g]], weights[g], total, shape)
    edge = pltpu.VMEM((2, height + 2, slab), F32)
    sent = calls(functools.partial(edges_kernel, groups), "edges", [(groups, height + 2, slab)] * 2, [*rims, *outer_rows], [edge])
    third = pick(lower_rows, chunks[2][0] - half, chunks[2][1] - half, sent[0])
    for received, ring in zip(sets, rings):
        received.append(lax.ppermute(third, "filt", ring))
    outer_cols = [lax.ppermute(v, "col", p) for v, p in zip(sent, col_pairs)]
    rows_fix = call(
        functools.partial(outer_rows_kernel, groups), "outer_rows", (2, width, outs), F32,
        [*outer_rows, *weights, *sent], cost(6 * width * groups, slab, outs), [pltpu.VMEM((3, 1, width, slab), BF16)],
    )
    for g in range(1, groups):
        a, b, c = sets[g - 1]
        total = accumulate([(0, 0, chunks[0][0], half - 1)], [a], weights[g], total, shape, rows_fix)
        total = accumulate([(0, 0, chunks[1][0], b.shape[0])], [b], weights[g], total, shape)
        if g < groups - 1:
            total = accumulate([(0, 0, chunks[2][0], c.shape[0])], [c], weights[g], total, shape)
    cols_fix = call(
        functools.partial(outer_cols_kernel, groups), "outer_cols", (2, height, outs), F32,
        [*outer_cols, *weights, total], cost(6 * 256 * groups, slab, outs),
    )
    top = call(upper_kernel, "upper", (outs, half, width), BF16, [total, rows_fix, cols_fix], cost(256, slab, outs))
    scratch = [
        pltpu.VMEM(shape, F32),
        pltpu.VMEM((3, c.shape[0], width, slab), BF16),
        pltpu.VMEM((outs, height - half, width), BF16),
        pltpu.SemaphoreType.DMA((2,)),
    ]
    span = (0, chunks[2][0], c.shape[0])
    return call(
        functools.partial(last_kernel, span), "last", (outs, height, width), BF16,
        [c, weights[-1], total, rows_fix, cols_fix, top], cost(9 * 256, slab, outs), scratch, HBM,
    )


def solution(mesh):
    return jax.shard_map(
        body,
        mesh=mesh,
        in_specs=(P("filt", "row", "col"), P(), P()),
        out_specs=P("filt", "row", "col"),
        check_vma=False,
    )
```

```python
import functools

import jax
import jax.numpy as jnp
from jax import lax
from jax.experimental import pallas as pl
from jax.experimental.pallas import tpu as pltpu
from jax.sharding import PartitionSpec as P

BF16, F32 = jnp.bfloat16, jnp.float32
VMEM = pl.BlockSpec(memory_space=pltpu.VMEM)
HBM = pl.BlockSpec(memory_space=pltpu.HBM)
PARAMS = pltpu.CompilerParams(vmem_limit_bytes=10 << 20)
WAIT = pl.CostEstimate(flops=4 * 10**9, bytes_accessed=1 << 20, transcendentals=0)
BLOCK = 4


def relayout_kernel(chunks, x_hbm, rim_ref, *refs):
    outs, (x_ref, col_ref, sems) = refs[:-3], refs[-3:]
    slab, rows, width = x_ref.shape
    parts = 2 if slab % 256 == 0 else 1
    step = slab // parts
    copies = [pltpu.make_async_copy(x_hbm.at[q * step : (q + 1) * step], x_ref.at[q * step : (q + 1) * step], sems.at[q]) for q in range(parts)]
    for copy in copies:
        copy.start()
    for q, copy in enumerate(copies):
        copy.wait()
        lanes = slice(q * step, (q + 1) * step)
        for base in range(0, rows, 8):
            group = jnp.swapaxes(x_ref[lanes, base : base + 8, :].astype(F32), 0, 1)
            for h in range(base, base + 8):
                pixels = group[h - base].T
                col_ref[h : h + 1, lanes] = pixels[0:1, :]
                col_ref[rows + h : rows + h + 1, lanes] = pixels[width - 1 : width, :]
                pixels = pixels.astype(BF16)
                if h == 0:
                    rim_ref[0:width, lanes] = pixels
                elif h == rows - 1:
                    rim_ref[width : 2 * width, lanes] = pixels
                else:
                    for out, (first, last) in zip(outs, chunks):
                        if first <= h < last:
                            out[h - first, :, lanes] = pixels
    rim_ref[2 * width :, :] = col_ref[...].astype(BF16)


def relayout(features, chunks):
    slab, rows, width = features.shape
    shapes = [(2 * width + 2 * rows, slab)] + [(last - first, width, slab) for first, last in chunks]
    return pl.pallas_call(
        functools.partial(relayout_kernel, chunks),
        out_shape=[jax.ShapeDtypeStruct(s, BF16) for s in shapes],
        in_specs=[HBM],
        out_specs=[VMEM] * len(shapes),
        scratch_shapes=[pltpu.VMEM(features.shape, BF16), pltpu.VMEM((2 * rows, slab), F32), pltpu.SemaphoreType.DMA((2,))],
        compiler_params=PARAMS,
        name="relayout",
    )(pltpu.with_memory_space_constraint(features, pltpu.HBM))


def put_row(x_ref, at, value):
    width, slab = value.shape
    edge = lax.broadcasted_iota(jnp.int32, (16, slab), 0)
    x_ref[1, at] = value
    x_ref[0, at, 0 : width - 16, :] = value[0 : width - 16]
    x_ref[0, at, width - 16 :, :] = jnp.where(edge == 15, 0, value[width - 16 :].astype(F32)).astype(BF16)
    x_ref[2, at, 16:, :] = value[16:]
    x_ref[2, at, 0:16, :] = jnp.where(edge == 0, 0, value[0:16].astype(F32)).astype(BF16)


def turn(part, b):
    return part if b == 1 else pltpu.roll(part, 1 if b == 0 else part.shape[0] - 1, 0)


def add_rows(spans, w_ref, total_ref, x_ref, written, initial=None):
    height, width, _ = total_ref.shape
    slab = w_ref.shape[2]
    at = 0
    for piece, local, row, count in spans:
        for start in range(0, count, BLOCK):
            size = min(BLOCK, count - start)
            for i in range(size):
                put_row(x_ref, at + i, piece[local + start + i])
            for a in range(3):
                low = max(0, row + start + 1 - a)
                high = min(height, row + start + size + 1 - a)
                if high <= low:
                    continue
                skip = low - (row + start + 1 - a)
                n = high - low
                for b in range(3):
                    lhs = x_ref[b, at + skip : at + skip + n].reshape(n * width, slab)
                    part = jnp.dot(lhs, w_ref[a, b], preferred_element_type=F32).reshape(n, width, -1)
                    for i in range(n):
                        term = turn(part[i], b)
                        if low + i in written:
                            total_ref[low + i] += term
                        else:
                            total_ref[low + i] = term + initial
                            written.add(low + i)
            at += size


def accumulate_kernel(spans, n, started, *refs):
    pieces, w_ref, total_ref, x_ref = refs[:n], refs[n], refs[-2], refs[-1]
    written = set(range(total_ref.shape[0])) if started else set()
    spans = [(pieces[p], local, row, count) for p, local, row, count in spans]
    add_rows(spans, w_ref, total_ref, x_ref, written, None if started else own_bias(refs[n + 1], total_ref.shape[2]))


def own_bias(bias_ref, outs):
    if bias_ref.shape[1] == outs:
        return bias_ref[...]
    return bias_ref[:, pl.ds(pl.multiple_of(lax.axis_index("filt") * outs, outs), outs)]


def accumulate(spans, pieces, weights, total, shape, after=None, bias=None):
    count = sum(s[3] for s in spans)
    width, slab = shape[1], weights.shape[2]
    operands = [*pieces, weights]
    aliases = {}
    if total is not None:
        aliases = {len(operands): 0}
        operands.append(total)
    else:
        operands.append(bias)
    if after is not None:
        operands.append(after)
    return pl.pallas_call(
        functools.partial(accumulate_kernel, spans, len(pieces), total is not None),
        out_shape=jax.ShapeDtypeStruct(shape, F32),
        in_specs=[VMEM] * len(operands),
        out_specs=VMEM,
        scratch_shapes=[pltpu.VMEM((3, count, width, slab), BF16)],
        input_output_aliases=aliases,
        compiler_params=PARAMS,
        cost_estimate=cost(count * width * 9, slab, shape[2]),
        name="accumulate",
    )(*operands)


def pick_kernel(low, high, rows_ref, after_ref, out_ref):
    out_ref[...] = rows_ref[low:high]


def pick(rows, low, high, after):
    shape = (high - low, *rows.shape[1:])
    return call(functools.partial(pick_kernel, low, high), "pick", shape, BF16, [rows, after], cost(1, 1, 1))


def cost(pixels, slab, outs):
    return pl.CostEstimate(flops=2 * pixels * slab * outs, bytes_accessed=1 << 20, transcendentals=0)


def parity(axis):
    return lax.rem(lax.axis_index(axis), 2)


def swap_pairs(axis):
    count = lax.axis_size(axis)
    return [[p for i in range(start, count - 1, 2) for p in ((i, i + 1), (i + 1, i))] for start in (1, 0)]


def outermost_kernel(groups, *refs):
    rims, outs = refs[:groups], refs[-2:]
    width = outs[0].shape[1]
    odd = parity("row")
    for swap, out_ref in enumerate(outs):
        start = pl.multiple_of((odd if swap == 0 else 1 - odd) * width, width)
        for g in range(groups):
            out_ref[g] = rims[g][pl.ds(start, width), :]


def edges_kernel(groups, *refs):
    rims, swapped, outs, col_ref = refs[:groups], refs[groups : groups + 2], refs[-3:-1], refs[-1]
    width = swapped[0].shape[1]
    height = outs[0].shape[1] - 2
    odd_row, odd_col = parity("row") == 1, parity("col") == 1
    for g in range(groups):
        for side, at in enumerate((0, width - 16)):
            pixels = [ref[g, at : at + 16, :].astype(F32)[side * 15 : side * 15 + 1, :] for ref in swapped]
            start = 2 * width + side * height
            col_ref[side, 0:1, :] = jnp.where(odd_row, pixels[1], pixels[0])
            col_ref[side, 1 : height + 1, :] = rims[g][start : start + height, :].astype(F32)
            col_ref[side, height + 1 :, :] = jnp.where(odd_row, pixels[0], pixels[1])
        outs[0][g] = jnp.where(odd_col, col_ref[1], col_ref[0]).astype(BF16)
        outs[1][g] = jnp.where(odd_col, col_ref[0], col_ref[1]).astype(BF16)


def outer_rows_kernel(groups, *refs):
    swapped, w_refs, fix_ref, x_ref = refs[:2], refs[2 : 2 + groups], refs[-2], refs[-1]
    odd = parity("row") == 1
    for i, a in enumerate((0, 2)):
        fix = None
        for g in range(groups):
            put_row(x_ref, 0, jnp.where(odd, swapped[1 - i][g], swapped[i][g]))
            for b in range(3):
                part = turn(jnp.dot(x_ref[b, 0], w_refs[g][a, b], preferred_element_type=F32), b)
                fix = part if fix is None else fix + part
        fix_ref[i] = fix


def outer_cols_kernel(groups, *refs):
    swapped, w_refs, fix_ref = refs[:2], refs[2 : 2 + groups], refs[-1]
    height = fix_ref.shape[1]
    odd = parity("col") == 1
    for i, b in enumerate((0, 2)):
        fix = None
        for g in range(groups):
            pixels = jnp.where(odd, swapped[1 - i][g], swapped[i][g])
            for a in range(3):
                part = jnp.dot(pixels, w_refs[g][a, b], preferred_element_type=F32)[a : a + height]
                fix = part if fix is None else fix + part
        fix_ref[i] = fix


def finish_row(value, h, rows_ref, cols_ref):
    height, width = cols_ref.shape[1], value.shape[0]
    if h == 0:
        value += rows_ref[0]
    if h == height - 1:
        value += rows_ref[1]
    edge = lax.broadcasted_iota(jnp.int32, (8, value.shape[1]), 0)
    first = value[0:8] + jnp.where(edge == 0, cols_ref[0, h : h + 1, :], 0)
    final = value[width - 8 :] + jnp.where(edge == 7, cols_ref[1, h : h + 1, :], 0)
    return jnp.concatenate([first, value[8 : width - 8], final], 0).T


def upper_kernel(total_ref, rows_ref, cols_ref, out_ref):
    turned = [finish_row(total_ref[h], h, rows_ref, cols_ref) for h in range(out_ref.shape[1])]
    out_ref[...] = jnp.swapaxes(jnp.stack(turned, 0), 0, 1).astype(BF16)


def middle_kernel(start, total_ref, rows_ref, cols_ref, out_ref):
    for i in range(out_ref.shape[0]):
        out_ref[i] = finish_row(total_ref[start + i], start + i, rows_ref, cols_ref)


def last_kernel(piece, w_ref, total_ref, rows_ref, cols_ref, upper_ref, middle_ref, out_ref, x_ref, lower_ref, sems):
    outs, height, width = out_ref.shape
    half, done = upper_ref.shape[1], middle_ref.shape[0]
    first = pltpu.make_async_copy(upper_ref, out_ref.at[:, 0:half, :], sems.at[0])
    first.start()
    count = piece.shape[0]
    for i in range(count):
        put_row(x_ref, i, piece[i])
    values = [total_ref[h] for h in range(half + done, height)]
    for a in range(3):
        for b in range(3):
            part = jnp.dot(x_ref[b].reshape(count * width, -1), w_ref[a, b], preferred_element_type=F32).reshape(count, width, outs)
            for i in range(count):
                values[i + 2 - a] += turn(part[i], b)
    turned = [middle_ref[i] for i in range(done)]
    turned += [finish_row(value, half + done + i, rows_ref, cols_ref) for i, value in enumerate(values)]
    lower_ref[...] = jnp.swapaxes(jnp.stack(turned, 0), 0, 1).astype(BF16)
    second = pltpu.make_async_copy(lower_ref, out_ref.at[:, half:height, :], sems.at[1])
    second.start()
    first.wait()
    second.wait()


def call(kernel, name, shape, dtype, operands, estimate, scratch=(), out=VMEM):
    return pl.pallas_call(
        kernel,
        out_shape=jax.ShapeDtypeStruct(shape, dtype),
        in_specs=[VMEM] * len(operands),
        out_specs=out,
        scratch_shapes=scratch,
        compiler_params=PARAMS,
        cost_estimate=estimate,
        name=name,
    )(*operands)


def calls(kernel, name, shapes, operands, scratch=(), estimate=None):
    return pl.pallas_call(
        kernel,
        out_shape=[jax.ShapeDtypeStruct(shape, BF16) for shape in shapes],
        in_specs=[VMEM] * len(operands),
        out_specs=[VMEM] * len(shapes),
        scratch_shapes=scratch,
        compiler_params=PARAMS,
        cost_estimate=estimate or cost(1, 1, 1),
        name=name,
    )(*operands)


def weights_kernel(groups, kernel_ref, *refs):
    outs, sems = refs[:-1], refs[-1]
    slab, width = outs[0].shape[2:]
    owner = lax.axis_index("filt")
    own = pl.ds(pl.multiple_of(owner * width, width), width)
    copies = []
    for shift, out in enumerate(outs):
        group = pl.ds(pl.multiple_of(lax.rem(owner - shift + groups, groups) * slab, slab), slab)
        for a in range(3):
            copies.append(pltpu.make_async_copy(kernel_ref.at[a, :, group, own], out.at[a], sems.at[shift, a]))
    for copy in copies:
        copy.start()
    for copy in copies:
        copy.wait()


def split_weights(kernel, groups, slab, outs):
    if outs % 128 == 0 and slab % 128 == 0:
        return pl.pallas_call(
            functools.partial(weights_kernel, groups),
            out_shape=[jax.ShapeDtypeStruct((3, 3, slab, outs), BF16)] * groups,
            in_specs=[HBM],
            out_specs=[VMEM] * groups,
            scratch_shapes=[pltpu.SemaphoreType.DMA((groups, 3))],
            compiler_params=pltpu.CompilerParams(vmem_limit_bytes=48 << 20),
            name="split_weights",
        )(kernel)
    owner = lax.axis_index("filt")
    own = lax.dynamic_slice_in_dim(kernel, owner * outs, outs, 3)
    order = [lax.rem(owner - shift + groups, groups) for shift in range(groups)]
    return [lax.dynamic_slice_in_dim(own, group * slab, slab, 2) for group in order]


def body(features, kernel, bias):
    groups = lax.axis_size("filt")
    slab, height, width = features.shape
    outs = kernel.shape[3] // groups
    half = height // 2
    chunks = ((1, half + 1), (half + 1, height - 2), (height - 2, height - 1))

    rim, upper_rows, lower_rows = relayout(features, (chunks[0], (half + 1, height - 1)))
    rings = [[(i, (i + shift) % groups) for i in range(groups)] for shift in range(1, groups)]
    rims = [rim] + [lax.ppermute(rim, "filt", ring) for ring in rings]
    sets = [[lax.ppermute(upper_rows, "filt", ring)] for ring in rings]
    pairs = [r[0 : 2 * width].reshape(2, width, slab) for r in rims]
    outer = [(0, 0, 0, 1), (0, 1, height - 1, 1)]
    shape = (height, width, outs)

    weights = split_weights(kernel, groups, slab, outs)
    bias = bias[None, :]
    if outs % 128 != 0:
        bias = lax.dynamic_slice_in_dim(bias, lax.axis_index("filt") * outs, outs, 1)
    spans = [*outer, (1, 0, 1, half), (2, 0, half + 1, height - half - 2)]
    second = pick(lower_rows, 0, chunks[1][1] - half - 1, weights[0])
    for received, ring in zip(sets, rings):
        received.append(lax.ppermute(second, "filt", ring))

    row_pairs, col_pairs = swap_pairs("row"), swap_pairs("col")
    sent = calls(functools.partial(outermost_kernel, groups), "outermost", [(groups, width, slab)] * 2, rims, estimate=WAIT)
    outer_rows = [lax.ppermute(v, "row", p) for v, p in zip(sent, row_pairs)]
    total = accumulate(spans, [pairs[0], upper_rows, lower_rows], weights[0], None, shape, rims[-1], bias)
    for g in range(1, groups):
        total = accumulate(outer, [pairs[g]], weights[g], total, shape)
    edge = pltpu.VMEM((2, height + 2, slab), F32)
    sent = calls(functools.partial(edges_kernel, groups), "edges", [(groups, height + 2, slab)] * 2, [*rims, *outer_rows], [edge])
    third = pick(lower_rows, chunks[2][0] - half - 1, chunks[2][1] - half - 1, sent[0])
    for received, ring in zip(sets, rings):
        received.append(lax.ppermute(third, "filt", ring))
    outer_cols = [lax.ppermute(v, "col", p) for v, p in zip(sent, col_pairs)]
    rows_fix = call(
        functools.partial(outer_rows_kernel, groups), "outer_rows", (2, width, outs), F32,
        [*outer_rows, *weights, *sent], cost(6 * width * groups, slab, outs), [pltpu.VMEM((3, 1, width, slab), BF16)],
    )
    for g in range(1, groups):
        a, b, c = sets[g - 1]
        total = accumulate([(0, 0, chunks[0][0], a.shape[0])], [a], weights[g], total, shape, rows_fix)
        if g < groups - 1:
            total = accumulate([(0, 0, chunks[1][0], b.shape[0])], [b], weights[g], total, shape)
            total = accumulate([(0, 0, chunks[2][0], c.shape[0])], [c], weights[g], total, shape)
    cols_fix = call(
        functools.partial(outer_cols_kernel, groups), "outer_cols", (2, height, outs), F32,
        [*outer_cols, *weights, total], cost(6 * 256 * groups, slab, outs),
    )
    top = call(upper_kernel, "upper", (outs, half, width), BF16, [total, rows_fix, cols_fix], cost(256, slab, outs))
    total = accumulate([(0, 0, chunks[1][0], b.shape[0])], [b], weights[-1], total, shape, top)
    done = chunks[2][0] - 1 - half
    middle = call(functools.partial(middle_kernel, half), "middle", (done, outs, width), F32, [total, rows_fix, cols_fix], cost(1, 1, 1))
    scratch = [
        pltpu.VMEM((3, c.shape[0], width, slab), BF16),
        pltpu.VMEM((outs, height - half, width), BF16),
        pltpu.SemaphoreType.DMA((2,)),
    ]
    return call(
        last_kernel, "last", (outs, height, width), BF16,
        [c, weights[-1], total, rows_fix, cols_fix, top, middle], cost(9 * 256, slab, outs), scratch, HBM,
    )


def solution(mesh):
    return jax.shard_map(
        body,
        mesh=mesh,
        in_specs=(P("filt", "row", "col"), P(), P()),
        out_specs=P("filt", "row", "col"),
        check_vma=False,
    )
```

```python
import functools

import jax
import jax.numpy as jnp
from jax import lax
from jax.experimental import pallas as pl
from jax.experimental.pallas import tpu as pltpu
from jax.sharding import PartitionSpec as P

BF16, F32 = jnp.bfloat16, jnp.float32
VMEM = pl.BlockSpec(memory_space=pltpu.VMEM)
HBM = pl.BlockSpec(memory_space=pltpu.HBM)
PARAMS = pltpu.CompilerParams(vmem_limit_bytes=10 << 20)
WAIT = pl.CostEstimate(flops=4 * 10**9, bytes_accessed=1 << 20, transcendentals=0)
BLOCK = 4


def relayout_kernel(chunks, x_hbm, rim_ref, *refs):
    outs, (x_ref, col_ref, sems) = refs[:-3], refs[-3:]
    slab, rows, width = x_ref.shape
    parts = 2 if slab % 256 == 0 else 1
    step = slab // parts
    copies = [pltpu.make_async_copy(x_hbm.at[q * step : (q + 1) * step], x_ref.at[q * step : (q + 1) * step], sems.at[q]) for q in range(parts)]
    for copy in copies:
        copy.start()
    for q, copy in enumerate(copies):
        copy.wait()
        lanes = slice(q * step, (q + 1) * step)
        group = jnp.swapaxes(x_ref[lanes], 0, 1)
        for h in range(rows):
            pixels = group[h].T
            col_ref[h : h + 1, lanes] = pixels[0:16].astype(F32)[0:1, :]
            col_ref[rows + h : rows + h + 1, lanes] = pixels[width - 16 :].astype(F32)[15:16, :]
            if h == 0:
                rim_ref[0:width, lanes] = pixels
            elif h == rows - 1:
                rim_ref[width : 2 * width, lanes] = pixels
            else:
                for out, (first, last) in zip(outs, chunks):
                    if first <= h < last:
                        out[h - first, :, lanes] = pixels
    rim_ref[2 * width :, :] = col_ref[...].astype(BF16)


def relayout(features, chunks):
    slab, rows, width = features.shape
    shapes = [(2 * width + 2 * rows, slab)] + [(last - first, width, slab) for first, last in chunks]
    return pl.pallas_call(
        functools.partial(relayout_kernel, chunks),
        out_shape=[jax.ShapeDtypeStruct(s, BF16) for s in shapes],
        in_specs=[HBM],
        out_specs=[VMEM] * len(shapes),
        scratch_shapes=[pltpu.VMEM(features.shape, BF16), pltpu.VMEM((2 * rows, slab), F32), pltpu.SemaphoreType.DMA((2,))],
        compiler_params=PARAMS,
        name="relayout",
    )(pltpu.with_memory_space_constraint(features, pltpu.HBM))


def put_row(x_ref, at, value):
    width, slab = value.shape
    edge = lax.broadcasted_iota(jnp.int32, (16, slab), 0)
    x_ref[1, at] = value
    x_ref[0, at, 0 : width - 16, :] = value[0 : width - 16]
    x_ref[0, at, width - 16 :, :] = jnp.where(edge == 15, 0, value[width - 16 :].astype(F32)).astype(BF16)
    x_ref[2, at, 16:, :] = value[16:]
    x_ref[2, at, 0:16, :] = jnp.where(edge == 0, 0, value[0:16].astype(F32)).astype(BF16)


def turn(part, b):
    return part if b == 1 else pltpu.roll(part, 1 if b == 0 else part.shape[0] - 1, 0)


def add_rows(spans, w_ref, total_ref, x_ref, written, initial=None):
    height, width, _ = total_ref.shape
    slab = w_ref.shape[2]
    at = 0
    for piece, local, row, count in spans:
        for start in range(0, count, BLOCK):
            size = min(BLOCK, count - start)
            for i in range(size):
                put_row(x_ref, at + i, piece[local + start + i])
            for a in range(3):
                low = max(0, row + start + 1 - a)
                high = min(height, row + start + size + 1 - a)
                if high <= low:
                    continue
                skip = low - (row + start + 1 - a)
                n = high - low
                for b in range(3):
                    lhs = x_ref[b, at + skip : at + skip + n].reshape(n * width, slab)
                    part = jnp.dot(lhs, w_ref[a, b], preferred_element_type=F32).reshape(n, width, -1)
                    for i in range(n):
                        term = turn(part[i], b)
                        if low + i in written:
                            total_ref[low + i] += term
                        else:
                            total_ref[low + i] = term + initial
                            written.add(low + i)
            at += size


def accumulate_kernel(spans, n, started, *refs):
    pieces, w_ref, total_ref, x_ref = refs[:n], refs[n], refs[-2], refs[-1]
    written = set(range(total_ref.shape[0])) if started else set()
    spans = [(pieces[p], local, row, count) for p, local, row, count in spans]
    add_rows(spans, w_ref, total_ref, x_ref, written, None if started else own_bias(refs[n + 1], total_ref.shape[2]))


def own_bias(bias_ref, outs):
    if bias_ref.shape[1] == outs:
        return bias_ref[...]
    return bias_ref[:, pl.ds(pl.multiple_of(lax.axis_index("filt") * outs, outs), outs)]


def accumulate(spans, pieces, weights, total, shape, after=None, bias=None):
    count = sum(s[3] for s in spans)
    width, slab = shape[1], weights.shape[2]
    operands = [*pieces, weights]
    aliases = {}
    if total is not None:
        aliases = {len(operands): 0}
        operands.append(total)
    else:
        operands.append(bias)
    if after is not None:
        operands.append(after)
    return pl.pallas_call(
        functools.partial(accumulate_kernel, spans, len(pieces), total is not None),
        out_shape=jax.ShapeDtypeStruct(shape, F32),
        in_specs=[VMEM] * len(operands),
        out_specs=VMEM,
        scratch_shapes=[pltpu.VMEM((3, count, width, slab), BF16)],
        input_output_aliases=aliases,
        compiler_params=PARAMS,
        cost_estimate=cost(count * width * 9, slab, shape[2]),
        name="accumulate",
    )(*operands)


def pick_kernel(low, high, rows_ref, after_ref, out_ref):
    out_ref[...] = rows_ref[low:high]


def pick(rows, low, high, after):
    shape = (high - low, *rows.shape[1:])
    return call(functools.partial(pick_kernel, low, high), "pick", shape, BF16, [rows, after], cost(1, 1, 1))


def cost(pixels, slab, outs):
    return pl.CostEstimate(flops=2 * pixels * slab * outs, bytes_accessed=1 << 20, transcendentals=0)


def parity(axis):
    return lax.rem(lax.axis_index(axis), 2)


def swap_pairs(axis):
    count = lax.axis_size(axis)
    return [[p for i in range(start, count - 1, 2) for p in ((i, i + 1), (i + 1, i))] for start in (1, 0)]


def outermost_kernel(groups, *refs):
    rims, outs = refs[:groups], refs[-2:]
    width = outs[0].shape[1]
    odd = parity("row")
    for swap, out_ref in enumerate(outs):
        start = pl.multiple_of((odd if swap == 0 else 1 - odd) * width, width)
        for g in range(groups):
            out_ref[g] = rims[g][pl.ds(start, width), :]


def edges_kernel(groups, *refs):
    rims, swapped, outs, col_ref = refs[:groups], refs[groups : groups + 2], refs[-3:-1], refs[-1]
    width = swapped[0].shape[1]
    height = outs[0].shape[1] - 2
    odd_row, odd_col = parity("row") == 1, parity("col") == 1
    for g in range(groups):
        for side, at in enumerate((0, width - 16)):
            pixels = [ref[g, at : at + 16, :].astype(F32)[side * 15 : side * 15 + 1, :] for ref in swapped]
            start = 2 * width + side * height
            col_ref[side, 0:1, :] = jnp.where(odd_row, pixels[1], pixels[0])
            col_ref[side, 1 : height + 1, :] = rims[g][start : start + height, :].astype(F32)
            col_ref[side, height + 1 :, :] = jnp.where(odd_row, pixels[0], pixels[1])
        outs[0][g] = jnp.where(odd_col, col_ref[1], col_ref[0]).astype(BF16)
        outs[1][g] = jnp.where(odd_col, col_ref[0], col_ref[1]).astype(BF16)


def outer_rows_kernel(groups, *refs):
    swapped, w_refs, fix_ref, x_ref = refs[:2], refs[2 : 2 + groups], refs[-2], refs[-1]
    odd = parity("row") == 1
    for i, a in enumerate((0, 2)):
        fix = None
        for g in range(groups):
            put_row(x_ref, 0, jnp.where(odd, swapped[1 - i][g], swapped[i][g]))
            for b in range(3):
                part = turn(jnp.dot(x_ref[b, 0], w_refs[g][a, b], preferred_element_type=F32), b)
                fix = part if fix is None else fix + part
        fix_ref[i] = fix


def outer_cols_kernel(groups, *refs):
    swapped, w_refs, fix_ref = refs[:2], refs[2 : 2 + groups], refs[-1]
    height = fix_ref.shape[1]
    odd = parity("col") == 1
    for i, b in enumerate((0, 2)):
        fix = None
        for g in range(groups):
            pixels = jnp.where(odd, swapped[1 - i][g], swapped[i][g])
            for a in range(3):
                part = jnp.dot(pixels, w_refs[g][a, b], preferred_element_type=F32)[a : a + height]
                fix = part if fix is None else fix + part
        fix_ref[i] = fix


def finish_row(value, h, rows_ref, cols_ref):
    height, width = cols_ref.shape[1], value.shape[0]
    if h == 0:
        value += rows_ref[0]
    if h == height - 1:
        value += rows_ref[1]
    edge = lax.broadcasted_iota(jnp.int32, (8, value.shape[1]), 0)
    first = value[0:8] + jnp.where(edge == 0, cols_ref[0, h : h + 1, :], 0)
    final = value[width - 8 :] + jnp.where(edge == 7, cols_ref[1, h : h + 1, :], 0)
    return jnp.concatenate([first, value[8 : width - 8], final], 0).astype(BF16).T


def upper_kernel(total_ref, rows_ref, cols_ref, out_ref):
    turned = [finish_row(total_ref[h], h, rows_ref, cols_ref) for h in range(out_ref.shape[1])]
    out_ref[...] = jnp.swapaxes(jnp.stack(turned, 0), 0, 1)


def middle_kernel(start, total_ref, rows_ref, cols_ref, out_ref):
    for i in range(out_ref.shape[0]):
        out_ref[i] = finish_row(total_ref[start + i], start + i, rows_ref, cols_ref)


def last_kernel(piece, w_ref, total_ref, rows_ref, cols_ref, upper_ref, middle_ref, out_ref, x_ref, lower_ref, sems):
    outs, height, width = out_ref.shape
    half, done = upper_ref.shape[1], middle_ref.shape[0]
    first = pltpu.make_async_copy(upper_ref, out_ref.at[:, 0:half, :], sems.at[0])
    first.start()
    count = piece.shape[0]
    for i in range(count):
        put_row(x_ref, i, piece[i])
    values = [total_ref[h] for h in range(half + done, height)]
    for a in range(3):
        for b in range(3):
            part = jnp.dot(x_ref[b].reshape(count * width, -1), w_ref[a, b], preferred_element_type=F32).reshape(count, width, outs)
            for i in range(count):
                values[i + 2 - a] += turn(part[i], b)
    turned = [middle_ref[i] for i in range(done)]
    turned += [finish_row(value, half + done + i, rows_ref, cols_ref) for i, value in enumerate(values)]
    lower_ref[...] = jnp.swapaxes(jnp.stack(turned, 0), 0, 1)
    second = pltpu.make_async_copy(lower_ref, out_ref.at[:, half:height, :], sems.at[1])
    second.start()
    first.wait()
    second.wait()


def call(kernel, name, shape, dtype, operands, estimate, scratch=(), out=VMEM):
    return pl.pallas_call(
        kernel,
        out_shape=jax.ShapeDtypeStruct(shape, dtype),
        in_specs=[VMEM] * len(operands),
        out_specs=out,
        scratch_shapes=scratch,
        compiler_params=PARAMS,
        cost_estimate=estimate,
        name=name,
    )(*operands)


def calls(kernel, name, shapes, operands, scratch=(), estimate=None):
    return pl.pallas_call(
        kernel,
        out_shape=[jax.ShapeDtypeStruct(shape, BF16) for shape in shapes],
        in_specs=[VMEM] * len(operands),
        out_specs=[VMEM] * len(shapes),
        scratch_shapes=scratch,
        compiler_params=PARAMS,
        cost_estimate=estimate or cost(1, 1, 1),
        name=name,
    )(*operands)


def weights_kernel(groups, kernel_ref, *refs):
    outs, sems = refs[:-1], refs[-1]
    slab, width = outs[0].shape[2:]
    owner = lax.axis_index("filt")
    own = pl.ds(pl.multiple_of(owner * width, width), width)
    copies = []
    for shift, out in enumerate(outs):
        group = pl.ds(pl.multiple_of(lax.rem(owner - shift + groups, groups) * slab, slab), slab)
        for a in range(3):
            copies.append(pltpu.make_async_copy(kernel_ref.at[a, :, group, own], out.at[a], sems.at[shift, a]))
    for copy in copies:
        copy.start()
    for copy in copies:
        copy.wait()


def split_weights(kernel, groups, slab, outs):
    if outs % 128 == 0 and slab % 128 == 0:
        return pl.pallas_call(
            functools.partial(weights_kernel, groups),
            out_shape=[jax.ShapeDtypeStruct((3, 3, slab, outs), BF16)] * groups,
            in_specs=[HBM],
            out_specs=[VMEM] * groups,
            scratch_shapes=[pltpu.SemaphoreType.DMA((groups, 3))],
            compiler_params=pltpu.CompilerParams(vmem_limit_bytes=48 << 20),
            name="split_weights",
        )(kernel)
    owner = lax.axis_index("filt")
    own = lax.dynamic_slice_in_dim(kernel, owner * outs, outs, 3)
    order = [lax.rem(owner - shift + groups, groups) for shift in range(groups)]
    return [lax.dynamic_slice_in_dim(own, group * slab, slab, 2) for group in order]


def body(features, kernel, bias):
    groups = lax.axis_size("filt")
    slab, height, width = features.shape
    outs = kernel.shape[3] // groups
    half = height // 2
    chunks = ((1, half + 2), (half + 2, height - 2), (height - 2, height - 1))

    rim, upper_rows, lower_rows = relayout(features, (chunks[0], (chunks[0][1], height - 1)))
    rings = [[(i, (i + shift) % groups) for i in range(groups)] for shift in range(1, groups)]
    rims = [rim] + [lax.ppermute(rim, "filt", ring) for ring in rings]
    sets = [[lax.ppermute(upper_rows, "filt", ring)] for ring in rings]
    pairs = [r[0 : 2 * width].reshape(2, width, slab) for r in rims]
    outer = [(0, 0, 0, 1), (0, 1, height - 1, 1)]
    shape = (height, width, outs)

    weights = split_weights(kernel, groups, slab, outs)
    bias = bias[None, :]
    if outs % 128 != 0:
        bias = lax.dynamic_slice_in_dim(bias, lax.axis_index("filt") * outs, outs, 1)
    spans = [*outer, (1, 0, 1, half + 1), (2, 0, half + 2, height - half - 3)]
    second = pick(lower_rows, 0, chunks[1][1] - chunks[1][0], weights[0])
    for received, ring in zip(sets, rings):
        received.append(lax.ppermute(second, "filt", ring))

    row_pairs, col_pairs = swap_pairs("row"), swap_pairs("col")
    sent = calls(functools.partial(outermost_kernel, groups), "outermost", [(groups, width, slab)] * 2, rims, estimate=WAIT)
    outer_rows = [lax.ppermute(v, "row", p) for v, p in zip(sent, row_pairs)]
    total = accumulate(spans, [pairs[0], upper_rows, lower_rows], weights[0], None, shape, rims[-1], bias)
    for g in range(1, groups):
        total = accumulate(outer, [pairs[g]], weights[g], total, shape)
    edge = pltpu.VMEM((2, height + 2, slab), F32)
    sent = calls(functools.partial(edges_kernel, groups), "edges", [(groups, height + 2, slab)] * 2, [*rims, *outer_rows], [edge])
    third = pick(lower_rows, chunks[2][0] - chunks[1][0], chunks[2][1] - chunks[1][0], sent[0])
    for received, ring in zip(sets, rings):
        received.append(lax.ppermute(third, "filt", ring))
    outer_cols = [lax.ppermute(v, "col", p) for v, p in zip(sent, col_pairs)]
    rows_fix = call(
        functools.partial(outer_rows_kernel, groups), "outer_rows", (2, width, outs), F32,
        [*outer_rows, *weights, *sent], cost(6 * width * groups, slab, outs), [pltpu.VMEM((3, 1, width, slab), BF16)],
    )
    for g in range(1, groups):
        a, b, c = sets[g - 1]
        total = accumulate([(0, 0, chunks[0][0], a.shape[0])], [a], weights[g], total, shape, rows_fix)
        if g < groups - 1:
            total = accumulate([(0, 0, chunks[1][0], b.shape[0])], [b], weights[g], total, shape)
            total = accumulate([(0, 0, chunks[2][0], c.shape[0])], [c], weights[g], total, shape)
    cols_fix = call(
        functools.partial(outer_cols_kernel, groups), "outer_cols", (2, height, outs), F32,
        [*outer_cols, *weights, total], cost(6 * 256 * groups, slab, outs),
    )
    top = call(upper_kernel, "upper", (outs, half, width), BF16, [total, rows_fix, cols_fix], cost(256, slab, outs))
    total = accumulate([(0, 0, chunks[1][0], b.shape[0])], [b], weights[-1], total, shape, top)
    done = chunks[2][0] - 1 - half
    middle = call(functools.partial(middle_kernel, half), "middle", (done, outs, width), BF16, [total, rows_fix, cols_fix], cost(1, 1, 1))
    scratch = [
        pltpu.VMEM((3, c.shape[0], width, slab), BF16),
        pltpu.VMEM((outs, height - half, width), BF16),
        pltpu.SemaphoreType.DMA((2,)),
    ]
    return call(
        last_kernel, "last", (outs, height, width), BF16,
        [c, weights[-1], total, rows_fix, cols_fix, top, middle], cost(9 * 256, slab, outs), scratch, HBM,
    )


def solution(mesh):
    return jax.shard_map(
        body,
        mesh=mesh,
        in_specs=(P("filt", "row", "col"), P(), P()),
        out_specs=P("filt", "row", "col"),
        check_vma=False,
    )
```

```python
import functools

import jax
import jax.numpy as jnp
from jax import lax
from jax.experimental import pallas as pl
from jax.experimental.pallas import tpu as pltpu
from jax.sharding import PartitionSpec as P

BF16, F32 = jnp.bfloat16, jnp.float32
VMEM = pl.BlockSpec(memory_space=pltpu.VMEM)
HBM = pl.BlockSpec(memory_space=pltpu.HBM)
PARAMS = pltpu.CompilerParams(vmem_limit_bytes=10 << 20)
WAIT = pl.CostEstimate(flops=4 * 10**9, bytes_accessed=1 << 20, transcendentals=0)
BLOCK = 4


def early_kernel(x_hbm, out_ref, x_ref, sems):
    slab = x_ref.shape[0]
    step = slab // 2 if slab % 256 == 0 else slab
    parts = [slice(at, at + step) for at in range(0, slab, step)]
    copies = [pltpu.make_async_copy(x_hbm.at[part, 0:8, :], x_ref.at[part], sems.at[i]) for i, part in enumerate(parts)]
    for copy in copies:
        copy.start()
    for copy, part in zip(copies, parts):
        copy.wait()
        group = jnp.swapaxes(x_ref[part], 0, 1)
        for h in range(out_ref.shape[0]):
            out_ref[h, :, part] = group[h + 1].T


def early(features, count):
    slab, _, width = features.shape
    return pl.pallas_call(
        early_kernel,
        out_shape=jax.ShapeDtypeStruct((count, width, slab), BF16),
        in_specs=[HBM],
        out_specs=VMEM,
        scratch_shapes=[pltpu.VMEM((slab, 8, width), BF16), pltpu.SemaphoreType.DMA((2,))],
        compiler_params=PARAMS,
        cost_estimate=WAIT,
        name="early",
    )(pltpu.with_memory_space_constraint(features, pltpu.HBM))


def relayout_kernel(chunks, x_ref, rim_ref, *refs):
    outs, col_ref = refs[:-1], refs[-1]
    slab, rows, width = x_ref.shape
    step = slab // 2 if slab % 256 == 0 else slab
    for lanes in [slice(at, at + step) for at in range(0, slab, step)]:
        group = jnp.swapaxes(x_ref[lanes], 0, 1)
        for h in range(rows):
            pixels = group[h].T
            col_ref[h : h + 1, lanes] = pixels[0:16].astype(F32)[0:1, :]
            col_ref[rows + h : rows + h + 1, lanes] = pixels[width - 16 :].astype(F32)[15:16, :]
            if h == 0:
                rim_ref[0:width, lanes] = pixels
            elif h == rows - 1:
                rim_ref[width : 2 * width, lanes] = pixels
            else:
                for out, (first, last) in zip(outs, chunks):
                    if first <= h < last:
                        out[h - first, :, lanes] = pixels
    rim_ref[2 * width :, :] = col_ref[...].astype(BF16)


def relayout(features, chunks):
    slab, rows, width = features.shape
    shapes = [(2 * width + 2 * rows, slab)] + [(last - first, width, slab) for first, last in chunks]
    return calls(functools.partial(relayout_kernel, chunks), "relayout", shapes, [features], [pltpu.VMEM((2 * rows, slab), F32)])


def put_row(x_ref, at, value):
    width, slab = value.shape
    edge = lax.broadcasted_iota(jnp.int32, (16, slab), 0)
    x_ref[1, at] = value
    x_ref[0, at, 0 : width - 16, :] = value[0 : width - 16]
    x_ref[0, at, width - 16 :, :] = jnp.where(edge == 15, 0, value[width - 16 :].astype(F32)).astype(BF16)
    x_ref[2, at, 16:, :] = value[16:]
    x_ref[2, at, 0:16, :] = jnp.where(edge == 0, 0, value[0:16].astype(F32)).astype(BF16)


def turn(part, b):
    return part if b == 1 else pltpu.roll(part, 1 if b == 0 else part.shape[0] - 1, 0)


def add_rows(spans, w_ref, total_ref, x_ref, written, initial=None):
    height, width, _ = total_ref.shape
    slab = w_ref.shape[2]
    at = 0
    for piece, local, row, count in spans:
        for start in range(0, count, BLOCK):
            size = min(BLOCK, count - start)
            for i in range(size):
                put_row(x_ref, at + i, piece[local + start + i])
            for a in range(3):
                low = max(0, row + start + 1 - a)
                high = min(height, row + start + size + 1 - a)
                if high <= low:
                    continue
                skip = low - (row + start + 1 - a)
                n = high - low
                for b in range(3):
                    lhs = x_ref[b, at + skip : at + skip + n].reshape(n * width, slab)
                    part = jnp.dot(lhs, w_ref[a, b], preferred_element_type=F32).reshape(n, width, -1)
                    for i in range(n):
                        term = turn(part[i], b)
                        if low + i in written:
                            total_ref[low + i] += term
                        else:
                            total_ref[low + i] = term + initial
                            written.add(low + i)
            at += size


def accumulate_kernel(spans, n, started, *refs):
    pieces, w_ref, total_ref, x_ref = refs[:n], refs[n], refs[-2], refs[-1]
    written = set(range(total_ref.shape[0])) if started else set()
    spans = [(pieces[p], local, row, count) for p, local, row, count in spans]
    add_rows(spans, w_ref, total_ref, x_ref, written, None if started else own_bias(refs[n + 1], total_ref.shape[2]))


def own_bias(bias_ref, outs):
    if bias_ref.shape[1] == outs:
        return bias_ref[...]
    return bias_ref[:, pl.ds(pl.multiple_of(lax.axis_index("filt") * outs, outs), outs)]


def accumulate(spans, pieces, weights, total, shape, after=None, bias=None):
    count = sum(s[3] for s in spans)
    width, slab = shape[1], weights.shape[2]
    operands = [*pieces, weights]
    aliases = {}
    if total is not None:
        aliases = {len(operands): 0}
        operands.append(total)
    else:
        operands.append(bias)
    if after is not None:
        operands.append(after)
    return pl.pallas_call(
        functools.partial(accumulate_kernel, spans, len(pieces), total is not None),
        out_shape=jax.ShapeDtypeStruct(shape, F32),
        in_specs=[VMEM] * len(operands),
        out_specs=VMEM,
        scratch_shapes=[pltpu.VMEM((3, count, width, slab), BF16)],
        input_output_aliases=aliases,
        compiler_params=PARAMS,
        cost_estimate=cost(count * width * 9, slab, shape[2]),
        name="accumulate",
    )(*operands)


def pick_kernel(low, high, rows_ref, after_ref, out_ref):
    out_ref[...] = rows_ref[low:high]


def pick(rows, low, high, after):
    shape = (high - low, *rows.shape[1:])
    return call(functools.partial(pick_kernel, low, high), "pick", shape, BF16, [rows, after], cost(1, 1, 1))


def cost(pixels, slab, outs):
    return pl.CostEstimate(flops=2 * pixels * slab * outs, bytes_accessed=1 << 20, transcendentals=0)


def parity(axis):
    return lax.rem(lax.axis_index(axis), 2)


def swap_pairs(axis):
    count = lax.axis_size(axis)
    return [[p for i in range(start, count - 1, 2) for p in ((i, i + 1), (i + 1, i))] for start in (1, 0)]


def outermost_kernel(groups, *refs):
    rims, outs = refs[:groups], refs[-2:]
    width = outs[0].shape[1]
    odd = parity("row")
    for swap, out_ref in enumerate(outs):
        start = pl.multiple_of((odd if swap == 0 else 1 - odd) * width, width)
        for g in range(groups):
            out_ref[g] = rims[g][pl.ds(start, width), :]


def edges_kernel(groups, *refs):
    rims, swapped, outs, col_ref = refs[:groups], refs[groups : groups + 2], refs[-3:-1], refs[-1]
    width = swapped[0].shape[1]
    height = outs[0].shape[1] - 2
    odd_row, odd_col = parity("row") == 1, parity("col") == 1
    for g in range(groups):
        for side, at in enumerate((0, width - 16)):
            pixels = [ref[g, at : at + 16, :].astype(F32)[side * 15 : side * 15 + 1, :] for ref in swapped]
            start = 2 * width + side * height
            col_ref[side, 0:1, :] = jnp.where(odd_row, pixels[1], pixels[0])
            col_ref[side, 1 : height + 1, :] = rims[g][start : start + height, :].astype(F32)
            col_ref[side, height + 1 :, :] = jnp.where(odd_row, pixels[0], pixels[1])
        outs[0][g] = jnp.where(odd_col, col_ref[1], col_ref[0]).astype(BF16)
        outs[1][g] = jnp.where(odd_col, col_ref[0], col_ref[1]).astype(BF16)


def outer_rows_kernel(groups, *refs):
    swapped, w_refs, fix_ref, x_ref = refs[:2], refs[2 : 2 + groups], refs[-2], refs[-1]
    odd = parity("row") == 1
    for i, a in enumerate((0, 2)):
        fix = None
        for g in range(groups):
            put_row(x_ref, 0, jnp.where(odd, swapped[1 - i][g], swapped[i][g]))
            for b in range(3):
                part = turn(jnp.dot(x_ref[b, 0], w_refs[g][a, b], preferred_element_type=F32), b)
                fix = part if fix is None else fix + part
        fix_ref[i] = fix


def outer_cols_kernel(groups, *refs):
    swapped, w_refs, fix_ref = refs[:2], refs[2 : 2 + groups], refs[-1]
    height = fix_ref.shape[1]
    odd = parity("col") == 1
    for i, b in enumerate((0, 2)):
        fix = None
        for g in range(groups):
            pixels = jnp.where(odd, swapped[1 - i][g], swapped[i][g])
            for a in range(3):
                part = jnp.dot(pixels, w_refs[g][a, b], preferred_element_type=F32)[a : a + height]
                fix = part if fix is None else fix + part
        fix_ref[i] = fix


def finish_row(value, h, rows_ref, cols_ref):
    height, width = cols_ref.shape[1], value.shape[0]
    if h == 0:
        value += rows_ref[0]
    if h == height - 1:
        value += rows_ref[1]
    edge = lax.broadcasted_iota(jnp.int32, (8, value.shape[1]), 0)
    first = value[0:8] + jnp.where(edge == 0, cols_ref[0, h : h + 1, :], 0)
    final = value[width - 8 :] + jnp.where(edge == 7, cols_ref[1, h : h + 1, :], 0)
    return jnp.concatenate([first, value[8 : width - 8], final], 0).astype(BF16).T


def upper_kernel(total_ref, rows_ref, cols_ref, out_ref):
    turned = [finish_row(total_ref[h], h, rows_ref, cols_ref) for h in range(out_ref.shape[1])]
    out_ref[...] = jnp.swapaxes(jnp.stack(turned, 0), 0, 1)


def middle_kernel(start, total_ref, rows_ref, cols_ref, out_ref):
    for i in range(out_ref.shape[0]):
        out_ref[i] = finish_row(total_ref[start + i], start + i, rows_ref, cols_ref)


def last_kernel(piece, w_ref, total_ref, rows_ref, cols_ref, upper_ref, middle_ref, out_ref, x_ref, lower_ref, sems):
    outs, height, width = out_ref.shape
    half, done = upper_ref.shape[1], middle_ref.shape[0]
    first = pltpu.make_async_copy(upper_ref, out_ref.at[:, 0:half, :], sems.at[0])
    first.start()
    count = piece.shape[0]
    for i in range(count):
        put_row(x_ref, i, piece[i])
    values = [total_ref[h] for h in range(half + done, height)]
    for a in range(3):
        for b in range(3):
            part = jnp.dot(x_ref[b].reshape(count * width, -1), w_ref[a, b], preferred_element_type=F32).reshape(count, width, outs)
            for i in range(count):
                values[i + 2 - a] += turn(part[i], b)
    turned = [middle_ref[i] for i in range(done)]
    turned += [finish_row(value, half + done + i, rows_ref, cols_ref) for i, value in enumerate(values)]
    lower_ref[...] = jnp.swapaxes(jnp.stack(turned, 0), 0, 1)
    second = pltpu.make_async_copy(lower_ref, out_ref.at[:, half:height, :], sems.at[1])
    second.start()
    first.wait()
    second.wait()


def call(kernel, name, shape, dtype, operands, estimate, scratch=(), out=VMEM):
    return pl.pallas_call(
        kernel,
        out_shape=jax.ShapeDtypeStruct(shape, dtype),
        in_specs=[VMEM] * len(operands),
        out_specs=out,
        scratch_shapes=scratch,
        compiler_params=PARAMS,
        cost_estimate=estimate,
        name=name,
    )(*operands)


def calls(kernel, name, shapes, operands, scratch=(), estimate=None):
    return pl.pallas_call(
        kernel,
        out_shape=[jax.ShapeDtypeStruct(shape, BF16) for shape in shapes],
        in_specs=[VMEM] * len(operands),
        out_specs=[VMEM] * len(shapes),
        scratch_shapes=scratch,
        compiler_params=PARAMS,
        cost_estimate=estimate or cost(1, 1, 1),
        name=name,
    )(*operands)


def weights_kernel(groups, kernel_ref, after_ref, *refs):
    outs, sems = refs[:-1], refs[-1]
    slab, width = outs[0].shape[2:]
    owner = lax.axis_index("filt")
    own = pl.ds(pl.multiple_of(owner * width, width), width)
    copies = []
    for shift, out in enumerate(outs):
        group = pl.ds(pl.multiple_of(lax.rem(owner - shift + groups, groups) * slab, slab), slab)
        for a in range(3):
            copies.append(pltpu.make_async_copy(kernel_ref.at[a, :, group, own], out.at[a], sems.at[shift, a]))
    for copy in copies:
        copy.start()
    for copy in copies:
        copy.wait()


def split_weights(kernel, groups, slab, outs, after):
    if outs % 128 == 0 and slab % 128 == 0:
        return pl.pallas_call(
            functools.partial(weights_kernel, groups),
            out_shape=[jax.ShapeDtypeStruct((3, 3, slab, outs), BF16)] * groups,
            in_specs=[HBM, VMEM],
            out_specs=[VMEM] * groups,
            scratch_shapes=[pltpu.SemaphoreType.DMA((groups, 3))],
            compiler_params=pltpu.CompilerParams(vmem_limit_bytes=48 << 20),
            cost_estimate=pl.CostEstimate(flops=2 * 10**9, bytes_accessed=1 << 20, transcendentals=0),
            name="split_weights",
        )(kernel, after)
    owner = lax.axis_index("filt")
    own = lax.dynamic_slice_in_dim(kernel, owner * outs, outs, 3)
    order = [lax.rem(owner - shift + groups, groups) for shift in range(groups)]
    return [lax.dynamic_slice_in_dim(own, group * slab, slab, 2) for group in order]


def body(features, kernel, bias):
    groups = lax.axis_size("filt")
    slab, height, width = features.shape
    outs = kernel.shape[3] // groups
    half = height // 2
    chunks = ((3, half + 2), (half + 2, height - 2), (height - 2, height - 1))

    rings = [[(i, (i + shift) % groups) for i in range(groups)] for shift in range(1, groups)]
    soon = early(features, chunks[0][0] - 1)
    soons = [lax.ppermute(soon, "filt", ring) for ring in rings]
    rim, upper_rows, lower_rows = relayout(features, (chunks[0], (chunks[0][1], height - 1)))
    rims = [rim] + [lax.ppermute(rim, "filt", ring) for ring in rings]
    sets = [[lax.ppermute(upper_rows, "filt", ring)] for ring in rings]
    pairs = [r[0 : 2 * width].reshape(2, width, slab) for r in rims]
    outer = [(0, 0, 0, 1), (0, 1, height - 1, 1)]
    shape = (height, width, outs)

    weights = split_weights(kernel, groups, slab, outs, soons[0])
    bias = bias[None, :]
    if outs % 128 != 0:
        bias = lax.dynamic_slice_in_dim(bias, lax.axis_index("filt") * outs, outs, 1)
    spans = [*outer, (1, 0, 1, soon.shape[0]), (2, 0, chunks[0][0], upper_rows.shape[0]), (3, 0, chunks[0][1], lower_rows.shape[0])]
    second = pick(lower_rows, 0, chunks[1][1] - chunks[1][0], weights[0])
    for received, ring in zip(sets, rings):
        received.append(lax.ppermute(second, "filt", ring))

    row_pairs, col_pairs = swap_pairs("row"), swap_pairs("col")
    sent = calls(functools.partial(outermost_kernel, groups), "outermost", [(groups, width, slab)] * 2, rims, estimate=WAIT)
    outer_rows = [lax.ppermute(v, "row", p) for v, p in zip(sent, row_pairs)]
    total = accumulate(spans, [pairs[0], soon, upper_rows, lower_rows], weights[0], None, shape, rims[-1], bias)
    for g in range(1, groups):
        total = accumulate(outer, [pairs[g]], weights[g], total, shape)
    edge = pltpu.VMEM((2, height + 2, slab), F32)
    sent = calls(functools.partial(edges_kernel, groups), "edges", [(groups, height + 2, slab)] * 2, [*rims, *outer_rows], [edge])
    third = pick(lower_rows, chunks[2][0] - chunks[1][0], chunks[2][1] - chunks[1][0], sent[0])
    for received, ring in zip(sets, rings):
        received.append(lax.ppermute(third, "filt", ring))
    outer_cols = [lax.ppermute(v, "col", p) for v, p in zip(sent, col_pairs)]
    rows_fix = call(
        functools.partial(outer_rows_kernel, groups), "outer_rows", (2, width, outs), F32,
        [*outer_rows, *weights, *sent], cost(6 * width * groups, slab, outs), [pltpu.VMEM((3, 1, width, slab), BF16)],
    )
    for g in range(1, groups):
        a, b, c = sets[g - 1]
        spans = [(0, 0, 1, soon.shape[0]), (1, 0, chunks[0][0], a.shape[0])]
        total = accumulate(spans, [soons[g - 1], a], weights[g], total, shape, rows_fix)
        if g < groups - 1:
            total = accumulate([(0, 0, chunks[1][0], b.shape[0])], [b], weights[g], total, shape)
            total = accumulate([(0, 0, chunks[2][0], c.shape[0])], [c], weights[g], total, shape)
    cols_fix = call(
        functools.partial(outer_cols_kernel, groups), "outer_cols", (2, height, outs), F32,
        [*outer_cols, *weights, total], cost(6 * 256 * groups, slab, outs),
    )
    top = call(upper_kernel, "upper", (outs, half, width), BF16, [total, rows_fix, cols_fix], cost(256, slab, outs))
    total = accumulate([(0, 0, chunks[1][0], b.shape[0])], [b], weights[-1], total, shape, top)
    done = chunks[2][0] - 1 - half
    middle = call(functools.partial(middle_kernel, half), "middle", (done, outs, width), BF16, [total, rows_fix, cols_fix], cost(1, 1, 1))
    scratch = [
        pltpu.VMEM((3, c.shape[0], width, slab), BF16),
        pltpu.VMEM((outs, height - half, width), BF16),
        pltpu.SemaphoreType.DMA((2,)),
    ]
    return call(
        last_kernel, "last", (outs, height, width), BF16,
        [c, weights[-1], total, rows_fix, cols_fix, top, middle], cost(9 * 256, slab, outs), scratch, HBM,
    )


def solution(mesh):
    return jax.shard_map(
        body,
        mesh=mesh,
        in_specs=(P("filt", "row", "col"), P(), P()),
        out_specs=P("filt", "row", "col"),
        check_vma=False,
    )
```

```python
import functools

import jax
import jax.numpy as jnp
from jax import lax
from jax.experimental import pallas as pl
from jax.experimental.pallas import tpu as pltpu
from jax.sharding import PartitionSpec as P

BF16, F32 = jnp.bfloat16, jnp.float32
VMEM = pl.BlockSpec(memory_space=pltpu.VMEM)
HBM = pl.BlockSpec(memory_space=pltpu.HBM)
PARAMS = pltpu.CompilerParams(vmem_limit_bytes=10 << 20)
WAIT = pl.CostEstimate(flops=4 * 10**9, bytes_accessed=1 << 20, transcendentals=0)
BLOCK = 4


def early_kernel(x_hbm, out_ref, x_ref, sems):
    slab = x_ref.shape[0]
    step = slab // 2 if slab % 256 == 0 else slab
    parts = [slice(at, at + step) for at in range(0, slab, step)]
    copies = [pltpu.make_async_copy(x_hbm.at[part, 0:8, :], x_ref.at[part], sems.at[i]) for i, part in enumerate(parts)]
    for copy in copies:
        copy.start()
    for copy, part in zip(copies, parts):
        copy.wait()
        group = jnp.swapaxes(x_ref[part], 0, 1)
        for h in range(out_ref.shape[0]):
            out_ref[h, :, part] = group[h + 1].T


def early(features, count):
    slab, _, width = features.shape
    return pl.pallas_call(
        early_kernel,
        out_shape=jax.ShapeDtypeStruct((count, width, slab), BF16),
        in_specs=[HBM],
        out_specs=VMEM,
        scratch_shapes=[pltpu.VMEM((slab, 8, width), BF16), pltpu.SemaphoreType.DMA((2,))],
        compiler_params=PARAMS,
        cost_estimate=WAIT,
        name="early",
    )(pltpu.with_memory_space_constraint(features, pltpu.HBM))


def relayout_kernel(chunks, x_ref, rim_ref, *refs):
    outs, col_ref = refs[:-1], refs[-1]
    slab, rows, width = x_ref.shape
    step = slab // 2 if slab % 256 == 0 else slab
    for lanes in [slice(at, at + step) for at in range(0, slab, step)]:
        group = jnp.swapaxes(x_ref[lanes], 0, 1)
        for h in range(rows):
            pixels = group[h].T
            col_ref[h : h + 1, lanes] = pixels[0:16].astype(F32)[0:1, :]
            col_ref[rows + h : rows + h + 1, lanes] = pixels[width - 16 :].astype(F32)[15:16, :]
            if h == 0:
                rim_ref[0:width, lanes] = pixels
            elif h == rows - 1:
                rim_ref[width : 2 * width, lanes] = pixels
            else:
                for out, (first, last) in zip(outs, chunks):
                    if first <= h < last:
                        out[h - first, :, lanes] = pixels
    rim_ref[2 * width :, :] = col_ref[...].astype(BF16)


def relayout(features, chunks):
    slab, rows, width = features.shape
    shapes = [(2 * width + 2 * rows, slab)] + [(last - first, width, slab) for first, last in chunks]
    return calls(functools.partial(relayout_kernel, chunks), "relayout", shapes, [features], [pltpu.VMEM((2 * rows, slab), F32)], pl.CostEstimate(flops=0 * 10**9, bytes_accessed=1 << 20, transcendentals=0))


def put_row(x_ref, at, value):
    width, slab = value.shape
    edge = lax.broadcasted_iota(jnp.int32, (16, slab), 0)
    x_ref[1, at] = value
    x_ref[0, at, 0 : width - 16, :] = value[0 : width - 16]
    x_ref[0, at, width - 16 :, :] = jnp.where(edge == 15, 0, value[width - 16 :].astype(F32)).astype(BF16)
    x_ref[2, at, 16:, :] = value[16:]
    x_ref[2, at, 0:16, :] = jnp.where(edge == 0, 0, value[0:16].astype(F32)).astype(BF16)


def turn(part, b):
    return part if b == 1 else pltpu.roll(part, 1 if b == 0 else part.shape[0] - 1, 0)


def add_rows(spans, w_ref, total_ref, x_ref, written, initial=None):
    height, width, _ = total_ref.shape
    slab = w_ref.shape[2]
    at = 0
    for piece, local, row, count in spans:
        for start in range(0, count, BLOCK):
            size = min(BLOCK, count - start)
            for i in range(size):
                put_row(x_ref, at + i, piece[local + start + i])
            for a in range(3):
                low = max(0, row + start + 1 - a)
                high = min(height, row + start + size + 1 - a)
                if high <= low:
                    continue
                skip = low - (row + start + 1 - a)
                n = high - low
                for b in range(3):
                    lhs = x_ref[b, at + skip : at + skip + n].reshape(n * width, slab)
                    part = jnp.dot(lhs, w_ref[a, b], preferred_element_type=F32).reshape(n, width, -1)
                    for i in range(n):
                        term = turn(part[i], b)
                        if low + i in written:
                            total_ref[low + i] += term
                        else:
                            total_ref[low + i] = term + initial
                            written.add(low + i)
            at += size


def accumulate_kernel(spans, n, started, *refs):
    pieces, w_ref, total_ref, x_ref = refs[:n], refs[n], refs[-2], refs[-1]
    written = set(range(total_ref.shape[0])) if started else set()
    spans = [(pieces[p], local, row, count) for p, local, row, count in spans]
    add_rows(spans, w_ref, total_ref, x_ref, written, None if started else own_bias(refs[n + 1], total_ref.shape[2]))


def own_bias(bias_ref, outs):
    if bias_ref.shape[1] == outs:
        return bias_ref[...]
    return bias_ref[:, pl.ds(pl.multiple_of(lax.axis_index("filt") * outs, outs), outs)]


def accumulate(spans, pieces, weights, total, shape, after=None, bias=None):
    count = sum(s[3] for s in spans)
    width, slab = shape[1], weights.shape[2]
    operands = [*pieces, weights]
    aliases = {}
    if total is not None:
        aliases = {len(operands): 0}
        operands.append(total)
    else:
        operands.append(bias)
    if after is not None:
        operands.append(after)
    return pl.pallas_call(
        functools.partial(accumulate_kernel, spans, len(pieces), total is not None),
        out_shape=jax.ShapeDtypeStruct(shape, F32),
        in_specs=[VMEM] * len(operands),
        out_specs=VMEM,
        scratch_shapes=[pltpu.VMEM((3, count, width, slab), BF16)],
        input_output_aliases=aliases,
        compiler_params=PARAMS,
        cost_estimate=cost(count * width * 9, slab, shape[2]),
        name="accumulate",
    )(*operands)


def pick_kernel(low, high, rows_ref, after_ref, out_ref):
    out_ref[...] = rows_ref[low:high]


def pick(rows, low, high, after):
    shape = (high - low, *rows.shape[1:])
    return call(functools.partial(pick_kernel, low, high), "pick", shape, BF16, [rows, after], cost(1, 1, 1))


def cost(pixels, slab, outs):
    return pl.CostEstimate(flops=2 * pixels * slab * outs, bytes_accessed=1 << 20, transcendentals=0)


def parity(axis):
    return lax.rem(lax.axis_index(axis), 2)


def swap_pairs(axis):
    count = lax.axis_size(axis)
    return [[p for i in range(start, count - 1, 2) for p in ((i, i + 1), (i + 1, i))] for start in (1, 0)]


def outermost_kernel(groups, *refs):
    rims, outs = refs[:groups], refs[-2:]
    width = outs[0].shape[1]
    odd = parity("row")
    for swap, out_ref in enumerate(outs):
        start = pl.multiple_of((odd if swap == 0 else 1 - odd) * width, width)
        for g in range(groups):
            out_ref[g] = rims[g][pl.ds(start, width), :]


def edges_kernel(groups, *refs):
    rims, swapped, outs, col_ref = refs[:groups], refs[groups : groups + 2], refs[-3:-1], refs[-1]
    width = swapped[0].shape[1]
    height = outs[0].shape[1] - 2
    odd_row, odd_col = parity("row") == 1, parity("col") == 1
    for g in range(groups):
        for side, at in enumerate((0, width - 16)):
            pixels = [ref[g, at : at + 16, :].astype(F32)[side * 15 : side * 15 + 1, :] for ref in swapped]
            start = 2 * width + side * height
            col_ref[side, 0:1, :] = jnp.where(odd_row, pixels[1], pixels[0])
            col_ref[side, 1 : height + 1, :] = rims[g][start : start + height, :].astype(F32)
            col_ref[side, height + 1 :, :] = jnp.where(odd_row, pixels[0], pixels[1])
        outs[0][g] = jnp.where(odd_col, col_ref[1], col_ref[0]).astype(BF16)
        outs[1][g] = jnp.where(odd_col, col_ref[0], col_ref[1]).astype(BF16)


def outer_rows_kernel(groups, *refs):
    swapped, w_refs, fix_ref, x_ref = refs[:2], refs[2 : 2 + groups], refs[-2], refs[-1]
    odd = parity("row") == 1
    for i, a in enumerate((0, 2)):
        fix = None
        for g in range(groups):
            put_row(x_ref, 0, jnp.where(odd, swapped[1 - i][g], swapped[i][g]))
            for b in range(3):
                part = turn(jnp.dot(x_ref[b, 0], w_refs[g][a, b], preferred_element_type=F32), b)
                fix = part if fix is None else fix + part
        fix_ref[i] = fix


def outer_cols_kernel(groups, *refs):
    swapped, w_refs, fix_ref = refs[:2], refs[2 : 2 + groups], refs[-1]
    height = fix_ref.shape[1]
    odd = parity("col") == 1
    for i, b in enumerate((0, 2)):
        fix = None
        for g in range(groups):
            pixels = jnp.where(odd, swapped[1 - i][g], swapped[i][g])
            for a in range(3):
                part = jnp.dot(pixels, w_refs[g][a, b], preferred_element_type=F32)[a : a + height]
                fix = part if fix is None else fix + part
        fix_ref[i] = fix


def finish_row(value, h, rows_ref, cols_ref):
    height, width = cols_ref.shape[1], value.shape[0]
    if h == 0:
        value += rows_ref[0]
    if h == height - 1:
        value += rows_ref[1]
    edge = lax.broadcasted_iota(jnp.int32, (8, value.shape[1]), 0)
    first = value[0:8] + jnp.where(edge == 0, cols_ref[0, h : h + 1, :], 0)
    final = value[width - 8 :] + jnp.where(edge == 7, cols_ref[1, h : h + 1, :], 0)
    return jnp.concatenate([first, value[8 : width - 8], final], 0).astype(BF16).T


def upper_kernel(total_ref, rows_ref, cols_ref, out_ref):
    turned = [finish_row(total_ref[h], h, rows_ref, cols_ref) for h in range(out_ref.shape[1])]
    out_ref[...] = jnp.swapaxes(jnp.stack(turned, 0), 0, 1)


def middle_kernel(start, total_ref, rows_ref, cols_ref, out_ref):
    for i in range(out_ref.shape[0]):
        out_ref[i] = finish_row(total_ref[start + i], start + i, rows_ref, cols_ref)


def last_kernel(piece, w_ref, total_ref, rows_ref, cols_ref, upper_ref, middle_ref, out_ref, x_ref, lower_ref, sems):
    outs, height, width = out_ref.shape
    half, done = upper_ref.shape[1], middle_ref.shape[0]
    first = pltpu.make_async_copy(upper_ref, out_ref.at[:, 0:half, :], sems.at[0])
    first.start()
    count = piece.shape[0]
    for i in range(count):
        put_row(x_ref, i, piece[i])
    values = [total_ref[h] for h in range(half + done, height)]
    for a in range(3):
        for b in range(3):
            part = jnp.dot(x_ref[b].reshape(count * width, -1), w_ref[a, b], preferred_element_type=F32).reshape(count, width, outs)
            for i in range(count):
                values[i + 2 - a] += turn(part[i], b)
    turned = [middle_ref[i] for i in range(done)]
    turned += [finish_row(value, half + done + i, rows_ref, cols_ref) for i, value in enumerate(values)]
    lower_ref[...] = jnp.swapaxes(jnp.stack(turned, 0), 0, 1)
    second = pltpu.make_async_copy(lower_ref, out_ref.at[:, half:height, :], sems.at[1])
    second.start()
    first.wait()
    second.wait()


def call(kernel, name, shape, dtype, operands, estimate, scratch=(), out=VMEM):
    return pl.pallas_call(
        kernel,
        out_shape=jax.ShapeDtypeStruct(shape, dtype),
        in_specs=[VMEM] * len(operands),
        out_specs=out,
        scratch_shapes=scratch,
        compiler_params=PARAMS,
        cost_estimate=estimate,
        name=name,
    )(*operands)


def calls(kernel, name, shapes, operands, scratch=(), estimate=None):
    return pl.pallas_call(
        kernel,
        out_shape=[jax.ShapeDtypeStruct(shape, BF16) for shape in shapes],
        in_specs=[VMEM] * len(operands),
        out_specs=[VMEM] * len(shapes),
        scratch_shapes=scratch,
        compiler_params=PARAMS,
        cost_estimate=estimate or cost(1, 1, 1),
        name=name,
    )(*operands)


def weights_kernel(groups, kernel_ref, *refs):
    outs, sems = refs[:-1], refs[-1]
    slab, width = outs[0].shape[2:]
    owner = lax.axis_index("filt")
    own = pl.ds(pl.multiple_of(owner * width, width), width)
    copies = []
    for shift, out in enumerate(outs):
        group = pl.ds(pl.multiple_of(lax.rem(owner - shift + groups, groups) * slab, slab), slab)
        for a in range(3):
            copies.append(pltpu.make_async_copy(kernel_ref.at[a, :, group, own], out.at[a], sems.at[shift, a]))
    for copy in copies:
        copy.start()
    for copy in copies:
        copy.wait()


def split_weights(kernel, groups, slab, outs):
    if outs % 128 == 0 and slab % 128 == 0:
        return pl.pallas_call(
            functools.partial(weights_kernel, groups),
            out_shape=[jax.ShapeDtypeStruct((3, 3, slab, outs), BF16)] * groups,
            in_specs=[HBM],
            out_specs=[VMEM] * groups,
            scratch_shapes=[pltpu.SemaphoreType.DMA((groups, 3))],
            compiler_params=pltpu.CompilerParams(vmem_limit_bytes=48 << 20),
            cost_estimate=pl.CostEstimate(flops=3 * 10**9, bytes_accessed=1 << 20, transcendentals=0),
            name="split_weights",
        )(kernel)
    owner = lax.axis_index("filt")
    own = lax.dynamic_slice_in_dim(kernel, owner * outs, outs, 3)
    order = [lax.rem(owner - shift + groups, groups) for shift in range(groups)]
    return [lax.dynamic_slice_in_dim(own, group * slab, slab, 2) for group in order]


def body(features, kernel, bias):
    groups = lax.axis_size("filt")
    slab, height, width = features.shape
    outs = kernel.shape[3] // groups
    half = height // 2
    chunks = ((3, half + 2), (half + 2, height - 2), (height - 2, height - 1))

    rings = [[(i, (i + shift) % groups) for i in range(groups)] for shift in range(1, groups)]
    soon = early(features, chunks[0][0] - 1)
    soons = [lax.ppermute(soon, "filt", ring) for ring in rings]
    rim, upper_rows, lower_rows = relayout(features, (chunks[0], (chunks[0][1], height - 1)))
    rims = [rim] + [lax.ppermute(rim, "filt", ring) for ring in rings]
    sets = [[lax.ppermute(upper_rows, "filt", ring)] for ring in rings]
    pairs = [r[0 : 2 * width].reshape(2, width, slab) for r in rims]
    outer = [(0, 0, 0, 1), (0, 1, height - 1, 1)]
    shape = (height, width, outs)

    weights = split_weights(kernel, groups, slab, outs)
    bias = bias[None, :]
    if outs % 128 != 0:
        bias = lax.dynamic_slice_in_dim(bias, lax.axis_index("filt") * outs, outs, 1)
    spans = [*outer, (1, 0, 1, soon.shape[0]), (2, 0, chunks[0][0], upper_rows.shape[0]), (3, 0, chunks[0][1], lower_rows.shape[0])]
    second = pick(lower_rows, 0, chunks[1][1] - chunks[1][0], weights[0])
    for received, ring in zip(sets, rings):
        received.append(lax.ppermute(second, "filt", ring))

    row_pairs, col_pairs = swap_pairs("row"), swap_pairs("col")
    sent = calls(functools.partial(outermost_kernel, groups), "outermost", [(groups, width, slab)] * 2, [*rims, soons[0]], estimate=pl.CostEstimate(flops=4 * 10**9, bytes_accessed=1 << 20, transcendentals=0))
    outer_rows = [lax.ppermute(v, "row", p) for v, p in zip(sent, row_pairs)]
    total = accumulate(spans, [pairs[0], soon, upper_rows, lower_rows], weights[0], None, shape, rims[-1], bias)
    for g in range(1, groups):
        total = accumulate(outer, [pairs[g]], weights[g], total, shape)
    edge = pltpu.VMEM((2, height + 2, slab), F32)
    sent = calls(functools.partial(edges_kernel, groups), "edges", [(groups, height + 2, slab)] * 2, [*rims, *outer_rows], [edge])
    third = pick(lower_rows, chunks[2][0] - chunks[1][0], chunks[2][1] - chunks[1][0], sent[0])
    for received, ring in zip(sets, rings):
        received.append(lax.ppermute(third, "filt", ring))
    outer_cols = [lax.ppermute(v, "col", p) for v, p in zip(sent, col_pairs)]
    rows_fix = call(
        functools.partial(outer_rows_kernel, groups), "outer_rows", (2, width, outs), F32,
        [*outer_rows, *weights, *sent], cost(6 * width * groups, slab, outs), [pltpu.VMEM((3, 1, width, slab), BF16)],
    )
    for g in range(1, groups):
        a, b, c = sets[g - 1]
        spans = [(0, 0, 1, soon.shape[0]), (1, 0, chunks[0][0], a.shape[0])]
        total = accumulate(spans, [soons[g - 1], a], weights[g], total, shape, rows_fix)
        if g < groups - 1:
            total = accumulate([(0, 0, chunks[1][0], b.shape[0])], [b], weights[g], total, shape)
            total = accumulate([(0, 0, chunks[2][0], c.shape[0])], [c], weights[g], total, shape)
    cols_fix = call(
        functools.partial(outer_cols_kernel, groups), "outer_cols", (2, height, outs), F32,
        [*outer_cols, *weights, total], cost(6 * 256 * groups, slab, outs),
    )
    top = call(upper_kernel, "upper", (outs, half, width), BF16, [total, rows_fix, cols_fix], cost(256, slab, outs))
    total = accumulate([(0, 0, chunks[1][0], b.shape[0])], [b], weights[-1], total, shape, top)
    done = chunks[2][0] - 1 - half
    middle = call(functools.partial(middle_kernel, half), "middle", (done, outs, width), BF16, [total, rows_fix, cols_fix], cost(1, 1, 1))
    scratch = [
        pltpu.VMEM((3, c.shape[0], width, slab), BF16),
        pltpu.VMEM((outs, height - half, width), BF16),
        pltpu.SemaphoreType.DMA((2,)),
    ]
    return call(
        last_kernel, "last", (outs, height, width), BF16,
        [c, weights[-1], total, rows_fix, cols_fix, top, middle], cost(9 * 256, slab, outs), scratch, HBM,
    )


def solution(mesh):
    return jax.shard_map(
        body,
        mesh=mesh,
        in_specs=(P("filt", "row", "col"), P(), P()),
        out_specs=P("filt", "row", "col"),
        check_vma=False,
    )
```

```python
import functools

import jax
import jax.numpy as jnp
from jax import lax
from jax.experimental import pallas as pl
from jax.experimental.pallas import tpu as pltpu
from jax.sharding import PartitionSpec as P

BF16, F32 = jnp.bfloat16, jnp.float32
VMEM = pl.BlockSpec(memory_space=pltpu.VMEM)
HBM = pl.BlockSpec(memory_space=pltpu.HBM)
PARAMS = pltpu.CompilerParams(vmem_limit_bytes=10 << 20)
WAIT = pl.CostEstimate(flops=4 * 10**9, bytes_accessed=1 << 20, transcendentals=0)
BLOCK = 4


def relayout_kernel(chunks, x_hbm, rim_ref, *refs):
    outs, (x_ref, col_ref, sems) = refs[:-3], refs[-3:]
    slab, rows, width = x_ref.shape
    parts = 2 if slab % 256 == 0 else 1
    step = slab // parts
    copies = [pltpu.make_async_copy(x_hbm.at[q * step : (q + 1) * step], x_ref.at[q * step : (q + 1) * step], sems.at[q]) for q in range(parts)]
    for copy in copies:
        copy.start()
    for q, copy in enumerate(copies):
        copy.wait()
        lanes = slice(q * step, (q + 1) * step)
        group = jnp.swapaxes(x_ref[lanes], 0, 1)
        for h in range(rows):
            pixels = group[h].T
            col_ref[h : h + 1, lanes] = pixels[0:16].astype(F32)[0:1, :]
            col_ref[rows + h : rows + h + 1, lanes] = pixels[width - 16 :].astype(F32)[15:16, :]
            if h == 0:
                rim_ref[0:width, lanes] = pixels
            elif h == rows - 1:
                rim_ref[width : 2 * width, lanes] = pixels
            else:
                for out, (first, last) in zip(outs, chunks):
                    if first <= h < last:
                        out[h - first, :, lanes] = pixels
    rim_ref[2 * width :, :] = col_ref[...].astype(BF16)


def relayout(features, chunks):
    slab, rows, width = features.shape
    shapes = [(2 * width + 2 * rows, slab)] + [(last - first, width, slab) for first, last in chunks]
    return pl.pallas_call(
        functools.partial(relayout_kernel, chunks),
        out_shape=[jax.ShapeDtypeStruct(s, BF16) for s in shapes],
        in_specs=[HBM],
        out_specs=[VMEM] * len(shapes),
        scratch_shapes=[pltpu.VMEM(features.shape, BF16), pltpu.VMEM((2 * rows, slab), F32), pltpu.SemaphoreType.DMA((2,))],
        compiler_params=PARAMS,
        name="relayout",
    )(pltpu.with_memory_space_constraint(features, pltpu.HBM))


def put_row(x_ref, at, value):
    width, slab = value.shape
    edge = lax.broadcasted_iota(jnp.int32, (16, slab), 0)
    x_ref[1, at] = value
    x_ref[0, at, 0 : width - 16, :] = value[0 : width - 16]
    x_ref[0, at, width - 16 :, :] = jnp.where(edge == 15, 0, value[width - 16 :].astype(F32)).astype(BF16)
    x_ref[2, at, 16:, :] = value[16:]
    x_ref[2, at, 0:16, :] = jnp.where(edge == 0, 0, value[0:16].astype(F32)).astype(BF16)


def turn(part, b):
    return part if b == 1 else pltpu.roll(part, 1 if b == 0 else part.shape[0] - 1, 0)


def add_rows(spans, w_ref, total_ref, x_ref, written, initial=None):
    height, width, _ = total_ref.shape
    slab = w_ref.shape[2]
    at = 0
    for piece, local, row, count in spans:
        for start in range(0, count, BLOCK):
            size = min(BLOCK, count - start)
            for i in range(size):
                put_row(x_ref, at + i, piece[local + start + i])
            for a in range(3):
                low = max(0, row + start + 1 - a)
                high = min(height, row + start + size + 1 - a)
                if high <= low:
                    continue
                skip = low - (row + start + 1 - a)
                n = high - low
                for b in range(3):
                    lhs = x_ref[b, at + skip : at + skip + n].reshape(n * width, slab)
                    part = jnp.dot(lhs, w_ref[a, b], preferred_element_type=F32).reshape(n, width, -1)
                    for i in range(n):
                        term = turn(part[i], b)
                        if low + i in written:
                            total_ref[low + i] += term
                        else:
                            total_ref[low + i] = term + initial
                            written.add(low + i)
            at += size


def accumulate_kernel(spans, n, started, *refs):
    pieces, w_ref, total_ref, x_ref = refs[:n], refs[n], refs[-2], refs[-1]
    written = set(range(total_ref.shape[0])) if started else set()
    spans = [(pieces[p], local, row, count) for p, local, row, count in spans]
    add_rows(spans, w_ref, total_ref, x_ref, written, None if started else own_bias(refs[n + 1], total_ref.shape[2]))


def own_bias(bias_ref, outs):
    if bias_ref.shape[1] == outs:
        return bias_ref[...]
    return bias_ref[:, pl.ds(pl.multiple_of(lax.axis_index("filt") * outs, outs), outs)]


def accumulate(spans, pieces, weights, total, shape, after=None, bias=None):
    count = sum(s[3] for s in spans)
    width, slab = shape[1], weights.shape[2]
    operands = [*pieces, weights]
    aliases = {}
    if total is not None:
        aliases = {len(operands): 0}
        operands.append(total)
    else:
        operands.append(bias)
    if after is not None:
        operands.append(after)
    return pl.pallas_call(
        functools.partial(accumulate_kernel, spans, len(pieces), total is not None),
        out_shape=jax.ShapeDtypeStruct(shape, F32),
        in_specs=[VMEM] * len(operands),
        out_specs=VMEM,
        scratch_shapes=[pltpu.VMEM((3, count, width, slab), BF16)],
        input_output_aliases=aliases,
        compiler_params=PARAMS,
        cost_estimate=cost(count * width * 9, slab, shape[2]),
        name="accumulate",
    )(*operands)


def pick_kernel(low, high, rows_ref, after_ref, out_ref):
    out_ref[...] = rows_ref[low:high]


def pick(rows, low, high, after):
    shape = (high - low, *rows.shape[1:])
    return call(functools.partial(pick_kernel, low, high), "pick", shape, BF16, [rows, after], cost(1, 1, 1))


def cost(pixels, slab, outs):
    return pl.CostEstimate(flops=2 * pixels * slab * outs, bytes_accessed=1 << 20, transcendentals=0)


def parity(axis):
    return lax.rem(lax.axis_index(axis), 2)


def swap_pairs(axis):
    count = lax.axis_size(axis)
    return [[p for i in range(start, count - 1, 2) for p in ((i, i + 1), (i + 1, i))] for start in (1, 0)]


def outermost_kernel(groups, *refs):
    rims, outs = refs[:groups], refs[-2:]
    width = outs[0].shape[1]
    odd = parity("row")
    for swap, out_ref in enumerate(outs):
        start = pl.multiple_of((odd if swap == 0 else 1 - odd) * width, width)
        for g in range(groups):
            out_ref[g] = rims[g][pl.ds(start, width), :]


def edges_kernel(groups, *refs):
    rims, swapped, outs, col_ref = refs[:groups], refs[groups : groups + 2], refs[-3:-1], refs[-1]
    width = swapped[0].shape[1]
    height = outs[0].shape[1] - 2
    odd_row, odd_col = parity("row") == 1, parity("col") == 1
    for g in range(groups):
        for side, at in enumerate((0, width - 16)):
            pixels = [ref[g, at : at + 16, :].astype(F32)[side * 15 : side * 15 + 1, :] for ref in swapped]
            start = 2 * width + side * height
            col_ref[side, 0:1, :] = jnp.where(odd_row, pixels[1], pixels[0])
            col_ref[side, 1 : height + 1, :] = rims[g][start : start + height, :].astype(F32)
            col_ref[side, height + 1 :, :] = jnp.where(odd_row, pixels[0], pixels[1])
        outs[0][g] = jnp.where(odd_col, col_ref[1], col_ref[0]).astype(BF16)
        outs[1][g] = jnp.where(odd_col, col_ref[0], col_ref[1]).astype(BF16)


def outer_rows_kernel(groups, *refs):
    swapped, w_refs, fix_ref, x_ref = refs[:2], refs[2 : 2 + groups], refs[-2], refs[-1]
    odd = parity("row") == 1
    for i, a in enumerate((0, 2)):
        fix = None
        for g in range(groups):
            put_row(x_ref, 0, jnp.where(odd, swapped[1 - i][g], swapped[i][g]))
            for b in range(3):
                part = turn(jnp.dot(x_ref[b, 0], w_refs[g][a, b], preferred_element_type=F32), b)
                fix = part if fix is None else fix + part
        fix_ref[i] = fix


def outer_cols_kernel(groups, *refs):
    swapped, w_refs, fix_ref = refs[:2], refs[2 : 2 + groups], refs[-1]
    height = fix_ref.shape[1]
    odd = parity("col") == 1
    for i, b in enumerate((0, 2)):
        fix = None
        for g in range(groups):
            pixels = jnp.where(odd, swapped[1 - i][g], swapped[i][g])
            for a in range(3):
                part = jnp.dot(pixels, w_refs[g][a, b], preferred_element_type=F32)[a : a + height]
                fix = part if fix is None else fix + part
        fix_ref[i] = fix


def finish_row(value, h, rows_ref, cols_ref):
    height, width = cols_ref.shape[1], value.shape[0]
    if h == 0:
        value += rows_ref[0]
    if h == height - 1:
        value += rows_ref[1]
    edge = lax.broadcasted_iota(jnp.int32, (8, value.shape[1]), 0)
    first = value[0:8] + jnp.where(edge == 0, cols_ref[0, h : h + 1, :], 0)
    final = value[width - 8 :] + jnp.where(edge == 7, cols_ref[1, h : h + 1, :], 0)
    return jnp.concatenate([first, value[8 : width - 8], final], 0).astype(BF16).T


def upper_kernel(total_ref, rows_ref, cols_ref, out_ref):
    turned = [finish_row(total_ref[h], h, rows_ref, cols_ref) for h in range(out_ref.shape[1])]
    out_ref[...] = jnp.swapaxes(jnp.stack(turned, 0), 0, 1)


def middle_kernel(start, total_ref, rows_ref, cols_ref, out_ref):
    for i in range(out_ref.shape[0]):
        out_ref[i] = finish_row(total_ref[start + i], start + i, rows_ref, cols_ref)


def last_kernel(piece, w_ref, total_ref, rows_ref, cols_ref, upper_ref, middle_ref, out_ref, x_ref, lower_ref, sems):
    outs, height, width = out_ref.shape
    half, done = upper_ref.shape[1], middle_ref.shape[0]
    first = pltpu.make_async_copy(upper_ref, out_ref.at[:, 0:half, :], sems.at[0])
    first.start()
    count = piece.shape[0]
    for i in range(count):
        put_row(x_ref, i, piece[i])
    values = [total_ref[h] for h in range(half + done, height)]
    for a in range(3):
        for b in range(3):
            part = jnp.dot(x_ref[b].reshape(count * width, -1), w_ref[a, b], preferred_element_type=F32).reshape(count, width, outs)
            for i in range(count):
                values[i + 2 - a] += turn(part[i], b)
    turned = [middle_ref[i] for i in range(done)]
    turned += [finish_row(value, half + done + i, rows_ref, cols_ref) for i, value in enumerate(values)]
    lower_ref[...] = jnp.swapaxes(jnp.stack(turned, 0), 0, 1)
    second = pltpu.make_async_copy(lower_ref, out_ref.at[:, half:height, :], sems.at[1])
    second.start()
    first.wait()
    second.wait()


def call(kernel, name, shape, dtype, operands, estimate, scratch=(), out=VMEM):
    return pl.pallas_call(
        kernel,
        out_shape=jax.ShapeDtypeStruct(shape, dtype),
        in_specs=[VMEM] * len(operands),
        out_specs=out,
        scratch_shapes=scratch,
        compiler_params=PARAMS,
        cost_estimate=estimate,
        name=name,
    )(*operands)


def calls(kernel, name, shapes, operands, scratch=(), estimate=None):
    return pl.pallas_call(
        kernel,
        out_shape=[jax.ShapeDtypeStruct(shape, BF16) for shape in shapes],
        in_specs=[VMEM] * len(operands),
        out_specs=[VMEM] * len(shapes),
        scratch_shapes=scratch,
        compiler_params=PARAMS,
        cost_estimate=estimate or cost(1, 1, 1),
        name=name,
    )(*operands)


def weights_kernel(groups, kernel_ref, *refs):
    outs, sems = refs[:-1], refs[-1]
    slab, width = outs[0].shape[2:]
    owner = lax.axis_index("filt")
    own = pl.ds(pl.multiple_of(owner * width, width), width)
    copies = []
    for shift, out in enumerate(outs):
        group = pl.ds(pl.multiple_of(lax.rem(owner - shift + groups, groups) * slab, slab), slab)
        for a in range(3):
            copies.append(pltpu.make_async_copy(kernel_ref.at[a, :, group, own], out.at[a], sems.at[shift, a]))
    for copy in copies:
        copy.start()
    for copy in copies:
        copy.wait()


def split_weights(kernel, groups, slab, outs):
    if outs % 128 == 0 and slab % 128 == 0:
        return pl.pallas_call(
            functools.partial(weights_kernel, groups),
            out_shape=[jax.ShapeDtypeStruct((3, 3, slab, outs), BF16)] * groups,
            in_specs=[HBM],
            out_specs=[VMEM] * groups,
            scratch_shapes=[pltpu.SemaphoreType.DMA((groups, 3))],
            compiler_params=pltpu.CompilerParams(vmem_limit_bytes=48 << 20),
            name="split_weights",
        )(kernel)
    owner = lax.axis_index("filt")
    own = lax.dynamic_slice_in_dim(kernel, owner * outs, outs, 3)
    order = [lax.rem(owner - shift + groups, groups) for shift in range(groups)]
    return [lax.dynamic_slice_in_dim(own, group * slab, slab, 2) for group in order]


def body(features, kernel, bias):
    groups = lax.axis_size("filt")
    slab, height, width = features.shape
    outs = kernel.shape[3] // groups
    half = height // 2
    chunks = ((1, half + 3), (half + 3, height - 2), (height - 2, height - 1))

    rim, upper_rows, lower_rows = relayout(features, (chunks[0], (chunks[0][1], height - 1)))
    rings = [[(i, (i + shift) % groups) for i in range(groups)] for shift in range(1, groups)]
    rims = [rim] + [lax.ppermute(rim, "filt", ring) for ring in rings]
    sets = [[lax.ppermute(upper_rows, "filt", ring)] for ring in rings]
    pairs = [r[0 : 2 * width].reshape(2, width, slab) for r in rims]
    outer = [(0, 0, 0, 1), (0, 1, height - 1, 1)]
    shape = (height, width, outs)

    weights = split_weights(kernel, groups, slab, outs)
    bias = bias[None, :]
    if outs % 128 != 0:
        bias = lax.dynamic_slice_in_dim(bias, lax.axis_index("filt") * outs, outs, 1)
    spans = [*outer, (1, 0, 1, half + 2), (2, 0, half + 3, height - half - 4)]
    second = pick(lower_rows, 0, chunks[1][1] - chunks[1][0], weights[0])
    for received, ring in zip(sets, rings):
        received.append(lax.ppermute(second, "filt", ring))

    row_pairs, col_pairs = swap_pairs("row"), swap_pairs("col")
    sent = calls(functools.partial(outermost_kernel, groups), "outermost", [(groups, width, slab)] * 2, rims, estimate=WAIT)
    outer_rows = [lax.ppermute(v, "row", p) for v, p in zip(sent, row_pairs)]
    total = accumulate(spans, [pairs[0], upper_rows, lower_rows], weights[0], None, shape, rims[-1], bias)
    for g in range(1, groups):
        total = accumulate(outer, [pairs[g]], weights[g], total, shape)
    edge = pltpu.VMEM((2, height + 2, slab), F32)
    sent = calls(functools.partial(edges_kernel, groups), "edges", [(groups, height + 2, slab)] * 2, [*rims, *outer_rows], [edge])
    third = pick(lower_rows, chunks[2][0] - chunks[1][0], chunks[2][1] - chunks[1][0], sent[0])
    for received, ring in zip(sets, rings):
        received.append(lax.ppermute(third, "filt", ring))
    outer_cols = [lax.ppermute(v, "col", p) for v, p in zip(sent, col_pairs)]
    rows_fix = call(
        functools.partial(outer_rows_kernel, groups), "outer_rows", (2, width, outs), F32,
        [*outer_rows, *weights, *sent], cost(6 * width * groups, slab, outs), [pltpu.VMEM((3, 1, width, slab), BF16)],
    )
    for g in range(1, groups):
        a, b, c = sets[g - 1]
        total = accumulate([(0, 0, chunks[0][0], a.shape[0])], [a], weights[g], total, shape, rows_fix)
        if g < groups - 1:
            total = accumulate([(0, 0, chunks[1][0], b.shape[0])], [b], weights[g], total, shape)
            total = accumulate([(0, 0, chunks[2][0], c.shape[0])], [c], weights[g], total, shape)
    cols_fix = call(
        functools.partial(outer_cols_kernel, groups), "outer_cols", (2, height, outs), F32,
        [*outer_cols, *weights, total], cost(6 * 256 * groups, slab, outs),
    )
    top = call(upper_kernel, "upper", (outs, half, width), BF16, [total, rows_fix, cols_fix], cost(256, slab, outs))
    total = accumulate([(0, 0, chunks[1][0], b.shape[0])], [b], weights[-1], total, shape, top)
    done = chunks[2][0] - 1 - half
    middle = call(functools.partial(middle_kernel, half), "middle", (done, outs, width), BF16, [total, rows_fix, cols_fix], cost(1, 1, 1))
    scratch = [
        pltpu.VMEM((3, c.shape[0], width, slab), BF16),
        pltpu.VMEM((outs, height - half, width), BF16),
        pltpu.SemaphoreType.DMA((2,)),
    ]
    return call(
        last_kernel, "last", (outs, height, width), BF16,
        [c, weights[-1], total, rows_fix, cols_fix, top, middle], cost(9 * 256, slab, outs), scratch, HBM,
    )


def solution(mesh):
    return jax.shard_map(
        body,
        mesh=mesh,
        in_specs=(P("filt", "row", "col"), P(), P()),
        out_specs=P("filt", "row", "col"),
        check_vma=False,
    )
```

```python
import functools

import jax
import jax.numpy as jnp
from jax import lax
from jax.experimental import pallas as pl
from jax.experimental.pallas import tpu as pltpu
from jax.sharding import PartitionSpec as P

BF16, F32 = jnp.bfloat16, jnp.float32
VMEM = pl.BlockSpec(memory_space=pltpu.VMEM)
HBM = pl.BlockSpec(memory_space=pltpu.HBM)
PARAMS = pltpu.CompilerParams(vmem_limit_bytes=10 << 20)
WAIT = pl.CostEstimate(flops=4 * 10**9, bytes_accessed=1 << 20, transcendentals=0)
BLOCK = 4


def relayout_kernel(chunks, x_hbm, rim_ref, *refs):
    outs, (x_ref, col_ref, sems) = refs[:-3], refs[-3:]
    slab, rows, width = x_ref.shape
    parts = 2 if slab % 256 == 0 else 1
    step = slab // parts
    copies = [pltpu.make_async_copy(x_hbm.at[q * step : (q + 1) * step], x_ref.at[q * step : (q + 1) * step], sems.at[q]) for q in range(parts)]
    for copy in copies:
        copy.start()
    for q, copy in enumerate(copies):
        copy.wait()
        lanes = slice(q * step, (q + 1) * step)
        group = jnp.swapaxes(x_ref[lanes], 0, 1)
        for h in range(rows):
            pixels = group[h].T
            col_ref[h : h + 1, lanes] = pixels[0:16].astype(F32)[0:1, :]
            col_ref[rows + h : rows + h + 1, lanes] = pixels[width - 16 :].astype(F32)[15:16, :]
            if h == 0:
                rim_ref[0:width, lanes] = pixels
            elif h == rows - 1:
                rim_ref[width : 2 * width, lanes] = pixels
            else:
                for out, (first, last) in zip(outs, chunks):
                    if first <= h < last:
                        out[h - first, :, lanes] = pixels
    rim_ref[2 * width :, :] = col_ref[...].astype(BF16)


def relayout(features, chunks):
    slab, rows, width = features.shape
    shapes = [(2 * width + 2 * rows, slab)] + [(last - first, width, slab) for first, last in chunks]
    return pl.pallas_call(
        functools.partial(relayout_kernel, chunks),
        out_shape=[jax.ShapeDtypeStruct(s, BF16) for s in shapes],
        in_specs=[HBM],
        out_specs=[VMEM] * len(shapes),
        scratch_shapes=[pltpu.VMEM(features.shape, BF16), pltpu.VMEM((2 * rows, slab), F32), pltpu.SemaphoreType.DMA((2,))],
        compiler_params=PARAMS,
        name="relayout",
    )(pltpu.with_memory_space_constraint(features, pltpu.HBM))


def put_row(x_ref, at, value):
    width, slab = value.shape
    edge = lax.broadcasted_iota(jnp.int32, (16, slab), 0)
    x_ref[1, at] = value
    x_ref[0, at, 0 : width - 16, :] = value[0 : width - 16]
    x_ref[0, at, width - 16 :, :] = jnp.where(edge == 15, 0, value[width - 16 :].astype(F32)).astype(BF16)
    x_ref[2, at, 16:, :] = value[16:]
    x_ref[2, at, 0:16, :] = jnp.where(edge == 0, 0, value[0:16].astype(F32)).astype(BF16)


def turn(part, b):
    return part if b == 1 else pltpu.roll(part, 1 if b == 0 else part.shape[0] - 1, 0)


def add_rows(spans, w_ref, total_ref, x_ref, base):
    written = set()
    height, width, _ = total_ref.shape
    slab = w_ref.shape[2]
    at = 0
    for piece, local, row, count in spans:
        for start in range(0, count, BLOCK):
            size = min(BLOCK, count - start)
            for i in range(size):
                put_row(x_ref, at + i, piece[local + start + i])
            for a in range(3):
                low = max(0, row + start + 1 - a)
                high = min(height, row + start + size + 1 - a)
                if high <= low:
                    continue
                skip = low - (row + start + 1 - a)
                n = high - low
                for b in range(3):
                    lhs = x_ref[b, at + skip : at + skip + n].reshape(n * width, slab)
                    part = jnp.dot(lhs, w_ref[a, b], preferred_element_type=F32).reshape(n, width, -1)
                    for i in range(n):
                        term = turn(part[i], b)
                        if low + i in written:
                            total_ref[low + i] += term
                        else:
                            total_ref[low + i] = term + base(low + i)
                            written.add(low + i)
            at += size
    return written


def accumulate_kernel(spans, n, started, *refs):
    pieces, w_ref, start_ref, total_ref, x_ref = refs[:n], refs[n], refs[n + 1], refs[-2], refs[-1]
    spans = [(pieces[p], local, row, count) for p, local, row, count in spans]
    if started:
        written = add_rows(spans, w_ref, total_ref, x_ref, lambda h: start_ref[h])
    else:
        bias = own_bias(start_ref, total_ref.shape[2])
        written = add_rows(spans, w_ref, total_ref, x_ref, lambda h: bias)
    for h in range(total_ref.shape[0]):
        if h not in written:
            total_ref[h] = start_ref[h]


def own_bias(bias_ref, outs):
    if bias_ref.shape[1] == outs:
        return bias_ref[...]
    return bias_ref[:, pl.ds(pl.multiple_of(lax.axis_index("filt") * outs, outs), outs)]


def accumulate(spans, pieces, weights, total, shape, after=None, bias=None):
    count = sum(s[3] for s in spans)
    width, slab = shape[1], weights.shape[2]
    operands = [*pieces, weights, bias if total is None else total]
    if after is not None:
        operands.append(after)
    return pl.pallas_call(
        functools.partial(accumulate_kernel, spans, len(pieces), total is not None),
        out_shape=jax.ShapeDtypeStruct(shape, F32),
        in_specs=[VMEM] * len(operands),
        out_specs=VMEM,
        scratch_shapes=[pltpu.VMEM((3, count, width, slab), BF16)],
        compiler_params=PARAMS,
        cost_estimate=cost(count * width * 9, slab, shape[2]),
        name="accumulate",
    )(*operands)


def pick_kernel(low, high, rows_ref, after_ref, out_ref):
    out_ref[...] = rows_ref[low:high]


def pick(rows, low, high, after):
    shape = (high - low, *rows.shape[1:])
    return call(functools.partial(pick_kernel, low, high), "pick", shape, BF16, [rows, after], cost(1, 1, 1))


def cost(pixels, slab, outs):
    return pl.CostEstimate(flops=2 * pixels * slab * outs, bytes_accessed=1 << 20, transcendentals=0)


def parity(axis):
    return lax.rem(lax.axis_index(axis), 2)


def swap_pairs(axis):
    count = lax.axis_size(axis)
    return [[p for i in range(start, count - 1, 2) for p in ((i, i + 1), (i + 1, i))] for start in (1, 0)]


def outermost_kernel(groups, *refs):
    rims, outs = refs[:groups], refs[-2:]
    width = outs[0].shape[1]
    odd = parity("row")
    for swap, out_ref in enumerate(outs):
        start = pl.multiple_of((odd if swap == 0 else 1 - odd) * width, width)
        for g in range(groups):
            out_ref[g] = rims[g][pl.ds(start, width), :]


def edges_kernel(groups, *refs):
    rims, swapped, outs, col_ref = refs[:groups], refs[groups : groups + 2], refs[-3:-1], refs[-1]
    width = swapped[0].shape[1]
    height = outs[0].shape[1] - 2
    odd_row, odd_col = parity("row") == 1, parity("col") == 1
    for g in range(groups):
        for side, at in enumerate((0, width - 16)):
            pixels = [ref[g, at : at + 16, :].astype(F32)[side * 15 : side * 15 + 1, :] for ref in swapped]
            start = 2 * width + side * height
            col_ref[side, 0:1, :] = jnp.where(odd_row, pixels[1], pixels[0])
            col_ref[side, 1 : height + 1, :] = rims[g][start : start + height, :].astype(F32)
            col_ref[side, height + 1 :, :] = jnp.where(odd_row, pixels[0], pixels[1])
        outs[0][g] = jnp.where(odd_col, col_ref[1], col_ref[0]).astype(BF16)
        outs[1][g] = jnp.where(odd_col, col_ref[0], col_ref[1]).astype(BF16)


def outer_rows_kernel(groups, *refs):
    swapped, w_refs, fix_ref, x_ref = refs[:2], refs[2 : 2 + groups], refs[-2], refs[-1]
    odd = parity("row") == 1
    for i, a in enumerate((0, 2)):
        fix = None
        for g in range(groups):
            put_row(x_ref, 0, jnp.where(odd, swapped[1 - i][g], swapped[i][g]))
            for b in range(3):
                part = turn(jnp.dot(x_ref[b, 0], w_refs[g][a, b], preferred_element_type=F32), b)
                fix = part if fix is None else fix + part
        fix_ref[i] = fix


def outer_cols_kernel(groups, *refs):
    swapped, w_refs, fix_ref = refs[:2], refs[2 : 2 + groups], refs[-1]
    height = fix_ref.shape[1]
    odd = parity("col") == 1
    for i, b in enumerate((0, 2)):
        fix = None
        for g in range(groups):
            pixels = jnp.where(odd, swapped[1 - i][g], swapped[i][g])
            for a in range(3):
                part = jnp.dot(pixels, w_refs[g][a, b], preferred_element_type=F32)[a : a + height]
                fix = part if fix is None else fix + part
        fix_ref[i] = fix


def finish_row(value, h, rows_ref, cols_ref):
    height, width = cols_ref.shape[1], value.shape[0]
    if h == 0:
        value += rows_ref[0]
    if h == height - 1:
        value += rows_ref[1]
    edge = lax.broadcasted_iota(jnp.int32, (8, value.shape[1]), 0)
    first = value[0:8] + jnp.where(edge == 0, cols_ref[0, h : h + 1, :], 0)
    final = value[width - 8 :] + jnp.where(edge == 7, cols_ref[1, h : h + 1, :], 0)
    return jnp.concatenate([first, value[8 : width - 8], final], 0).astype(BF16).T


def upper_kernel(total_ref, rows_ref, cols_ref, out_ref):
    turned = [finish_row(total_ref[h], h, rows_ref, cols_ref) for h in range(out_ref.shape[1])]
    out_ref[...] = jnp.swapaxes(jnp.stack(turned, 0), 0, 1)


def second_kernel(row, start, piece, w_ref, total_ref, rows_ref, cols_ref, after_ref, done_ref, rest_ref, sum_ref, x_ref):
    count, done = piece.shape[0], done_ref.shape[0]
    written = add_rows([(piece, 0, row, count)], w_ref, sum_ref, x_ref, lambda h: total_ref[h])
    for i in range(done + rest_ref.shape[0]):
        value = (sum_ref if start + i in written else total_ref)[start + i]
        if i < done:
            done_ref[i] = finish_row(value, start + i, rows_ref, cols_ref)
        else:
            rest_ref[i - done] = value


def last_kernel(piece, w_ref, rest_ref, rows_ref, cols_ref, upper_ref, middle_ref, out_ref, x_ref, lower_ref, sems):
    outs, height, width = out_ref.shape
    half, done = upper_ref.shape[1], middle_ref.shape[0]
    first = pltpu.make_async_copy(upper_ref, out_ref.at[:, 0:half, :], sems.at[0])
    first.start()
    count = piece.shape[0]
    for i in range(count):
        put_row(x_ref, i, piece[i])
    values = [rest_ref[i] for i in range(height - half - done)]
    for a in range(3):
        for b in range(3):
            part = jnp.dot(x_ref[b].reshape(count * width, -1), w_ref[a, b], preferred_element_type=F32).reshape(count, width, outs)
            for i in range(count):
                values[i + 2 - a] += turn(part[i], b)
    turned = [middle_ref[i] for i in range(done)]
    turned += [finish_row(value, half + done + i, rows_ref, cols_ref) for i, value in enumerate(values)]
    lower_ref[...] = jnp.swapaxes(jnp.stack(turned, 0), 0, 1)
    second = pltpu.make_async_copy(lower_ref, out_ref.at[:, half:height, :], sems.at[1])
    second.start()
    first.wait()
    second.wait()


def call(kernel, name, shape, dtype, operands, estimate, scratch=(), out=VMEM):
    return pl.pallas_call(
        kernel,
        out_shape=jax.ShapeDtypeStruct(shape, dtype),
        in_specs=[VMEM] * len(operands),
        out_specs=out,
        scratch_shapes=scratch,
        compiler_params=PARAMS,
        cost_estimate=estimate,
        name=name,
    )(*operands)


def calls(kernel, name, shapes, operands, scratch=(), estimate=None):
    return pl.pallas_call(
        kernel,
        out_shape=[jax.ShapeDtypeStruct(shape, BF16) for shape in shapes],
        in_specs=[VMEM] * len(operands),
        out_specs=[VMEM] * len(shapes),
        scratch_shapes=scratch,
        compiler_params=PARAMS,
        cost_estimate=estimate or cost(1, 1, 1),
        name=name,
    )(*operands)


def weights_kernel(groups, kernel_ref, *refs):
    outs, sems = refs[:-1], refs[-1]
    slab, width = outs[0].shape[2:]
    owner = lax.axis_index("filt")
    own = pl.ds(pl.multiple_of(owner * width, width), width)
    copies = []
    for shift, out in enumerate(outs):
        group = pl.ds(pl.multiple_of(lax.rem(owner - shift + groups, groups) * slab, slab), slab)
        for a in range(3):
            copies.append(pltpu.make_async_copy(kernel_ref.at[a, :, group, own], out.at[a], sems.at[shift, a]))
    for copy in copies:
        copy.start()
    for copy in copies:
        copy.wait()


def split_weights(kernel, groups, slab, outs):
    if outs % 128 == 0 and slab % 128 == 0:
        return pl.pallas_call(
            functools.partial(weights_kernel, groups),
            out_shape=[jax.ShapeDtypeStruct((3, 3, slab, outs), BF16)] * groups,
            in_specs=[HBM],
            out_specs=[VMEM] * groups,
            scratch_shapes=[pltpu.SemaphoreType.DMA((groups, 3))],
            compiler_params=pltpu.CompilerParams(vmem_limit_bytes=48 << 20),
            name="split_weights",
        )(kernel)
    owner = lax.axis_index("filt")
    own = lax.dynamic_slice_in_dim(kernel, owner * outs, outs, 3)
    order = [lax.rem(owner - shift + groups, groups) for shift in range(groups)]
    return [lax.dynamic_slice_in_dim(own, group * slab, slab, 2) for group in order]


def body(features, kernel, bias):
    groups = lax.axis_size("filt")
    slab, height, width = features.shape
    outs = kernel.shape[3] // groups
    half = height // 2
    chunks = ((1, half + 3), (half + 3, height - 2), (height - 2, height - 1))

    rim, upper_rows, lower_rows = relayout(features, (chunks[0], (chunks[0][1], height - 1)))
    rings = [[(i, (i + shift) % groups) for i in range(groups)] for shift in range(1, groups)]
    rims = [rim] + [lax.ppermute(rim, "filt", ring) for ring in rings]
    sets = [[lax.ppermute(upper_rows, "filt", ring)] for ring in rings]
    pairs = [r[0 : 2 * width].reshape(2, width, slab) for r in rims]
    outer = [(0, 0, 0, 1), (0, 1, height - 1, 1)]
    shape = (height, width, outs)

    weights = split_weights(kernel, groups, slab, outs)
    bias = bias[None, :]
    if outs % 128 != 0:
        bias = lax.dynamic_slice_in_dim(bias, lax.axis_index("filt") * outs, outs, 1)
    spans = [*outer, (1, 0, 1, half + 2), (2, 0, half + 3, height - half - 4)]
    second = pick(lower_rows, 0, chunks[1][1] - chunks[1][0], weights[0])
    for received, ring in zip(sets, rings):
        received.append(lax.ppermute(second, "filt", ring))

    row_pairs, col_pairs = swap_pairs("row"), swap_pairs("col")
    sent = calls(functools.partial(outermost_kernel, groups), "outermost", [(groups, width, slab)] * 2, rims, estimate=WAIT)
    outer_rows = [lax.ppermute(v, "row", p) for v, p in zip(sent, row_pairs)]
    total = accumulate(spans, [pairs[0], upper_rows, lower_rows], weights[0], None, shape, rims[-1], bias)
    edge = pltpu.VMEM((2, height + 2, slab), F32)
    sent = calls(functools.partial(edges_kernel, groups), "edges", [(groups, height + 2, slab)] * 2, [*rims, *outer_rows], [edge])
    third = pick(lower_rows, chunks[2][0] - chunks[1][0], chunks[2][1] - chunks[1][0], sent[0])
    for received, ring in zip(sets, rings):
        received.append(lax.ppermute(third, "filt", ring))
    outer_cols = [lax.ppermute(v, "col", p) for v, p in zip(sent, col_pairs)]
    rows_fix = call(
        functools.partial(outer_rows_kernel, groups), "outer_rows", (2, width, outs), F32,
        [*outer_rows, *weights, *sent], cost(6 * width * groups, slab, outs), [pltpu.VMEM((3, 1, width, slab), BF16)],
    )
    for g in range(1, groups):
        a, b, c = sets[g - 1]
        spans, chosen = [*outer, (1, 0, chunks[0][0], a.shape[0])], [pairs[g], a]
        if g < groups - 1:
            spans += [(2, 0, chunks[1][0], b.shape[0]), (3, 0, chunks[2][0], c.shape[0])]
            chosen += [b, c]
        total = accumulate(spans, chosen, weights[g], total, shape, rows_fix)
    cols_fix = call(
        functools.partial(outer_cols_kernel, groups), "outer_cols", (2, height, outs), F32,
        [*outer_cols, *weights, total], cost(6 * 256 * groups, slab, outs),
    )
    top = call(upper_kernel, "upper", (outs, half, width), BF16, [total, rows_fix, cols_fix], cost(256, slab, outs))
    done = chunks[2][0] - 1 - half
    middle, rest = pl.pallas_call(
        functools.partial(second_kernel, chunks[1][0], half),
        out_shape=[jax.ShapeDtypeStruct((done, outs, width), BF16), jax.ShapeDtypeStruct((half - done, width, outs), F32)],
        in_specs=[VMEM] * 6,
        out_specs=[VMEM] * 2,
        scratch_shapes=[pltpu.VMEM(shape, F32), pltpu.VMEM((3, b.shape[0], width, slab), BF16)],
        compiler_params=PARAMS,
        cost_estimate=cost(b.shape[0] * width * 9, slab, outs),
        name="second",
    )(b, weights[-1], total, rows_fix, cols_fix, top)
    scratch = [
        pltpu.VMEM((3, c.shape[0], width, slab), BF16),
        pltpu.VMEM((outs, height - half, width), BF16),
        pltpu.SemaphoreType.DMA((2,)),
    ]
    return call(
        last_kernel, "last", (outs, height, width), BF16,
        [c, weights[-1], rest, rows_fix, cols_fix, top, middle], cost(9 * 256, slab, outs), scratch, HBM,
    )


def solution(mesh):
    return jax.shard_map(
        body,
        mesh=mesh,
        in_specs=(P("filt", "row", "col"), P(), P()),
        out_specs=P("filt", "row", "col"),
        check_vma=False,
    )
```
